512 devices in a mesh: rows: 64 (over z, x, core), cols: 8 (over y).
Axes of the slice: x: 4, y: 8, z: 8, core: 2. Of those that a mesh axis runs over, the one named last changes fastest.
Arguments:
- rhs: float32 [3, 128, 256, 128], P(None, 'rows', 'cols'), may hold values from -6 to 6
- diag_inv: float32 [3, 128, 256, 256], P(None, 'rows', 'cols'), may hold values from -1 to 3.1, as said below
- factor_tiles: float32 [2, 128, 8, 256, 256], P(None, 'rows', None, 'cols'), may hold values from -0.125 to 0.125
- tile_source: int32 [2, 128, 8], P(None, 'rows'), may hold values from 0 to 255, as said below
- tile_count: int32 [2, 128], P(None, 'rows'), may hold values from 1 to 8, as said below
Outputs:
- solution: float32 [3, 128, 256, 128], P(None, 'rows', 'cols')
The draws below stay inside these ranges and needn't reach their ends.
Inputs may be any that keep to these rules, and one draw needn't show every extreme that they name: `tile_source`: each source lies at a lower level than its target; supernode g mod 128 belongs to rows index (g mod 128) // 2, and that index differs from the target's by at most 7. The 8 sources of one supernode are distinct. `tile_count`: slots at or beyond the count hold no tile of the factor. At every target level some supernode has all 8 slots live. `diag_inv`: each block is lower triangular with a positive diagonal.
All inputs are finite; a program needn't handle non-finite values.
Results may differ from the reference program's by a relative error of at most 0.0003.
Values sent between devices are 32-bit elements; how exact they have to be, the bound alone decides.
A program may use at most 64 MiB of HBM per device.

```python
import math
import jax
import jax.numpy as jnp
from jax import lax

B = 256
NRHS = 128
SUP_DEV = 2
LEV = 3
TPS = 8
KDEV = 7
NSUP = 128


def draw_diag_inv(key, part):
    key_off, key_diag = jax.random.split(key, 2)
    row_ids = jnp.arange(B, dtype=jnp.int32)[:, None]
    col_ids = jnp.arange(B, dtype=jnp.int32)[None, :]
    below = (col_ids < row_ids).astype(jnp.float32)
    identity = (col_ids == row_ids).astype(jnp.float32)
    spread = 0.6 / math.sqrt(B)
    off_diag = jax.random.normal(key_off, (LEV, NSUP, B, B), jnp.float32) * spread
    diagonal = jax.random.uniform(key_diag, (LEV, NSUP, B, 1), jnp.float32, 0.6, 1.4)
    return off_diag * below + diagonal * identity


def draw_tile_source(key, part):
    row_total = NSUP // SUP_DEV
    window_len = 2 * KDEV + 1
    cand_total = (LEV - 1) * window_len * SUP_DEV
    candidate = jnp.arange(cand_total, dtype=jnp.int32)
    cand_level = candidate // (window_len * SUP_DEV)
    cand_offset = candidate // SUP_DEV % window_len - KDEV
    cand_slot = candidate % SUP_DEV
    target_level = jnp.arange(1, LEV, dtype=jnp.int32)[:, None, None]
    target = jnp.arange(NSUP, dtype=jnp.int32)[None, :, None]
    device = target // SUP_DEV + cand_offset
    valid = (cand_level < target_level) & (device >= 0) & (device < row_total)
    noise = jax.random.randint(key, (LEV - 1, NSUP, cand_total), 0, 1 << 20)
    score = jnp.where(valid, noise * cand_total + candidate, (1 << 30) + candidate)
    corner = (target_level == LEV - 1) & (target == NSUP - 1) | (target_level == 1) & (target == 0)
    forced = (cand_level == target_level - 1) & (cand_offset == 0) & (cand_slot == target % SUP_DEV)
    score = jnp.where(corner & forced, -1, score)
    picked = jnp.argsort(score, axis=-1)[:, :, :TPS]
    chosen_device = target // SUP_DEV + cand_offset[picked]
    return (cand_level[picked] * NSUP + chosen_device * SUP_DEV + cand_slot[picked]).astype(jnp.int32)


def draw_tile_count(key, part):
    key_base, key_hot, key_pick = jax.random.split(key, 3)
    base = jax.random.randint(key_base, (LEV - 1, NSUP), 1, min(5, TPS + 1))
    hot = jax.random.randint(key_hot, (LEV - 1, NSUP), 0, 8) == 0
    chosen = jax.random.randint(key_pick, (LEV - 1, 1), 0, NSUP)
    filled = hot | (jnp.arange(NSUP, dtype=jnp.int32)[None, :] == chosen)
    return jnp.where(filled, TPS, base).astype(jnp.int32)


def shard_levels(key, shape, shards, low, largest):
    gain = 1.0
    for position, blocks in shards:
        heights = jax.random.uniform(jax.random.fold_in(jax.random.fold_in(key, 6), position), (blocks,), jnp.float32, low / len(shards), largest / len(shards))
        gain = gain * jnp.repeat(jnp.exp(heights), shape[position] // blocks).reshape((-1,) + (1,) * (len(shape) - 1 - position))
    return gain


def bell_draw(key, shape, width, bound, pieces=(), kind=jnp.bfloat16):
    values = jax.random.normal(key, shape, jnp.float32) * width
    if len(pieces) > 0:
        values = shard_levels(key, shape, pieces, -0.22, 0.18) * values
    return jnp.clip(values, min=-bound, max=bound).astype(kind)


def setup_inputs(seed: int = 0) -> dict:
    arg_keys = jax.random.split(jax.random.key(seed), 6)
    rhs = bell_draw(arg_keys[0], (LEV, NSUP, B, NRHS), 1.0, 6.0, ((1, 64), (2, 8)), jnp.float32)
    diag_inv = draw_diag_inv(jax.random.fold_in(arg_keys[5], 71), 0)
    factor_tiles = bell_draw(arg_keys[2], (LEV - 1, NSUP, TPS, B, B), (TPS * B) ** -0.5, 0.125, ((1, 64), (3, 8)), jnp.float32)
    tile_source = draw_tile_source(jax.random.fold_in(arg_keys[5], 71), 0)
    tile_count = draw_tile_count(jax.random.fold_in(arg_keys[5], 71), 0)
    return {"rhs": rhs, "diag_inv": diag_inv, "factor_tiles": factor_tiles, "tile_source": tile_source, "tile_count": tile_count}


def reference(rhs, diag_inv, factor_tiles, tile_source, tile_count):
    highest = lax.Precision.HIGHEST
    slot_ids = jnp.arange(TPS, dtype=jnp.int32)
    forward = jnp.zeros((LEV * NSUP, B, NRHS), jnp.float32)
    for height in range(LEV):
        if height > 0:
            def update_one(operands):
                tile_set, sources, live_count = operands
                live_rows = (slot_ids < live_count).astype(jnp.float32)
                picked = forward[sources] * live_rows[:, None, None]
                return jnp.einsum("kji,kjr->ir", tile_set, picked, precision=highest)

            update_sum = lax.map(update_one, (factor_tiles[height - 1], tile_source[height - 1], tile_count[height - 1]))
            residual = rhs[height] - update_sum
        else:
            residual = rhs[height]
        values = jnp.einsum("sij,sjr->sir", diag_inv[height], residual, precision=highest)
        forward = forward.at[height * NSUP:(height + 1) * NSUP].set(values)
    carried = jnp.zeros((LEV * NSUP, B, NRHS), jnp.float32)
    solution = jnp.zeros((LEV * NSUP, B, NRHS), jnp.float32)
    for height in reversed(range(LEV)):
        first_row = height * NSUP
        last_row = (height + 1) * NSUP
        residual = forward[first_row:last_row] - carried[first_row:last_row]
        values = jnp.einsum("sji,sjr->sir", diag_inv[height], residual, precision=highest)
        solution = solution.at[first_row:last_row].set(values)
        if height > 0:
            def spread_one(carry_sum, operands):
                tile_set, sources, live_count, own_values = operands
                live_rows = (slot_ids < live_count).astype(jnp.float32)
                term_set = jnp.einsum("kji,ir->kjr", tile_set, own_values, precision=highest) * live_rows[:, None, None]
                return carry_sum.at[sources].add(term_set), None

            carried, unused = lax.scan(spread_one, carried, (factor_tiles[height - 1], tile_source[height - 1], tile_count[height - 1], values))
    return solution.reshape(LEV, NSUP, B, NRHS)
```

```python
import functools

import jax
import jax.numpy as jnp
from jax import lax
from jax.experimental import pallas as pl
from jax.experimental.pallas import tpu as pltpu
from jax.sharding import PartitionSpec as P

KDEV = 7
MESH = pl.DeviceIdType.MESH
OFFSETS = [d for d in range(-KDEV, KDEV + 1) if d != 0]


def _params(cid):
    return pltpu.CompilerParams(collective_id=cid, has_side_effects=True)


def _vmem():
    return pl.BlockSpec(memory_space=pltpu.VMEM)


def _cols_barrier(n, me, row):
    barrier = pltpu.get_barrier_semaphore()
    for k in range(1, n):
        pl.semaphore_signal(
            barrier, 1, device_id=(row, lax.rem(me + k, n)), device_id_type=MESH
        )
    pl.semaphore_wait(barrier, n - 1)


def _cols_copy(src_ref, dst_ref, send, recv, row, peer):
    return pltpu.make_async_remote_copy(
        src_ref=src_ref,
        dst_ref=dst_ref,
        send_sem=send,
        recv_sem=recv,
        device_id=(row, peer),
        device_id_type=MESH,
    )


def _scatter_phase(n, me, row, x_ref, base_ref, got, send, recv):
    sends = []
    for k in range(1, n):
        peer = lax.rem(me + k, n)
        c = _cols_copy(x_ref.at[peer], got.at[me], send.at[peer], recv.at[me], row, peer)
        c.start()
        sends.append(c)
    acc = base_ref[...] + x_ref[me]
    for k in range(1, n):
        src = lax.rem(me + n - k, n)
        c = _cols_copy(x_ref.at[src], got.at[src], send.at[src], recv.at[src], row, src)
        c.wait_recv()
        acc = acc + got[src]
    for c in sends:
        c.wait_send()
    return acc


def _gather_phase(n, me, row, src_ref, got, out_ref, send, recv):
    sends = []
    for k in range(1, n):
        peer = lax.rem(me + k, n)
        c = _cols_copy(src_ref, got.at[me], send.at[peer], recv.at[me], row, peer)
        c.start()
        sends.append(c)
    out_ref[me] = src_ref[...]
    for k in range(1, n):
        src = lax.rem(me + n - k, n)
        c = _cols_copy(src_ref, got.at[src], send.at[src], recv.at[src], row, src)
        c.wait_recv()
        out_ref[src] = got[src]
    for c in sends:
        c.wait_send()


def _allreduce_kernel(x_ref, base_ref, full_ref, own_ref, got1, got2, red, s1, r1, s2, r2):
    n = x_ref.shape[0]
    me = lax.axis_index("cols")
    row = lax.axis_index("rows")
    _cols_barrier(n, me, row)
    acc = _scatter_phase(n, me, row, x_ref, base_ref, got1, s1, r1)
    red[...] = acc
    own_ref[...] = acc
    _gather_phase(n, me, row, red, got2, full_ref, s2, r2)


def _reduce_scatter_kernel(x_ref, base_ref, own_ref, got1, s1, r1):
    n = x_ref.shape[0]
    me = lax.axis_index("cols")
    row = lax.axis_index("rows")
    _cols_barrier(n, me, row)
    own_ref[...] = _scatter_phase(n, me, row, x_ref, base_ref, got1, s1, r1)


def _all_gather_kernel(y_ref, full_ref, got2, s2, r2):
    n = full_ref.shape[0]
    me = lax.axis_index("cols")
    row = lax.axis_index("rows")
    _cols_barrier(n, me, row)
    _gather_phase(n, me, row, y_ref, got2, full_ref, s2, r2)


def cols_allreduce(x, base, cid):
    n = x.shape[0]
    blk = base.shape
    return pl.pallas_call(
        _allreduce_kernel,
        out_shape=(
            jax.ShapeDtypeStruct((n,) + blk, jnp.float32),
            jax.ShapeDtypeStruct(blk, jnp.float32),
        ),
        in_specs=[_vmem(), _vmem()],
        out_specs=(_vmem(), _vmem()),
        scratch_shapes=[
            pltpu.VMEM((n,) + blk, jnp.float32),
            pltpu.VMEM((n,) + blk, jnp.float32),
            pltpu.VMEM(blk, jnp.float32),
            pltpu.SemaphoreType.DMA((n,)),
            pltpu.SemaphoreType.DMA((n,)),
            pltpu.SemaphoreType.DMA((n,)),
            pltpu.SemaphoreType.DMA((n,)),
        ],
        compiler_params=_params(cid),
    )(x, base)


def cols_reduce_scatter(x, base, cid):
    n = x.shape[0]
    blk = base.shape
    return pl.pallas_call(
        _reduce_scatter_kernel,
        out_shape=jax.ShapeDtypeStruct(blk, jnp.float32),
        in_specs=[_vmem(), _vmem()],
        out_specs=_vmem(),
        scratch_shapes=[
            pltpu.VMEM((n,) + blk, jnp.float32),
            pltpu.SemaphoreType.DMA((n,)),
            pltpu.SemaphoreType.DMA((n,)),
        ],
        compiler_params=_params(cid),
    )(x, base)


def cols_all_gather(y, n, cid):
    blk = y.shape
    return pl.pallas_call(
        _all_gather_kernel,
        out_shape=jax.ShapeDtypeStruct((n,) + blk, jnp.float32),
        in_specs=[_vmem()],
        out_specs=_vmem(),
        scratch_shapes=[
            pltpu.VMEM((n,) + blk, jnp.float32),
            pltpu.SemaphoreType.DMA((n,)),
            pltpu.SemaphoreType.DMA((n,)),
        ],
        compiler_params=_params(cid),
    )(y)


def _rows_barrier(count, me, col):
    barrier = pltpu.get_barrier_semaphore()
    for d in OFFSETS:
        pl.semaphore_signal(
            barrier, 1, device_id=(lax.rem(me + d + count, count), col), device_id_type=MESH
        )
    pl.semaphore_wait(barrier, len(OFFSETS))


def _rows_copy(src_ref, dst_ref, send, recv, target, col):
    return pltpu.make_async_remote_copy(
        src_ref=src_ref,
        dst_ref=dst_ref,
        send_sem=send,
        recv_sem=recv,
        device_id=(target, col),
        device_id_type=MESH,
    )


def _rows_bcast_kernel(count, v_ref, win_ref, got, send, recv):
    me = lax.axis_index("rows")
    col = lax.axis_index("cols")
    _rows_barrier(count, me, col)
    sends = []
    for d in OFFSETS:
        target = lax.rem(me + d + count, count)
        c = _rows_copy(v_ref, got.at[KDEV - d], send.at[KDEV + d], recv.at[KDEV - d], target, col)
        c.start()
        sends.append(c)
    win_ref[KDEV] = v_ref[...]
    for o in OFFSETS:
        w = KDEV + o
        source = lax.rem(me + o + count, count)
        c = _rows_copy(v_ref, got.at[w], send.at[w], recv.at[w], source, col)
        c.wait_recv()
        win_ref[w] = got[w]
    for c in sends:
        c.wait_send()


def _rows_reduce_kernel(count, x_ref, sum_ref, got, send, recv):
    me = lax.axis_index("rows")
    col = lax.axis_index("cols")
    _rows_barrier(count, me, col)
    sends = []
    for d in OFFSETS:
        target = lax.rem(me + d + count, count)
        c = _rows_copy(
            x_ref.at[KDEV + d], got.at[KDEV - d], send.at[KDEV + d], recv.at[KDEV - d], target, col
        )
        c.start()
        sends.append(c)
    acc = x_ref[KDEV]
    for o in OFFSETS:
        w = KDEV + o
        source = lax.rem(me + o + count, count)
        c = _rows_copy(x_ref.at[w], got.at[w], send.at[w], recv.at[w], source, col)
        c.wait_recv()
        acc = acc + got[w]
    sum_ref[...] = acc
    for c in sends:
        c.wait_send()


def rows_bcast(v, count, cid):
    slots = 2 * KDEV + 1
    return pl.pallas_call(
        functools.partial(_rows_bcast_kernel, count),
        out_shape=jax.ShapeDtypeStruct((slots,) + v.shape, jnp.float32),
        in_specs=[_vmem()],
        out_specs=_vmem(),
        scratch_shapes=[
            pltpu.VMEM((slots,) + v.shape, jnp.float32),
            pltpu.SemaphoreType.DMA((slots,)),
            pltpu.SemaphoreType.DMA((slots,)),
        ],
        compiler_params=_params(cid),
    )(v)


def rows_reduce(x, count, cid):
    slots = 2 * KDEV + 1
    return pl.pallas_call(
        functools.partial(_rows_reduce_kernel, count),
        out_shape=jax.ShapeDtypeStruct(x.shape[1:], jnp.float32),
        in_specs=[_vmem()],
        out_specs=_vmem(),
        scratch_shapes=[
            pltpu.VMEM(x.shape, jnp.float32),
            pltpu.SemaphoreType.DMA((slots,)),
            pltpu.SemaphoreType.DMA((slots,)),
        ],
        compiler_params=_params(cid),
    )(x)


def to_chunks(block, n):
    s, rows, r = block.shape
    return block.reshape(s, n, rows // n, r).transpose(1, 0, 2, 3)


def from_chunks(chunks):
    n, s, c, r = chunks.shape
    return chunks.transpose(1, 0, 2, 3).reshape(s, n * c, r)


def local(rhs, diag_inv, factor_tiles, tile_source, tile_count):
    levels = rhs.shape[0]
    owned_count = rhs.shape[1]
    share_rows = rhs.shape[2]
    columns = rhs.shape[3]
    slot_count = tile_source.shape[2]
    reach_dev = KDEV
    window_len = 2 * reach_dev + 1
    row_count = lax.axis_size("rows")
    col_count = lax.axis_size("cols")
    total_sup = row_count * owned_count
    row_place = lax.axis_index("rows")
    highest = lax.Precision.HIGHEST
    slot_ids = jnp.arange(slot_count, dtype=jnp.int32)
    ids = iter(range(64))

    def window_places(sources):
        src_level = sources // total_sup
        within = sources % total_sup
        return (
            src_level * window_len + within // owned_count - row_place + reach_dev
        ) * owned_count + within % owned_count

    def live_mask(counts):
        return (slot_ids[None, :] < counts[:, None]).astype(jnp.float32)

    forward_values = []
    windows = []
    for height in range(levels):
        if height == 0:
            whole_block = from_chunks(cols_all_gather(rhs[0], col_count, next(ids)))
        else:
            stacked = jnp.stack(windows, 0).reshape(
                height * window_len * owned_count, share_rows, columns
            )
            places = window_places(tile_source[height - 1])
            picked = (
                jnp.take(stacked, places, axis=0)
                * live_mask(tile_count[height - 1])[:, :, None, None]
            )
            partial_value = jnp.einsum(
                "skci,skcr->sir", factor_tiles[height - 1], picked, precision=highest
            )
            full, unused = cols_allreduce(
                to_chunks(-partial_value, col_count), rhs[height], next(ids)
            )
            whole_block = from_chunks(full)
        values = jnp.einsum("sci,sir->scr", diag_inv[height], whole_block, precision=highest)
        forward_values.append(values)
        if height + 1 < levels:
            windows.append(rows_bcast(values, row_count, next(ids)))
    carried = [jnp.zeros_like(forward_values[0]) for height in range(levels)]
    solution = [None] * levels
    zero_block = jnp.zeros_like(forward_values[0])
    for height in reversed(range(levels)):
        partial_value = jnp.einsum(
            "sci,scr->sir",
            diag_inv[height],
            forward_values[height] - carried[height],
            precision=highest,
        )
        chunks = to_chunks(partial_value, col_count)
        if height > 0:
            full, own_share = cols_allreduce(chunks, zero_block, next(ids))
            whole_block = from_chunks(full)
        else:
            own_share = cols_reduce_scatter(chunks, zero_block, next(ids))
        solution[height] = own_share
        if height > 0:
            term_set = jnp.einsum(
                "skci,sir->skcr", factor_tiles[height - 1], whole_block, precision=highest
            )
            term_set = term_set * live_mask(tile_count[height - 1])[:, :, None, None]
            places = window_places(tile_source[height - 1]).reshape(-1)
            targets = height * window_len * owned_count
            one_hot = (jnp.arange(targets, dtype=jnp.int32)[:, None] == places[None, :]).astype(
                jnp.float32
            )
            outgoing = jnp.einsum(
                "ms,slg->mlg",
                one_hot,
                term_set.reshape(owned_count * slot_count, share_rows, columns),
                precision=highest,
            )
            push_outgoing = outgoing.reshape(height, window_len, owned_count, share_rows, columns)
            received = rows_reduce(
                push_outgoing.transpose(1, 0, 2, 3, 4), row_count, next(ids)
            )
            for lower_level in range(height):
                carried[lower_level] = carried[lower_level] + received[lower_level]
    return jnp.stack(solution, 0)


def solution(mesh):
    placed = (
        P(None, "rows", "cols", None),
        P(None, "rows", "cols", None),
        P(None, "rows", None, "cols", None),
        P(None, "rows", None),
        P(None, "rows"),
    )
    return jax.shard_map(
        local, mesh=mesh, in_specs=placed, out_specs=P(None, "rows", "cols", None), check_vma=False
    )
```

```python
import functools

import jax
import jax.numpy as jnp
from jax import lax
from jax.experimental import pallas as pl
from jax.experimental.pallas import tpu as pltpu
from jax.sharding import PartitionSpec as P

KDEV = 7
MESH = pl.DeviceIdType.MESH
OFFSETS = [d for d in range(-KDEV, KDEV + 1) if d != 0]


def _params(cid):
    return pltpu.CompilerParams(collective_id=cid, has_side_effects=True)


def _vmem():
    return pl.BlockSpec(memory_space=pltpu.VMEM)


def _cols_barrier(n, me, row):
    barrier = pltpu.get_barrier_semaphore()
    for k in range(1, n):
        pl.semaphore_signal(
            barrier, 1, device_id=(row, lax.rem(me + k, n)), device_id_type=MESH
        )
    pl.semaphore_wait(barrier, n - 1)


def _cols_copy(src_ref, dst_ref, send, recv, row, peer):
    return pltpu.make_async_remote_copy(
        src_ref=src_ref,
        dst_ref=dst_ref,
        send_sem=send,
        recv_sem=recv,
        device_id=(row, peer),
        device_id_type=MESH,
    )


def _rows_of(ref, index, chunk):
    return ref.at[:, pl.ds(pl.multiple_of(index * chunk, chunk), chunk), :]


def _reduce_scatter_kernel(x_ref, own_ref, got, send, recv):
    n = got.shape[0]
    chunk = got.shape[2]
    me = lax.axis_index("cols")
    row = lax.axis_index("rows")
    _cols_barrier(n, me, row)
    sends = []
    for k in range(1, n):
        peer = lax.rem(me + k, n)
        c = _cols_copy(_rows_of(x_ref, peer, chunk), got.at[me], send.at[peer], recv.at[me], row, peer)
        c.start()
        sends.append(c)
    acc = _rows_of(x_ref, me, chunk)[...]
    for k in range(1, n):
        src = lax.rem(me + n - k, n)
        c = _cols_copy(_rows_of(x_ref, src, chunk), got.at[src], send.at[src], recv.at[src], row, src)
        c.wait_recv()
        acc = acc + got[src]
    own_ref[...] = acc
    for c in sends:
        c.wait_send()


def _all_gather_kernel(y_ref, full_ref, got, send, recv):
    n = got.shape[0]
    chunk = got.shape[2]
    me = lax.axis_index("cols")
    row = lax.axis_index("rows")
    _cols_barrier(n, me, row)
    sends = []
    for k in range(1, n):
        peer = lax.rem(me + k, n)
        c = _cols_copy(y_ref, got.at[me], send.at[peer], recv.at[me], row, peer)
        c.start()
        sends.append(c)
    _rows_of(full_ref, me, chunk)[...] = y_ref[...]
    for k in range(1, n):
        src = lax.rem(me + n - k, n)
        c = _cols_copy(y_ref, got.at[src], send.at[src], recv.at[src], row, src)
        c.wait_recv()
        _rows_of(full_ref, src, chunk)[...] = got[src]
    for c in sends:
        c.wait_send()


def cols_reduce_scatter(x, n, cid):
    s, rows, r = x.shape
    blk = (s, rows // n, r)
    return pl.pallas_call(
        _reduce_scatter_kernel,
        out_shape=jax.ShapeDtypeStruct(blk, jnp.float32),
        in_specs=[_vmem()],
        out_specs=_vmem(),
        scratch_shapes=[
            pltpu.VMEM((n,) + blk, jnp.float32),
            pltpu.SemaphoreType.DMA((n,)),
            pltpu.SemaphoreType.DMA((n,)),
        ],
        compiler_params=_params(cid),
    )(x)


def cols_all_gather(y, n, cid):
    s, chunk, r = y.shape
    return pl.pallas_call(
        _all_gather_kernel,
        out_shape=jax.ShapeDtypeStruct((s, n * chunk, r), jnp.float32),
        in_specs=[_vmem()],
        out_specs=_vmem(),
        scratch_shapes=[
            pltpu.VMEM((n,) + y.shape, jnp.float32),
            pltpu.SemaphoreType.DMA((n,)),
            pltpu.SemaphoreType.DMA((n,)),
        ],
        compiler_params=_params(cid),
    )(y)


def _rows_barrier(count, me, col):
    barrier = pltpu.get_barrier_semaphore()
    for d in OFFSETS:
        pl.semaphore_signal(
            barrier, 1, device_id=(lax.rem(me + d + count, count), col), device_id_type=MESH
        )
    pl.semaphore_wait(barrier, len(OFFSETS))


def _rows_copy(src_ref, dst_ref, send, recv, target, col):
    return pltpu.make_async_remote_copy(
        src_ref=src_ref,
        dst_ref=dst_ref,
        send_sem=send,
        recv_sem=recv,
        device_id=(target, col),
        device_id_type=MESH,
    )


def _rows_bcast_kernel(count, v_ref, win_ref, got, send, recv):
    me = lax.axis_index("rows")
    col = lax.axis_index("cols")
    _rows_barrier(count, me, col)
    sends = []
    for d in OFFSETS:
        target = lax.rem(me + d + count, count)
        c = _rows_copy(v_ref, got.at[KDEV - d], send.at[KDEV + d], recv.at[KDEV - d], target, col)
        c.start()
        sends.append(c)
    win_ref[KDEV] = v_ref[...]
    for o in OFFSETS:
        w = KDEV + o
        source = lax.rem(me + o + count, count)
        c = _rows_copy(v_ref, got.at[w], send.at[w], recv.at[w], source, col)
        c.wait_recv()
        win_ref[w] = got[w]
    for c in sends:
        c.wait_send()


def _rows_reduce_kernel(count, x_ref, sum_ref, got, send, recv):
    me = lax.axis_index("rows")
    col = lax.axis_index("cols")
    _rows_barrier(count, me, col)
    sends = []
    for d in OFFSETS:
        target = lax.rem(me + d + count, count)
        c = _rows_copy(
            x_ref.at[KDEV + d], got.at[KDEV - d], send.at[KDEV + d], recv.at[KDEV - d], target, col
        )
        c.start()
        sends.append(c)
    acc = x_ref[KDEV]
    for o in OFFSETS:
        w = KDEV + o
        source = lax.rem(me + o + count, count)
        c = _rows_copy(x_ref.at[w], got.at[w], send.at[w], recv.at[w], source, col)
        c.wait_recv()
        acc = acc + got[w]
    sum_ref[...] = acc
    for c in sends:
        c.wait_send()


def rows_bcast(v, count, cid):
    slots = 2 * KDEV + 1
    return pl.pallas_call(
        functools.partial(_rows_bcast_kernel, count),
        out_shape=jax.ShapeDtypeStruct((slots,) + v.shape, jnp.float32),
        in_specs=[_vmem()],
        out_specs=_vmem(),
        scratch_shapes=[
            pltpu.VMEM((slots,) + v.shape, jnp.float32),
            pltpu.SemaphoreType.DMA((slots,)),
            pltpu.SemaphoreType.DMA((slots,)),
        ],
        compiler_params=_params(cid),
    )(v)


def rows_reduce(x, count, cid):
    slots = 2 * KDEV + 1
    return pl.pallas_call(
        functools.partial(_rows_reduce_kernel, count),
        out_shape=jax.ShapeDtypeStruct(x.shape[1:], jnp.float32),
        in_specs=[_vmem()],
        out_specs=_vmem(),
        scratch_shapes=[
            pltpu.VMEM(x.shape, jnp.float32),
            pltpu.SemaphoreType.DMA((slots,)),
            pltpu.SemaphoreType.DMA((slots,)),
        ],
        compiler_params=_params(cid),
    )(x)


def local(rhs, diag_inv, factor_tiles, tile_source, tile_count):
    levels = rhs.shape[0]
    owned_count = rhs.shape[1]
    share_rows = rhs.shape[2]
    columns = rhs.shape[3]
    slot_count = tile_source.shape[2]
    reach_dev = KDEV
    window_len = 2 * reach_dev + 1
    row_count = lax.axis_size("rows")
    col_count = lax.axis_size("cols")
    total_sup = row_count * owned_count
    row_place = lax.axis_index("rows")
    my_rows = lax.axis_index("cols") * share_rows
    highest = lax.Precision.HIGHEST
    slot_ids = jnp.arange(slot_count, dtype=jnp.int32)
    ids = iter(range(64))
    diag_whole = lax.all_gather(diag_inv[1:], "cols", axis=2, tiled=True)

    def window_places(sources):
        src_level = sources // total_sup
        within = sources % total_sup
        return (
            src_level * window_len + within // owned_count - row_place + reach_dev
        ) * owned_count + within % owned_count

    def live_mask(counts):
        return (slot_ids[None, :] < counts[:, None]).astype(jnp.float32)

    def own_rows(block):
        return lax.dynamic_slice_in_dim(block, my_rows, share_rows, axis=1)

    forward_values = []
    windows = []
    for height in range(levels):
        if height == 0:
            whole_block = cols_all_gather(rhs[0], col_count, next(ids))
            values = jnp.einsum("sci,sir->scr", diag_inv[0], whole_block, precision=highest)
        else:
            stacked = jnp.stack(windows, 0).reshape(
                height * window_len * owned_count, share_rows, columns
            )
            places = window_places(tile_source[height - 1])
            picked = (
                jnp.take(stacked, places, axis=0)
                * live_mask(tile_count[height - 1])[:, :, None, None]
            )
            partial_value = jnp.einsum(
                "skci,skcr->sir", factor_tiles[height - 1], picked, precision=highest
            )
            share = lax.dynamic_update_slice_in_dim(
                -partial_value, rhs[height] - own_rows(partial_value), my_rows, axis=1
            )
            spread = jnp.einsum(
                "sij,sjr->sir", diag_whole[height - 1], share, precision=highest
            )
            values = cols_reduce_scatter(spread, col_count, next(ids))
        forward_values.append(values)
        if height + 1 < levels:
            windows.append(rows_bcast(values, row_count, next(ids)))
    carried = [jnp.zeros_like(forward_values[0]) for height in range(levels)]
    solution = [None] * levels
    for height in reversed(range(levels)):
        residual = forward_values[height] - carried[height]
        if height > 0:
            whole_residual = cols_all_gather(residual, col_count, next(ids))
            whole_block = jnp.einsum(
                "sji,sjr->sir", diag_whole[height - 1], whole_residual, precision=highest
            )
            solution[height] = own_rows(whole_block)
        else:
            partial_value = jnp.einsum(
                "sci,scr->sir", diag_inv[0], residual, precision=highest
            )
            solution[height] = cols_reduce_scatter(partial_value, col_count, next(ids))
        if height > 0:
            term_set = jnp.einsum(
                "skci,sir->skcr", factor_tiles[height - 1], whole_block, precision=highest
            )
            term_set = term_set * live_mask(tile_count[height - 1])[:, :, None, None]
            places = window_places(tile_source[height - 1]).reshape(-1)
            targets = height * window_len * owned_count
            one_hot = (jnp.arange(targets, dtype=jnp.int32)[:, None] == places[None, :]).astype(
                jnp.float32
            )
            outgoing = jnp.einsum(
                "ms,slg->mlg",
                one_hot,
                term_set.reshape(owned_count * slot_count, share_rows, columns),
                precision=highest,
            )
            push_outgoing = outgoing.reshape(height, window_len, owned_count, share_rows, columns)
            received = rows_reduce(
                push_outgoing.transpose(1, 0, 2, 3, 4), row_count, next(ids)
            )
            for lower_level in range(height):
                carried[lower_level] = carried[lower_level] + received[lower_level]
    return jnp.stack(solution, 0)


def solution(mesh):
    placed = (
        P(None, "rows", "cols", None),
        P(None, "rows", "cols", None),
        P(None, "rows", None, "cols", None),
        P(None, "rows", None),
        P(None, "rows"),
    )
    return jax.shard_map(
        local, mesh=mesh, in_specs=placed, out_specs=P(None, "rows", "cols", None), check_vma=False
    )
```

```python
import functools

import jax
import jax.numpy as jnp
from jax import lax
from jax.experimental import pallas as pl
from jax.experimental.pallas import tpu as pltpu
from jax.sharding import PartitionSpec as P

KDEV = 7
MESH = pl.DeviceIdType.MESH
OFFSETS = [d for d in range(-KDEV, KDEV + 1) if d != 0]


def _params(cid):
    return pltpu.CompilerParams(collective_id=cid, has_side_effects=True)


def _vmem():
    return pl.BlockSpec(memory_space=pltpu.VMEM)


class Place:
    def __init__(self, n, count):
        self.n = n
        self.count = count
        self.col = lax.axis_index("cols")
        self.row = lax.axis_index("rows")

    def col_peer(self, k):
        return lax.rem(self.col + k, self.n)

    def row_peer(self, d):
        return lax.rem(self.row + d + self.count, self.count)

    def barrier(self, cols, rows):
        targets = []
        if cols:
            targets += [(self.row, self.col_peer(k)) for k in range(1, self.n)]
        if rows:
            targets += [(self.row_peer(d), self.col) for d in OFFSETS]
        barrier = pltpu.get_barrier_semaphore()
        for t in targets:
            pl.semaphore_signal(barrier, 1, device_id=t, device_id_type=MESH)
        pl.semaphore_wait(barrier, len(targets))


def _copy(src_ref, dst_ref, send, recv, device):
    return pltpu.make_async_remote_copy(
        src_ref=src_ref,
        dst_ref=dst_ref,
        send_sem=send,
        recv_sem=recv,
        device_id=device,
        device_id_type=MESH,
    )


def _rows_of(ref, index, chunk):
    return ref.at[:, pl.ds(pl.multiple_of(index * chunk, chunk), chunk), :]


def _start_all(copies):
    for c in copies:
        c.start()
    return copies


def _wait_sends(copies):
    for c in copies:
        c.wait_send()


def scatter_start(p, x_ref, got, send, recv):
    chunk = got.shape[2]
    out = []
    for k in range(1, p.n):
        peer = p.col_peer(k)
        out.append(
            _copy(_rows_of(x_ref, peer, chunk), got.at[p.col], send.at[peer], recv.at[p.col], (p.row, peer))
        )
    return _start_all(out)


def scatter_finish(p, x_ref, got, send, recv):
    chunk = got.shape[2]
    acc = _rows_of(x_ref, p.col, chunk)[...]
    for k in range(1, p.n):
        src = p.col_peer(p.n - k)
        _copy(_rows_of(x_ref, src, chunk), got.at[src], send.at[src], recv.at[src], (p.row, src)).wait_recv()
        acc = acc + got[src]
    return acc


def gather_start(p, y_ref, got, send, recv):
    out = []
    for k in range(1, p.n):
        peer = p.col_peer(k)
        out.append(_copy(y_ref, got.at[p.col], send.at[peer], recv.at[p.col], (p.row, peer)))
    return _start_all(out)


def gather_finish(p, y_ref, got, send, recv, full_ref):
    chunk = got.shape[2]
    _rows_of(full_ref, p.col, chunk)[...] = y_ref[...]
    for k in range(1, p.n):
        src = p.col_peer(p.n - k)
        _copy(y_ref, got.at[src], send.at[src], recv.at[src], (p.row, src)).wait_recv()
        _rows_of(full_ref, src, chunk)[...] = got[src]


def bcast_start(p, v_ref, got, send, recv):
    out = []
    for d in OFFSETS:
        out.append(_copy(v_ref, got.at[KDEV - d], send.at[KDEV + d], recv.at[KDEV - d], (p.row_peer(d), p.col)))
    return _start_all(out)


def bcast_finish(p, v_ref, got, send, recv, win_ref):
    win_ref[KDEV] = v_ref[...]
    for o in OFFSETS:
        w = KDEV + o
        _copy(v_ref, got.at[w], send.at[w], recv.at[w], (p.row_peer(o), p.col)).wait_recv()
        win_ref[w] = got[w]


def spread_start(p, x_ref, got, send, recv):
    out = []
    for d in OFFSETS:
        out.append(
            _copy(x_ref.at[KDEV + d], got.at[KDEV - d], send.at[KDEV + d], recv.at[KDEV - d], (p.row_peer(d), p.col))
        )
    return _start_all(out)


def spread_finish(p, x_ref, got, send, recv):
    acc = x_ref[KDEV]
    for o in OFFSETS:
        w = KDEV + o
        _copy(x_ref.at[w], got.at[w], send.at[w], recv.at[w], (p.row_peer(o), p.col)).wait_recv()
        acc = acc + got[w]
    return acc


def _gather_kernel(n, count, y_ref, full_ref, got, s, r):
    p = Place(n, count)
    p.barrier(True, False)
    sends = gather_start(p, y_ref, got, s, r)
    gather_finish(p, y_ref, got, s, r, full_ref)
    _wait_sends(sends)


def _scatter_kernel(n, count, x_ref, own_ref, got, s, r):
    p = Place(n, count)
    p.barrier(True, False)
    sends = scatter_start(p, x_ref, got, s, r)
    own_ref[...] = scatter_finish(p, x_ref, got, s, r)
    _wait_sends(sends)


def _bcast_gather_kernel(n, count, v_ref, d_ref, win_ref, dfull_ref, got_w, sw, rw, got_d, sd, rd):
    p = Place(n, count)
    p.barrier(True, True)
    sends = bcast_start(p, v_ref, got_w, sw, rw) + gather_start(p, d_ref, got_d, sd, rd)
    bcast_finish(p, v_ref, got_w, sw, rw, win_ref)
    gather_finish(p, d_ref, got_d, sd, rd, dfull_ref)
    _wait_sends(sends)


def _scatter_bcast_gather_kernel(
    n, count, x_ref, d_ref, own_ref, win_ref, dfull_ref, got_x, sx, rx, got_w, sw, rw, got_d, sd, rd
):
    p = Place(n, count)
    p.barrier(True, True)
    sends = scatter_start(p, x_ref, got_x, sx, rx)
    own_ref[...] = scatter_finish(p, x_ref, got_x, sx, rx)
    sends += bcast_start(p, own_ref, got_w, sw, rw) + gather_start(p, d_ref, got_d, sd, rd)
    bcast_finish(p, own_ref, got_w, sw, rw, win_ref)
    gather_finish(p, d_ref, got_d, sd, rd, dfull_ref)
    _wait_sends(sends)


def _scatter_gather_kernel(n, count, x_ref, own_ref, full_ref, got_x, sx, rx, got_y, sy, ry):
    p = Place(n, count)
    p.barrier(True, False)
    sends = scatter_start(p, x_ref, got_x, sx, rx)
    own_ref[...] = scatter_finish(p, x_ref, got_x, sx, rx)
    sends += gather_start(p, own_ref, got_y, sy, ry)
    gather_finish(p, own_ref, got_y, sy, ry, full_ref)
    _wait_sends(sends)


def _spread_gather_kernel(n, count, x_ref, f_ref, sum_ref, full_ref, got_b, sb, rb, res, got_y, sy, ry):
    p = Place(n, count)
    p.barrier(True, True)
    sends = spread_start(p, x_ref, got_b, sb, rb)
    acc = spread_finish(p, x_ref, got_b, sb, rb)
    sum_ref[...] = acc
    res[...] = f_ref[...] - acc[acc.shape[0] - 1]
    sends += gather_start(p, res, got_y, sy, ry)
    gather_finish(p, res, got_y, sy, ry, full_ref)
    _wait_sends(sends)


def _spread_kernel(n, count, x_ref, sum_ref, got_b, sb, rb):
    p = Place(n, count)
    p.barrier(False, True)
    sends = spread_start(p, x_ref, got_b, sb, rb)
    sum_ref[...] = spread_finish(p, x_ref, got_b, sb, rb)
    _wait_sends(sends)


def _f32(shape):
    return jax.ShapeDtypeStruct(shape, jnp.float32)


def _dma(k):
    return [pltpu.SemaphoreType.DMA((k,)), pltpu.SemaphoreType.DMA((k,))]


def _call(body, n, count, cid, args, outs, scratch):
    return pl.pallas_call(
        functools.partial(body, n, count),
        out_shape=tuple(_f32(o) for o in outs),
        in_specs=[_vmem() for a in args],
        out_specs=tuple(_vmem() for o in outs),
        scratch_shapes=scratch,
        compiler_params=_params(cid),
    )(*args)


def local(rhs, diag_inv, factor_tiles, tile_source, tile_count):
    levels = rhs.shape[0]
    owned_count = rhs.shape[1]
    share_rows = rhs.shape[2]
    columns = rhs.shape[3]
    slot_count = tile_source.shape[2]
    reach_dev = KDEV
    window_len = 2 * reach_dev + 1
    n = lax.axis_size("cols")
    count = lax.axis_size("rows")
    total_sup = count * owned_count
    row_place = lax.axis_index("rows")
    my_rows = lax.axis_index("cols") * share_rows
    highest = lax.Precision.HIGHEST
    slot_ids = jnp.arange(slot_count, dtype=jnp.int32)
    assert levels == 3 and count >= window_len
    blk = (owned_count, share_rows, columns)
    whole = (owned_count, n * share_rows, columns)
    dblk = diag_inv.shape[1:]
    dwhole = (owned_count, n * share_rows, diag_inv.shape[3])
    win = (window_len,) + blk
    slots = window_len

    def window_places(sources):
        src_level = sources // total_sup
        within = sources % total_sup
        return (
            src_level * window_len + within // owned_count - row_place + reach_dev
        ) * owned_count + within % owned_count

    def live_mask(counts):
        return (slot_ids[None, :] < counts[:, None]).astype(jnp.float32)

    def own_rows(block):
        return lax.dynamic_slice_in_dim(block, my_rows, share_rows, axis=1)

    def forward_share(height, windows):
        stacked = jnp.stack(windows, 0).reshape(height * window_len * owned_count, share_rows, columns)
        places = window_places(tile_source[height - 1])
        picked = jnp.take(stacked, places, axis=0) * live_mask(tile_count[height - 1])[:, :, None, None]
        partial_value = jnp.einsum(
            "skci,skcr->sir", factor_tiles[height - 1], picked, precision=highest
        )
        return lax.dynamic_update_slice_in_dim(
            -partial_value, rhs[height] - own_rows(partial_value), my_rows, axis=1
        )

    def buckets(height, whole_block):
        term_set = jnp.einsum(
            "skci,sir->skcr", factor_tiles[height - 1], whole_block, precision=highest
        )
        term_set = term_set * live_mask(tile_count[height - 1])[:, :, None, None]
        places = window_places(tile_source[height - 1]).reshape(-1)
        targets = height * window_len * owned_count
        one_hot = (jnp.arange(targets, dtype=jnp.int32)[:, None] == places[None, :]).astype(
            jnp.float32
        )
        outgoing = jnp.einsum(
            "ms,slg->mlg",
            one_hot,
            term_set.reshape(owned_count * slot_count, share_rows, columns),
            precision=highest,
        )
        push_outgoing = outgoing.reshape(height, window_len, owned_count, share_rows, columns)
        return push_outgoing.transpose(1, 0, 2, 3, 4)

    (whole0,) = _call(_gather_kernel, n, count, 0, [rhs[0]], [whole], [pltpu.VMEM((n,) + blk, jnp.float32)] + _dma(n))
    fv0 = jnp.einsum("sci,sir->scr", diag_inv[0], whole0, precision=highest)
    win0, d1 = _call(
        _bcast_gather_kernel, n, count, 1, [fv0, diag_inv[1]], [win, dwhole],
        [pltpu.VMEM(win, jnp.float32)] + _dma(slots) + [pltpu.VMEM((n,) + dblk, jnp.float32)] + _dma(n),
    )
    spread1 = jnp.einsum("sij,sjr->sir", d1, forward_share(1, [win0]), precision=highest)
    fv1, win1, d2 = _call(
        _scatter_bcast_gather_kernel, n, count, 2, [spread1, diag_inv[2]], [blk, win, dwhole],
        [pltpu.VMEM((n,) + blk, jnp.float32)] + _dma(n)
        + [pltpu.VMEM(win, jnp.float32)] + _dma(slots)
        + [pltpu.VMEM((n,) + dblk, jnp.float32)] + _dma(n),
    )
    spread2 = jnp.einsum("sij,sjr->sir", d2, forward_share(2, [win0, win1]), precision=highest)
    fv2, whole_res2 = _call(
        _scatter_gather_kernel, n, count, 3, [spread2], [blk, whole],
        [pltpu.VMEM((n,) + blk, jnp.float32)] + _dma(n) + [pltpu.VMEM((n,) + blk, jnp.float32)] + _dma(n),
    )
    sol2 = jnp.einsum("sji,sjr->sir", d2, whole_res2, precision=highest)
    out2 = buckets(2, sol2)
    got2, whole_res1 = _call(
        _spread_gather_kernel, n, count, 4, [out2, fv1], [out2.shape[1:], whole],
        [pltpu.VMEM(out2.shape, jnp.float32)] + _dma(slots)
        + [pltpu.VMEM(blk, jnp.float32), pltpu.VMEM((n,) + blk, jnp.float32)] + _dma(n),
    )
    sol1 = jnp.einsum("sji,sjr->sir", d1, whole_res1, precision=highest)
    out1 = buckets(1, sol1)
    (got1,) = _call(
        _spread_kernel, n, count, 5, [out1], [out1.shape[1:]],
        [pltpu.VMEM(out1.shape, jnp.float32)] + _dma(slots),
    )
    res0 = fv0 - (got2[0] + got1[0])
    partial0 = jnp.einsum("sci,scr->sir", diag_inv[0], res0, precision=highest)
    (sol0,) = _call(_scatter_kernel, n, count, 6, [partial0], [blk], [pltpu.VMEM((n,) + blk, jnp.float32)] + _dma(n))
    return jnp.stack([sol0, own_rows(sol1), own_rows(sol2)], 0)


def solution(mesh):
    placed = (
        P(None, "rows", "cols", None),
        P(None, "rows", "cols", None),
        P(None, "rows", None, "cols", None),
        P(None, "rows", None),
        P(None, "rows"),
    )
    return jax.shard_map(
        local, mesh=mesh, in_specs=placed, out_specs=P(None, "rows", "cols", None), check_vma=False
    )
```

```python
import functools

import jax
import jax.numpy as jnp
from jax import lax
from jax.experimental import pallas as pl
from jax.experimental.pallas import tpu as pltpu
from jax.sharding import PartitionSpec as P

KDEV = 7
MESH = pl.DeviceIdType.MESH
OFFSETS = [d for d in range(-KDEV, KDEV + 1) if d != 0]


def _params(cid):
    return pltpu.CompilerParams(collective_id=cid, has_side_effects=True)


def _vmem():
    return pl.BlockSpec(memory_space=pltpu.VMEM)


class Place:
    def __init__(self, n, count):
        self.n = n
        self.count = count
        self.col = lax.axis_index("cols")
        self.row = lax.axis_index("rows")

    def col_peer(self, k):
        return lax.rem(self.col + k, self.n)

    def row_peer(self, d):
        return lax.rem(self.row + d + self.count, self.count)

    def barrier(self, cols, rows):
        targets = []
        if cols:
            targets += [(self.row, self.col_peer(k)) for k in range(1, self.n)]
        if rows:
            targets += [(self.row_peer(d), self.col) for d in OFFSETS]
        barrier = pltpu.get_barrier_semaphore()
        for t in targets:
            pl.semaphore_signal(barrier, 1, device_id=t, device_id_type=MESH)
        pl.semaphore_wait(barrier, len(targets))


def _copy(src_ref, dst_ref, send, recv, device):
    return pltpu.make_async_remote_copy(
        src_ref=src_ref,
        dst_ref=dst_ref,
        send_sem=send,
        recv_sem=recv,
        device_id=device,
        device_id_type=MESH,
    )


def _rows_of(ref, index, chunk):
    return ref.at[:, pl.ds(pl.multiple_of(index * chunk, chunk), chunk), :]


def _start_all(copies):
    for c in copies:
        c.start()
    return copies


def _wait_sends(copies):
    for c in copies:
        c.wait_send()


def scatter_start(p, x_ref, got, send, recv):
    chunk = got.shape[2]
    out = []
    for k in range(1, p.n):
        peer = p.col_peer(k)
        out.append(
            _copy(_rows_of(x_ref, peer, chunk), got.at[p.col], send.at[peer], recv.at[p.col], (p.row, peer))
        )
    return _start_all(out)


def scatter_finish(p, x_ref, got, send, recv):
    chunk = got.shape[2]
    acc = _rows_of(x_ref, p.col, chunk)[...]
    for k in range(1, p.n):
        src = p.col_peer(p.n - k)
        _copy(_rows_of(x_ref, src, chunk), got.at[src], send.at[src], recv.at[src], (p.row, src)).wait_recv()
        acc = acc + got[src]
    return acc


def gather_start(p, y_ref, got, send, recv):
    out = []
    for k in range(1, p.n):
        peer = p.col_peer(k)
        out.append(_copy(y_ref, got.at[p.col], send.at[peer], recv.at[p.col], (p.row, peer)))
    return _start_all(out)


def gather_finish(p, y_ref, got, send, recv, full_ref):
    chunk = got.shape[2]
    _rows_of(full_ref, p.col, chunk)[...] = y_ref[...]
    for k in range(1, p.n):
        src = p.col_peer(p.n - k)
        _copy(y_ref, got.at[src], send.at[src], recv.at[src], (p.row, src)).wait_recv()
        _rows_of(full_ref, src, chunk)[...] = got[src]


def bcast_start(p, v_ref, got, send, recv):
    out = []
    for d in OFFSETS:
        out.append(_copy(v_ref, got.at[KDEV - d], send.at[KDEV + d], recv.at[KDEV - d], (p.row_peer(d), p.col)))
    return _start_all(out)


def bcast_finish(p, v_ref, got, send, recv, win_ref):
    win_ref[KDEV] = v_ref[...]
    for o in OFFSETS:
        w = KDEV + o
        _copy(v_ref, got.at[w], send.at[w], recv.at[w], (p.row_peer(o), p.col)).wait_recv()
        win_ref[w] = got[w]


def spread_start(p, x_ref, got, send, recv):
    out = []
    for d in OFFSETS:
        out.append(
            _copy(x_ref.at[KDEV + d], got.at[KDEV - d], send.at[KDEV + d], recv.at[KDEV - d], (p.row_peer(d), p.col))
        )
    return _start_all(out)


def spread_finish(p, x_ref, got, send, recv):
    acc = x_ref[KDEV]
    for o in OFFSETS:
        w = KDEV + o
        _copy(x_ref.at[w], got.at[w], send.at[w], recv.at[w], (p.row_peer(o), p.col)).wait_recv()
        acc = acc + got[w]
    return acc


def _gather_kernel(n, count, y_ref, full_ref, got, s, r):
    p = Place(n, count)
    p.barrier(True, False)
    sends = gather_start(p, y_ref, got, s, r)
    gather_finish(p, y_ref, got, s, r, full_ref)
    _wait_sends(sends)


def _scatter_kernel(n, count, x_ref, own_ref, got, s, r):
    p = Place(n, count)
    p.barrier(True, False)
    sends = scatter_start(p, x_ref, got, s, r)
    own_ref[...] = scatter_finish(p, x_ref, got, s, r)
    _wait_sends(sends)


def _bcast_gather_kernel(n, count, v_ref, d_ref, win_ref, dfull_ref, got_w, sw, rw, got_d, sd, rd):
    p = Place(n, count)
    p.barrier(True, True)
    sends = bcast_start(p, v_ref, got_w, sw, rw) + gather_start(p, d_ref, got_d, sd, rd)
    bcast_finish(p, v_ref, got_w, sw, rw, win_ref)
    gather_finish(p, d_ref, got_d, sd, rd, dfull_ref)
    _wait_sends(sends)


def _scatter_bcast_gather_kernel(
    n, count, x_ref, d_ref, own_ref, win_ref, dfull_ref, got_x, sx, rx, got_w, sw, rw, got_d, sd, rd
):
    p = Place(n, count)
    p.barrier(True, True)
    sends = scatter_start(p, x_ref, got_x, sx, rx)
    own_ref[...] = scatter_finish(p, x_ref, got_x, sx, rx)
    sends += bcast_start(p, own_ref, got_w, sw, rw) + gather_start(p, d_ref, got_d, sd, rd)
    bcast_finish(p, own_ref, got_w, sw, rw, win_ref)
    gather_finish(p, d_ref, got_d, sd, rd, dfull_ref)
    _wait_sends(sends)


def _scatter_gather_kernel(n, count, x_ref, own_ref, full_ref, got_x, sx, rx, got_y, sy, ry):
    p = Place(n, count)
    p.barrier(True, False)
    sends = scatter_start(p, x_ref, got_x, sx, rx)
    own_ref[...] = scatter_finish(p, x_ref, got_x, sx, rx)
    sends += gather_start(p, own_ref, got_y, sy, ry)
    gather_finish(p, own_ref, got_y, sy, ry, full_ref)
    _wait_sends(sends)


def _spread_gather_kernel(n, count, x_ref, f_ref, sum_ref, full_ref, got_b, sb, rb, res, got_y, sy, ry):
    p = Place(n, count)
    p.barrier(True, True)
    sends = spread_start(p, x_ref, got_b, sb, rb)
    acc = spread_finish(p, x_ref, got_b, sb, rb)
    sum_ref[...] = acc
    res[...] = f_ref[...] - acc[acc.shape[0] - 1]
    sends += gather_start(p, res, got_y, sy, ry)
    gather_finish(p, res, got_y, sy, ry, full_ref)
    _wait_sends(sends)


def _spread_kernel(n, count, x_ref, sum_ref, got_b, sb, rb):
    p = Place(n, count)
    p.barrier(False, True)
    sends = spread_start(p, x_ref, got_b, sb, rb)
    sum_ref[...] = spread_finish(p, x_ref, got_b, sb, rb)
    _wait_sends(sends)


def _dots(a_ref, b_ref, transpose_a=False):
    outs = []
    for s in range(a_ref.shape[0]):
        a = a_ref[s]
        if transpose_a:
            a = a.T
        outs.append(jnp.dot(a, b_ref[s], precision=lax.Precision.HIGHEST, preferred_element_type=jnp.float32))
    return jnp.stack(outs, 0)


def _first_kernel(n, count, y_ref, d0_ref, d1_ref, fv_ref, win_ref, dfull_ref, got_y, sy, ry, whole, got_w, sw, rw, got_d, sd, rd):
    p = Place(n, count)
    p.barrier(True, True)
    sends = gather_start(p, y_ref, got_y, sy, ry)
    gather_finish(p, y_ref, got_y, sy, ry, whole)
    fv_ref[...] = _dots(d0_ref, whole)
    sends += bcast_start(p, fv_ref, got_w, sw, rw) + gather_start(p, d1_ref, got_d, sd, rd)
    bcast_finish(p, fv_ref, got_w, sw, rw, win_ref)
    gather_finish(p, d1_ref, got_d, sd, rd, dfull_ref)
    _wait_sends(sends)


def _level1_kernel(
    n, count, share_ref, dw_ref, d_ref, own_ref, win_ref, dfull_ref, x_ref, got_x, sx, rx, got_w, sw, rw, got_d, sd, rd
):
    p = Place(n, count)
    p.barrier(True, True)
    x_ref[...] = _dots(dw_ref, share_ref)
    sends = scatter_start(p, x_ref, got_x, sx, rx)
    own_ref[...] = scatter_finish(p, x_ref, got_x, sx, rx)
    sends += bcast_start(p, own_ref, got_w, sw, rw) + gather_start(p, d_ref, got_d, sd, rd)
    bcast_finish(p, own_ref, got_w, sw, rw, win_ref)
    gather_finish(p, d_ref, got_d, sd, rd, dfull_ref)
    _wait_sends(sends)


def _level2_kernel(n, count, share_ref, dw_ref, own_ref, sol_ref, x_ref, got_x, sx, rx, full, got_y, sy, ry):
    p = Place(n, count)
    p.barrier(True, False)
    x_ref[...] = _dots(dw_ref, share_ref)
    sends = scatter_start(p, x_ref, got_x, sx, rx)
    own_ref[...] = scatter_finish(p, x_ref, got_x, sx, rx)
    sends += gather_start(p, own_ref, got_y, sy, ry)
    gather_finish(p, own_ref, got_y, sy, ry, full)
    sol_ref[...] = _dots(dw_ref, full, transpose_a=True)
    _wait_sends(sends)


def _back2_kernel(n, count, x_ref, f_ref, dw_ref, sum_ref, sol_ref, got_b, sb, rb, res, full, got_y, sy, ry):
    p = Place(n, count)
    p.barrier(True, True)
    sends = spread_start(p, x_ref, got_b, sb, rb)
    acc = spread_finish(p, x_ref, got_b, sb, rb)
    sum_ref[...] = acc
    res[...] = f_ref[...] - acc[acc.shape[0] - 1]
    sends += gather_start(p, res, got_y, sy, ry)
    gather_finish(p, res, got_y, sy, ry, full)
    sol_ref[...] = _dots(dw_ref, full, transpose_a=True)
    _wait_sends(sends)


def _last_kernel(n, count, res_ref, d0_ref, own_ref, x_ref, got, s, r):
    p = Place(n, count)
    p.barrier(True, False)
    x_ref[...] = _dots(d0_ref, res_ref, transpose_a=True)
    sends = scatter_start(p, x_ref, got, s, r)
    own_ref[...] = scatter_finish(p, x_ref, got, s, r)
    _wait_sends(sends)


def _f32(shape):
    return jax.ShapeDtypeStruct(shape, jnp.float32)


def _dma(k):
    return [pltpu.SemaphoreType.DMA((k,)), pltpu.SemaphoreType.DMA((k,))]


def _call(body, n, count, cid, args, outs, scratch):
    return pl.pallas_call(
        functools.partial(body, n, count),
        out_shape=tuple(_f32(o) for o in outs),
        in_specs=[_vmem() for a in args],
        out_specs=tuple(_vmem() for o in outs),
        scratch_shapes=scratch,
        compiler_params=_params(cid),
    )(*args)


def local(rhs, diag_inv, factor_tiles, tile_source, tile_count):
    levels = rhs.shape[0]
    owned_count = rhs.shape[1]
    share_rows = rhs.shape[2]
    columns = rhs.shape[3]
    slot_count = tile_source.shape[2]
    reach_dev = KDEV
    window_len = 2 * reach_dev + 1
    n = lax.axis_size("cols")
    count = lax.axis_size("rows")
    total_sup = count * owned_count
    row_place = lax.axis_index("rows")
    my_rows = lax.axis_index("cols") * share_rows
    highest = lax.Precision.HIGHEST
    slot_ids = jnp.arange(slot_count, dtype=jnp.int32)
    assert levels == 3 and count >= window_len
    blk = (owned_count, share_rows, columns)
    whole = (owned_count, n * share_rows, columns)
    dblk = diag_inv.shape[1:]
    dwhole = (owned_count, n * share_rows, diag_inv.shape[3])
    win = (window_len,) + blk
    slots = window_len

    def window_places(sources):
        src_level = sources // total_sup
        within = sources % total_sup
        return (
            src_level * window_len + within // owned_count - row_place + reach_dev
        ) * owned_count + within % owned_count

    def live_mask(counts):
        return (slot_ids[None, :] < counts[:, None]).astype(jnp.float32)

    def own_rows(block):
        return lax.dynamic_slice_in_dim(block, my_rows, share_rows, axis=1)

    def forward_share(height, windows):
        stacked = jnp.stack(windows, 0).reshape(height * window_len * owned_count, share_rows, columns)
        places = window_places(tile_source[height - 1])
        picked = jnp.take(stacked, places, axis=0) * live_mask(tile_count[height - 1])[:, :, None, None]
        partial_value = jnp.einsum(
            "skci,skcr->sir", factor_tiles[height - 1], picked, precision=highest
        )
        return lax.dynamic_update_slice_in_dim(
            -partial_value, rhs[height] - own_rows(partial_value), my_rows, axis=1
        )

    def buckets(height, whole_block):
        term_set = jnp.einsum(
            "skci,sir->skcr", factor_tiles[height - 1], whole_block, precision=highest
        )
        term_set = term_set * live_mask(tile_count[height - 1])[:, :, None, None]
        places = window_places(tile_source[height - 1]).reshape(-1)
        targets = height * window_len * owned_count
        one_hot = (jnp.arange(targets, dtype=jnp.int32)[:, None] == places[None, :]).astype(
            jnp.float32
        )
        outgoing = jnp.einsum(
            "ms,slg->mlg",
            one_hot,
            term_set.reshape(owned_count * slot_count, share_rows, columns),
            precision=highest,
        )
        push_outgoing = outgoing.reshape(height, window_len, owned_count, share_rows, columns)
        return push_outgoing.transpose(1, 0, 2, 3, 4)

    def vm(shape):
        return pltpu.VMEM(shape, jnp.float32)

    fv0, win0, d1 = _call(
        _first_kernel, n, count, 0, [rhs[0], diag_inv[0], diag_inv[1]], [blk, win, dwhole],
        [vm((n,) + blk)] + _dma(n) + [vm(whole)] + [vm(win)] + _dma(slots) + [vm((n,) + dblk)] + _dma(n),
    )
    fv1, win1, d2 = _call(
        _level1_kernel, n, count, 1, [forward_share(1, [win0]), d1, diag_inv[2]], [blk, win, dwhole],
        [vm(whole), vm((n,) + blk)] + _dma(n) + [vm(win)] + _dma(slots) + [vm((n,) + dblk)] + _dma(n),
    )
    fv2, sol2 = _call(
        _level2_kernel, n, count, 2, [forward_share(2, [win0, win1]), d2], [blk, whole],
        [vm(whole), vm((n,) + blk)] + _dma(n) + [vm(whole), vm((n,) + blk)] + _dma(n),
    )
    out2 = buckets(2, sol2)
    got2, sol1 = _call(
        _back2_kernel, n, count, 3, [out2, fv1, d1], [out2.shape[1:], whole],
        [vm(out2.shape)] + _dma(slots) + [vm(blk), vm(whole), vm((n,) + blk)] + _dma(n),
    )
    out1 = buckets(1, sol1)
    (got1,) = _call(_spread_kernel, n, count, 4, [out1], [out1.shape[1:]], [vm(out1.shape)] + _dma(slots))
    res0 = fv0 - (got2[0] + got1[0])
    (sol0,) = _call(
        _last_kernel, n, count, 5, [res0, diag_inv[0]], [blk], [vm(whole), vm((n,) + blk)] + _dma(n)
    )
    return jnp.stack([sol0, own_rows(sol1), own_rows(sol2)], 0)


def solution(mesh):
    placed = (
        P(None, "rows", "cols", None),
        P(None, "rows", "cols", None),
        P(None, "rows", None, "cols", None),
        P(None, "rows", None),
        P(None, "rows"),
    )
    return jax.shard_map(
        local, mesh=mesh, in_specs=placed, out_specs=P(None, "rows", "cols", None), check_vma=False
    )
```

```python
import functools

import jax
import jax.numpy as jnp
from jax import lax
from jax.experimental import pallas as pl
from jax.experimental.pallas import tpu as pltpu
from jax.sharding import PartitionSpec as P

KDEV = 7
MESH = pl.DeviceIdType.MESH
OFFSETS = [d for d in range(-KDEV, KDEV + 1) if d != 0]


def _params(cid):
    return pltpu.CompilerParams(collective_id=cid, has_side_effects=True)


def _vmem():
    return pl.BlockSpec(memory_space=pltpu.VMEM)


class Place:
    def __init__(self, n, count):
        self.n = n
        self.count = count
        self.col = lax.axis_index("cols")
        self.row = lax.axis_index("rows")

    def col_peer(self, k):
        return lax.rem(self.col + k, self.n)

    def row_peer(self, d):
        return lax.rem(self.row + d + self.count, self.count)

    def barrier(self, cols, rows):
        targets = []
        if cols:
            targets += [(self.row, self.col_peer(k)) for k in range(1, self.n)]
        if rows:
            targets += [(self.row_peer(d), self.col) for d in OFFSETS]
        barrier = pltpu.get_barrier_semaphore()
        for t in targets:
            pl.semaphore_signal(barrier, 1, device_id=t, device_id_type=MESH)
        pl.semaphore_wait(barrier, len(targets))


def _copy(src_ref, dst_ref, send, recv, device):
    return pltpu.make_async_remote_copy(
        src_ref=src_ref,
        dst_ref=dst_ref,
        send_sem=send,
        recv_sem=recv,
        device_id=device,
        device_id_type=MESH,
    )


def _rows_of(ref, index, chunk):
    return ref.at[:, pl.ds(pl.multiple_of(index * chunk, chunk), chunk), :]


def _start_all(copies):
    for c in copies:
        c.start()
    return copies


def _wait_sends(copies):
    for c in copies:
        c.wait_send()


def scatter_start(p, x_ref, got, send, recv):
    chunk = got.shape[2]
    out = []
    for k in range(1, p.n):
        peer = p.col_peer(k)
        out.append(
            _copy(_rows_of(x_ref, peer, chunk), got.at[p.col], send.at[peer], recv.at[p.col], (p.row, peer))
        )
    return _start_all(out)


def scatter_finish(p, x_ref, got, send, recv):
    chunk = got.shape[2]
    acc = _rows_of(x_ref, p.col, chunk)[...]
    for k in range(1, p.n):
        src = p.col_peer(p.n - k)
        _copy(_rows_of(x_ref, src, chunk), got.at[src], send.at[src], recv.at[src], (p.row, src)).wait_recv()
        acc = acc + got[src]
    return acc


def gather_start(p, y_ref, got, send, recv):
    out = []
    for k in range(1, p.n):
        peer = p.col_peer(k)
        out.append(_copy(y_ref, got.at[p.col], send.at[peer], recv.at[p.col], (p.row, peer)))
    return _start_all(out)


def gather_finish(p, y_ref, got, send, recv, full_ref):
    chunk = got.shape[2]
    _rows_of(full_ref, p.col, chunk)[...] = y_ref[...]
    for k in range(1, p.n):
        src = p.col_peer(p.n - k)
        _copy(y_ref, got.at[src], send.at[src], recv.at[src], (p.row, src)).wait_recv()
        _rows_of(full_ref, src, chunk)[...] = got[src]


def bcast_start(p, v_ref, got, send, recv):
    out = []
    for d in OFFSETS:
        out.append(_copy(v_ref, got.at[KDEV - d], send.at[KDEV + d], recv.at[KDEV - d], (p.row_peer(d), p.col)))
    return _start_all(out)


def bcast_finish(p, v_ref, got, send, recv, win_ref):
    win_ref[KDEV] = v_ref[...]
    for o in OFFSETS:
        w = KDEV + o
        _copy(v_ref, got.at[w], send.at[w], recv.at[w], (p.row_peer(o), p.col)).wait_recv()
        win_ref[w] = got[w]


def spread_start(p, x_ref, got, send, recv):
    out = []
    for d in OFFSETS:
        out.append(
            _copy(x_ref.at[KDEV + d], got.at[KDEV - d], send.at[KDEV + d], recv.at[KDEV - d], (p.row_peer(d), p.col))
        )
    return _start_all(out)


def spread_finish(p, x_ref, got, send, recv):
    acc = x_ref[KDEV]
    for o in OFFSETS:
        w = KDEV + o
        _copy(x_ref.at[w], got.at[w], send.at[w], recv.at[w], (p.row_peer(o), p.col)).wait_recv()
        acc = acc + got[w]
    return acc


def _gather_kernel(n, count, y_ref, full_ref, got, s, r):
    p = Place(n, count)
    p.barrier(True, False)
    sends = gather_start(p, y_ref, got, s, r)
    gather_finish(p, y_ref, got, s, r, full_ref)
    _wait_sends(sends)


def _scatter_kernel(n, count, x_ref, own_ref, got, s, r):
    p = Place(n, count)
    p.barrier(True, False)
    sends = scatter_start(p, x_ref, got, s, r)
    own_ref[...] = scatter_finish(p, x_ref, got, s, r)
    _wait_sends(sends)


def _bcast_gather_kernel(n, count, v_ref, d_ref, win_ref, dfull_ref, got_w, sw, rw, got_d, sd, rd):
    p = Place(n, count)
    p.barrier(True, True)
    sends = bcast_start(p, v_ref, got_w, sw, rw) + gather_start(p, d_ref, got_d, sd, rd)
    bcast_finish(p, v_ref, got_w, sw, rw, win_ref)
    gather_finish(p, d_ref, got_d, sd, rd, dfull_ref)
    _wait_sends(sends)


def _scatter_bcast_gather_kernel(
    n, count, x_ref, d_ref, own_ref, win_ref, dfull_ref, got_x, sx, rx, got_w, sw, rw, got_d, sd, rd
):
    p = Place(n, count)
    p.barrier(True, True)
    sends = scatter_start(p, x_ref, got_x, sx, rx)
    own_ref[...] = scatter_finish(p, x_ref, got_x, sx, rx)
    sends += bcast_start(p, own_ref, got_w, sw, rw) + gather_start(p, d_ref, got_d, sd, rd)
    bcast_finish(p, own_ref, got_w, sw, rw, win_ref)
    gather_finish(p, d_ref, got_d, sd, rd, dfull_ref)
    _wait_sends(sends)


def _scatter_gather_kernel(n, count, x_ref, own_ref, full_ref, got_x, sx, rx, got_y, sy, ry):
    p = Place(n, count)
    p.barrier(True, False)
    sends = scatter_start(p, x_ref, got_x, sx, rx)
    own_ref[...] = scatter_finish(p, x_ref, got_x, sx, rx)
    sends += gather_start(p, own_ref, got_y, sy, ry)
    gather_finish(p, own_ref, got_y, sy, ry, full_ref)
    _wait_sends(sends)


def _spread_gather_kernel(n, count, x_ref, f_ref, sum_ref, full_ref, got_b, sb, rb, res, got_y, sy, ry):
    p = Place(n, count)
    p.barrier(True, True)
    sends = spread_start(p, x_ref, got_b, sb, rb)
    acc = spread_finish(p, x_ref, got_b, sb, rb)
    sum_ref[...] = acc
    res[...] = f_ref[...] - acc[acc.shape[0] - 1]
    sends += gather_start(p, res, got_y, sy, ry)
    gather_finish(p, res, got_y, sy, ry, full_ref)
    _wait_sends(sends)


def _spread_kernel(n, count, x_ref, sum_ref, got_b, sb, rb):
    p = Place(n, count)
    p.barrier(False, True)
    sends = spread_start(p, x_ref, got_b, sb, rb)
    sum_ref[...] = spread_finish(p, x_ref, got_b, sb, rb)
    _wait_sends(sends)


def _dots(a_ref, b_ref, transpose_a=False):
    outs = []
    for s in range(a_ref.shape[0]):
        a = a_ref[s]
        if transpose_a:
            a = a.T
        outs.append(jnp.dot(a, b_ref[s], precision=lax.Precision.HIGHEST, preferred_element_type=jnp.float32))
    return jnp.stack(outs, 0)


def _first_kernel(n, count, y_ref, d0_ref, d1_ref, fv_ref, win_ref, dfull_ref, got_y, sy, ry, whole, got_w, sw, rw, got_d, sd, rd):
    p = Place(n, count)
    p.barrier(True, True)
    sends = gather_start(p, y_ref, got_y, sy, ry)
    gather_finish(p, y_ref, got_y, sy, ry, whole)
    fv_ref[...] = _dots(d0_ref, whole)
    sends += bcast_start(p, fv_ref, got_w, sw, rw) + gather_start(p, d1_ref, got_d, sd, rd)
    bcast_finish(p, fv_ref, got_w, sw, rw, win_ref)
    gather_finish(p, d1_ref, got_d, sd, rd, dfull_ref)
    _wait_sends(sends)


def _level1_kernel(
    n, count, share_ref, dw_ref, d_ref, own_ref, win_ref, dfull_ref, x_ref, got_x, sx, rx, got_w, sw, rw, got_d, sd, rd
):
    p = Place(n, count)
    p.barrier(True, True)
    x_ref[...] = _dots(dw_ref, share_ref)
    sends = scatter_start(p, x_ref, got_x, sx, rx)
    own_ref[...] = scatter_finish(p, x_ref, got_x, sx, rx)
    sends += bcast_start(p, own_ref, got_w, sw, rw) + gather_start(p, d_ref, got_d, sd, rd)
    bcast_finish(p, own_ref, got_w, sw, rw, win_ref)
    gather_finish(p, d_ref, got_d, sd, rd, dfull_ref)
    _wait_sends(sends)


def _level2_kernel(n, count, share_ref, dw_ref, own_ref, sol_ref, x_ref, got_x, sx, rx, full, got_y, sy, ry):
    p = Place(n, count)
    p.barrier(True, False)
    x_ref[...] = _dots(dw_ref, share_ref)
    sends = scatter_start(p, x_ref, got_x, sx, rx)
    own_ref[...] = scatter_finish(p, x_ref, got_x, sx, rx)
    sends += gather_start(p, own_ref, got_y, sy, ry)
    gather_finish(p, own_ref, got_y, sy, ry, full)
    sol_ref[...] = _dots(dw_ref, full, transpose_a=True)
    _wait_sends(sends)


def _back2_kernel(n, count, x_ref, f_ref, dw_ref, sum_ref, sol_ref, got_b, sb, rb, res, full, got_y, sy, ry):
    p = Place(n, count)
    p.barrier(True, True)
    sends = spread_start(p, x_ref, got_b, sb, rb)
    acc = spread_finish(p, x_ref, got_b, sb, rb)
    sum_ref[...] = acc
    res[...] = f_ref[...] - acc[acc.shape[0] - 1]
    sends += gather_start(p, res, got_y, sy, ry)
    gather_finish(p, res, got_y, sy, ry, full)
    sol_ref[...] = _dots(dw_ref, full, transpose_a=True)
    _wait_sends(sends)


def _last_kernel(n, count, res_ref, d0_ref, own_ref, x_ref, got, s, r):
    p = Place(n, count)
    p.barrier(True, False)
    x_ref[...] = _dots(d0_ref, res_ref, transpose_a=True)
    sends = scatter_start(p, x_ref, got, s, r)
    own_ref[...] = scatter_finish(p, x_ref, got, s, r)
    _wait_sends(sends)


def _final_kernel(n, count, x_ref, f_ref, d0_ref, own_ref, got_b, sb, rb, x2_ref, got, s, r):
    p = Place(n, count)
    p.barrier(True, True)
    sends = spread_start(p, x_ref, got_b, sb, rb)
    acc = spread_finish(p, x_ref, got_b, sb, rb)
    res = f_ref[...] - acc[0]
    outs = []
    for q in range(d0_ref.shape[0]):
        outs.append(
            jnp.dot(d0_ref[q].T, res[q], precision=lax.Precision.HIGHEST, preferred_element_type=jnp.float32)
        )
    x2_ref[...] = jnp.stack(outs, 0)
    sends += scatter_start(p, x2_ref, got, s, r)
    own_ref[...] = scatter_finish(p, x2_ref, got, s, r)
    _wait_sends(sends)


def _f32(shape):
    return jax.ShapeDtypeStruct(shape, jnp.float32)


def _dma(k):
    return [pltpu.SemaphoreType.DMA((k,)), pltpu.SemaphoreType.DMA((k,))]


def _call(body, n, count, cid, args, outs, scratch):
    return pl.pallas_call(
        functools.partial(body, n, count),
        out_shape=tuple(_f32(o) for o in outs),
        in_specs=[_vmem() for a in args],
        out_specs=tuple(_vmem() for o in outs),
        scratch_shapes=scratch,
        compiler_params=_params(cid),
    )(*args)


def local(rhs, diag_inv, factor_tiles, tile_source, tile_count):
    levels = rhs.shape[0]
    owned_count = rhs.shape[1]
    share_rows = rhs.shape[2]
    columns = rhs.shape[3]
    slot_count = tile_source.shape[2]
    reach_dev = KDEV
    window_len = 2 * reach_dev + 1
    n = lax.axis_size("cols")
    count = lax.axis_size("rows")
    total_sup = count * owned_count
    row_place = lax.axis_index("rows")
    my_rows = lax.axis_index("cols") * share_rows
    highest = lax.Precision.HIGHEST
    slot_ids = jnp.arange(slot_count, dtype=jnp.int32)
    assert levels == 3 and count >= window_len
    blk = (owned_count, share_rows, columns)
    whole = (owned_count, n * share_rows, columns)
    dblk = diag_inv.shape[1:]
    dwhole = (owned_count, n * share_rows, diag_inv.shape[3])
    win = (window_len,) + blk
    slots = window_len

    def window_places(sources):
        src_level = sources // total_sup
        within = sources % total_sup
        return (
            src_level * window_len + within // owned_count - row_place + reach_dev
        ) * owned_count + within % owned_count

    def live_mask(counts):
        return (slot_ids[None, :] < counts[:, None]).astype(jnp.float32)

    def own_rows(block):
        return lax.dynamic_slice_in_dim(block, my_rows, share_rows, axis=1)

    def forward_share(height, windows):
        stacked = jnp.stack(windows, 0).reshape(height * window_len * owned_count, share_rows, columns)
        places = window_places(tile_source[height - 1])
        picked = jnp.take(stacked, places, axis=0) * live_mask(tile_count[height - 1])[:, :, None, None]
        partial_value = jnp.einsum(
            "skci,skcr->sir", factor_tiles[height - 1], picked, precision=highest
        )
        return lax.dynamic_update_slice_in_dim(
            -partial_value, rhs[height] - own_rows(partial_value), my_rows, axis=1
        )

    def buckets(height, whole_block):
        term_set = jnp.einsum(
            "skci,sir->skcr", factor_tiles[height - 1], whole_block, precision=highest
        )
        term_set = term_set * live_mask(tile_count[height - 1])[:, :, None, None]
        places = window_places(tile_source[height - 1]).reshape(-1)
        targets = height * window_len * owned_count
        one_hot = (jnp.arange(targets, dtype=jnp.int32)[:, None] == places[None, :]).astype(
            jnp.float32
        )
        outgoing = jnp.einsum(
            "ms,slg->mlg",
            one_hot,
            term_set.reshape(owned_count * slot_count, share_rows, columns),
            precision=highest,
        )
        push_outgoing = outgoing.reshape(height, window_len, owned_count, share_rows, columns)
        return push_outgoing.transpose(1, 0, 2, 3, 4)

    def vm(shape):
        return pltpu.VMEM(shape, jnp.float32)

    fv0, win0, d1 = _call(
        _first_kernel, n, count, 0, [rhs[0], diag_inv[0], diag_inv[1]], [blk, win, dwhole],
        [vm((n,) + blk)] + _dma(n) + [vm(whole)] + [vm(win)] + _dma(slots) + [vm((n,) + dblk)] + _dma(n),
    )
    fv1, win1, d2 = _call(
        _level1_kernel, n, count, 1, [forward_share(1, [win0]), d1, diag_inv[2]], [blk, win, dwhole],
        [vm(whole), vm((n,) + blk)] + _dma(n) + [vm(win)] + _dma(slots) + [vm((n,) + dblk)] + _dma(n),
    )
    fv2, sol2 = _call(
        _level2_kernel, n, count, 2, [forward_share(2, [win0, win1]), d2], [blk, whole],
        [vm(whole), vm((n,) + blk)] + _dma(n) + [vm(whole), vm((n,) + blk)] + _dma(n),
    )
    out2 = buckets(2, sol2)
    got2, sol1 = _call(
        _back2_kernel, n, count, 3, [out2[:, 1:], fv1, d1], [out2[:, 1:].shape[1:], whole],
        [vm(out2[:, 1:].shape)] + _dma(slots) + [vm(blk), vm(whole), vm((n,) + blk)] + _dma(n),
    )
    out1 = buckets(1, sol1) + out2[:, :1]
    (sol0,) = _call(
        _final_kernel, n, count, 4, [out1, fv0, diag_inv[0]], [blk],
        [vm(out1.shape)] + _dma(slots) + [vm(whole), vm((n,) + blk)] + _dma(n),
    )
    return jnp.stack([sol0, own_rows(sol1), own_rows(sol2)], 0)


def solution(mesh):
    placed = (
        P(None, "rows", "cols", None),
        P(None, "rows", "cols", None),
        P(None, "rows", None, "cols", None),
        P(None, "rows", None),
        P(None, "rows"),
    )
    return jax.shard_map(
        local, mesh=mesh, in_specs=placed, out_specs=P(None, "rows", "cols", None), check_vma=False
    )
```

```python
import functools

import jax
import jax.numpy as jnp
from jax import lax
from jax.experimental import pallas as pl
from jax.experimental.pallas import tpu as pltpu
from jax.sharding import PartitionSpec as P

KDEV = 7
MESH = pl.DeviceIdType.MESH
OFFSETS = [d for d in range(-KDEV, KDEV + 1) if d != 0]


def _params(cid):
    return pltpu.CompilerParams(collective_id=cid, has_side_effects=True)


def _vmem():
    return pl.BlockSpec(memory_space=pltpu.VMEM)


class Place:
    def __init__(self, n, count):
        self.n = n
        self.count = count
        self.col = lax.axis_index("cols")
        self.row = lax.axis_index("rows")

    def col_peer(self, k):
        return lax.rem(self.col + k, self.n)

    def row_peer(self, d):
        return lax.rem(self.row + d + self.count, self.count)

    def barrier(self, cols, rows):
        targets = []
        if cols:
            targets += [(self.row, self.col_peer(k)) for k in range(1, self.n)]
        if rows:
            targets += [(self.row_peer(d), self.col) for d in OFFSETS]
        barrier = pltpu.get_barrier_semaphore()
        for t in targets:
            pl.semaphore_signal(barrier, 1, device_id=t, device_id_type=MESH)
        pl.semaphore_wait(barrier, len(targets))


def _copy(src_ref, dst_ref, send, recv, device):
    return pltpu.make_async_remote_copy(
        src_ref=src_ref,
        dst_ref=dst_ref,
        send_sem=send,
        recv_sem=recv,
        device_id=device,
        device_id_type=MESH,
    )


def _rows_of(ref, index, chunk):
    return ref.at[:, pl.ds(pl.multiple_of(index * chunk, chunk), chunk), :]


def _start_all(copies):
    for c in copies:
        c.start()
    return copies


def _wait_sends(copies):
    for c in copies:
        c.wait_send()


def scatter_start(p, x_ref, got, send, recv):
    chunk = got.shape[2]
    out = []
    for k in range(1, p.n):
        peer = p.col_peer(k)
        out.append(
            _copy(_rows_of(x_ref, peer, chunk), got.at[p.col], send.at[peer], recv.at[p.col], (p.row, peer))
        )
    return _start_all(out)


def scatter_finish(p, x_ref, got, send, recv):
    chunk = got.shape[2]
    acc = _rows_of(x_ref, p.col, chunk)[...]
    for k in range(1, p.n):
        src = p.col_peer(p.n - k)
        _copy(_rows_of(x_ref, src, chunk), got.at[src], send.at[src], recv.at[src], (p.row, src)).wait_recv()
        acc = acc + got[src]
    return acc


def gather_start(p, y_ref, got, send, recv):
    out = []
    for k in range(1, p.n):
        peer = p.col_peer(k)
        out.append(_copy(y_ref, got.at[p.col], send.at[peer], recv.at[p.col], (p.row, peer)))
    return _start_all(out)


def gather_finish(p, y_ref, got, send, recv, full_ref):
    chunk = got.shape[2]
    _rows_of(full_ref, p.col, chunk)[...] = y_ref[...]
    for k in range(1, p.n):
        src = p.col_peer(p.n - k)
        _copy(y_ref, got.at[src], send.at[src], recv.at[src], (p.row, src)).wait_recv()
        _rows_of(full_ref, src, chunk)[...] = got[src]


def bcast_start(p, v_ref, got, send, recv):
    out = []
    for d in OFFSETS:
        out.append(_copy(v_ref, got.at[KDEV - d], send.at[KDEV + d], recv.at[KDEV - d], (p.row_peer(d), p.col)))
    return _start_all(out)


def bcast_finish(p, v_ref, got, send, recv, win_ref):
    win_ref[KDEV] = v_ref[...]
    for o in OFFSETS:
        w = KDEV + o
        _copy(v_ref, got.at[w], send.at[w], recv.at[w], (p.row_peer(o), p.col)).wait_recv()
        win_ref[w] = got[w]


def spread_start(p, x_ref, got, send, recv):
    out = []
    for d in OFFSETS:
        out.append(
            _copy(x_ref.at[KDEV + d], got.at[KDEV - d], send.at[KDEV + d], recv.at[KDEV - d], (p.row_peer(d), p.col))
        )
    return _start_all(out)


def spread_finish(p, x_ref, got, send, recv):
    acc = x_ref[KDEV]
    for o in OFFSETS:
        w = KDEV + o
        _copy(x_ref.at[w], got.at[w], send.at[w], recv.at[w], (p.row_peer(o), p.col)).wait_recv()
        acc = acc + got[w]
    return acc


def _gather_kernel(n, count, y_ref, full_ref, got, s, r):
    p = Place(n, count)
    p.barrier(True, False)
    sends = gather_start(p, y_ref, got, s, r)
    gather_finish(p, y_ref, got, s, r, full_ref)
    _wait_sends(sends)


def _scatter_kernel(n, count, x_ref, own_ref, got, s, r):
    p = Place(n, count)
    p.barrier(True, False)
    sends = scatter_start(p, x_ref, got, s, r)
    own_ref[...] = scatter_finish(p, x_ref, got, s, r)
    _wait_sends(sends)


def _bcast_gather_kernel(n, count, v_ref, d_ref, win_ref, dfull_ref, got_w, sw, rw, got_d, sd, rd):
    p = Place(n, count)
    p.barrier(True, True)
    sends = bcast_start(p, v_ref, got_w, sw, rw) + gather_start(p, d_ref, got_d, sd, rd)
    bcast_finish(p, v_ref, got_w, sw, rw, win_ref)
    gather_finish(p, d_ref, got_d, sd, rd, dfull_ref)
    _wait_sends(sends)


def _scatter_bcast_gather_kernel(
    n, count, x_ref, d_ref, own_ref, win_ref, dfull_ref, got_x, sx, rx, got_w, sw, rw, got_d, sd, rd
):
    p = Place(n, count)
    p.barrier(True, True)
    sends = scatter_start(p, x_ref, got_x, sx, rx)
    own_ref[...] = scatter_finish(p, x_ref, got_x, sx, rx)
    sends += bcast_start(p, own_ref, got_w, sw, rw) + gather_start(p, d_ref, got_d, sd, rd)
    bcast_finish(p, own_ref, got_w, sw, rw, win_ref)
    gather_finish(p, d_ref, got_d, sd, rd, dfull_ref)
    _wait_sends(sends)


def _scatter_gather_kernel(n, count, x_ref, own_ref, full_ref, got_x, sx, rx, got_y, sy, ry):
    p = Place(n, count)
    p.barrier(True, False)
    sends = scatter_start(p, x_ref, got_x, sx, rx)
    own_ref[...] = scatter_finish(p, x_ref, got_x, sx, rx)
    sends += gather_start(p, own_ref, got_y, sy, ry)
    gather_finish(p, own_ref, got_y, sy, ry, full_ref)
    _wait_sends(sends)


def _spread_gather_kernel(n, count, x_ref, f_ref, sum_ref, full_ref, got_b, sb, rb, res, got_y, sy, ry):
    p = Place(n, count)
    p.barrier(True, True)
    sends = spread_start(p, x_ref, got_b, sb, rb)
    acc = spread_finish(p, x_ref, got_b, sb, rb)
    sum_ref[...] = acc
    res[...] = f_ref[...] - acc[acc.shape[0] - 1]
    sends += gather_start(p, res, got_y, sy, ry)
    gather_finish(p, res, got_y, sy, ry, full_ref)
    _wait_sends(sends)


def _spread_kernel(n, count, x_ref, sum_ref, got_b, sb, rb):
    p = Place(n, count)
    p.barrier(False, True)
    sends = spread_start(p, x_ref, got_b, sb, rb)
    sum_ref[...] = spread_finish(p, x_ref, got_b, sb, rb)
    _wait_sends(sends)


def _dots(a_ref, b_ref, transpose_a=False):
    outs = []
    for s in range(a_ref.shape[0]):
        a = a_ref[s]
        if transpose_a:
            a = a.T
        outs.append(jnp.dot(a, b_ref[s], precision=lax.Precision.HIGHEST, preferred_element_type=jnp.float32))
    return jnp.stack(outs, 0)


def _first_kernel(n, count, y_ref, d0_ref, d1_ref, fv_ref, win_ref, dfull_ref, got_y, sy, ry, whole, got_w, sw, rw, got_d, sd, rd):
    p = Place(n, count)
    p.barrier(True, True)
    sends = gather_start(p, y_ref, got_y, sy, ry)
    gather_finish(p, y_ref, got_y, sy, ry, whole)
    fv_ref[...] = _dots(d0_ref, whole)
    sends += bcast_start(p, fv_ref, got_w, sw, rw) + gather_start(p, d1_ref, got_d, sd, rd)
    bcast_finish(p, fv_ref, got_w, sw, rw, win_ref)
    gather_finish(p, d1_ref, got_d, sd, rd, dfull_ref)
    _wait_sends(sends)


def _level1_kernel(
    n, count, share_ref, dw_ref, d_ref, own_ref, win_ref, dfull_ref, x_ref, got_x, sx, rx, got_w, sw, rw, got_d, sd, rd
):
    p = Place(n, count)
    p.barrier(True, True)
    x_ref[...] = _dots(dw_ref, share_ref)
    sends = scatter_start(p, x_ref, got_x, sx, rx)
    own_ref[...] = scatter_finish(p, x_ref, got_x, sx, rx)
    sends += bcast_start(p, own_ref, got_w, sw, rw) + gather_start(p, d_ref, got_d, sd, rd)
    bcast_finish(p, own_ref, got_w, sw, rw, win_ref)
    gather_finish(p, d_ref, got_d, sd, rd, dfull_ref)
    _wait_sends(sends)


def _level2_kernel(n, count, share_ref, dw_ref, own_ref, sol_ref, x_ref, got_x, sx, rx, full, got_y, sy, ry):
    p = Place(n, count)
    p.barrier(True, False)
    x_ref[...] = _dots(dw_ref, share_ref)
    sends = scatter_start(p, x_ref, got_x, sx, rx)
    own_ref[...] = scatter_finish(p, x_ref, got_x, sx, rx)
    sends += gather_start(p, own_ref, got_y, sy, ry)
    gather_finish(p, own_ref, got_y, sy, ry, full)
    sol_ref[...] = _dots(dw_ref, full, transpose_a=True)
    _wait_sends(sends)


def _back2_kernel(n, count, x_ref, f_ref, dw_ref, sum_ref, sol_ref, got_b, sb, rb, res, full, got_y, sy, ry):
    p = Place(n, count)
    p.barrier(True, True)
    sends = spread_start(p, x_ref, got_b, sb, rb)
    acc = spread_finish(p, x_ref, got_b, sb, rb)
    sum_ref[...] = acc
    res[...] = f_ref[...] - acc[acc.shape[0] - 1]
    sends += gather_start(p, res, got_y, sy, ry)
    gather_finish(p, res, got_y, sy, ry, full)
    sol_ref[...] = _dots(dw_ref, full, transpose_a=True)
    _wait_sends(sends)


def _last_kernel(n, count, res_ref, d0_ref, own_ref, x_ref, got, s, r):
    p = Place(n, count)
    p.barrier(True, False)
    x_ref[...] = _dots(d0_ref, res_ref, transpose_a=True)
    sends = scatter_start(p, x_ref, got, s, r)
    own_ref[...] = scatter_finish(p, x_ref, got, s, r)
    _wait_sends(sends)


def _final_kernel(n, count, x_ref, f_ref, d0_ref, own_ref, got_b, sb, rb, x2_ref, got, s, r):
    p = Place(n, count)
    p.barrier(True, True)
    sends = spread_start(p, x_ref, got_b, sb, rb)
    acc = spread_finish(p, x_ref, got_b, sb, rb)
    res = f_ref[...] - acc[0]
    outs = []
    for q in range(d0_ref.shape[0]):
        outs.append(
            jnp.dot(d0_ref[q].T, res[q], precision=lax.Precision.HIGHEST, preferred_element_type=jnp.float32)
        )
    x2_ref[...] = jnp.stack(outs, 0)
    sends += scatter_start(p, x2_ref, got, s, r)
    own_ref[...] = scatter_finish(p, x2_ref, got, s, r)
    _wait_sends(sends)


def _mm(a, b):
    return jnp.dot(a, b, precision=lax.Precision.HIGHEST, preferred_element_type=jnp.float32)


def _fill_buckets(bucket_ref, rows, level):
    slots, owned, share, r = bucket_ref.shape
    span = owned * share
    for w in range(slots):
        start = (level * slots + w) * span
        for q in range(owned):
            bucket_ref[w, q] = rows[start + q * share : start + (q + 1) * share]


def _products(t_ref, sol_ref, w_ref):
    owned, span, unused = t_ref.shape
    total = None
    for q in range(owned):
        terms = _mm(t_ref[q], sol_ref[q])
        part = _mm(w_ref[:, q * span : (q + 1) * span], terms)
        total = part if total is None else total + part
    return total


def _tail_kernel(
    n, count,
    share_ref, d2_ref, d1_ref, d0_ref, f1_ref, f0_ref, t2_ref, t1_ref, w2_ref, w1_ref,
    s0_ref, s1_ref, s2_ref,
    x2, got_x2, sx2, rx2, res2, got_y2, sy2, ry2, full2, sol2,
    bucket1, got_b1, sb1, rb1, res1, got_y1, sy1, ry1, full1, sol1,
    bucket0, got_b0, sb0, rb0, x0, got_x0, sx0, rx0,
):
    p = Place(n, count)
    p.barrier(True, True)
    share = s0_ref.shape[1]
    x2[...] = _dots(d2_ref, share_ref)
    sends = scatter_start(p, x2, got_x2, sx2, rx2)
    res2[...] = scatter_finish(p, x2, got_x2, sx2, rx2)
    sends += gather_start(p, res2, got_y2, sy2, ry2)
    gather_finish(p, res2, got_y2, sy2, ry2, full2)
    sol2[...] = _dots(d2_ref, full2, transpose_a=True)
    s2_ref[...] = _rows_of(sol2, p.col, share)[...]
    routed2 = _products(t2_ref, sol2, w2_ref)
    _fill_buckets(bucket1, routed2, 1)
    sends += spread_start(p, bucket1, got_b1, sb1, rb1)
    res1[...] = f1_ref[...] - spread_finish(p, bucket1, got_b1, sb1, rb1)
    sends += gather_start(p, res1, got_y1, sy1, ry1)
    gather_finish(p, res1, got_y1, sy1, ry1, full1)
    sol1[...] = _dots(d1_ref, full1, transpose_a=True)
    s1_ref[...] = _rows_of(sol1, p.col, share)[...]
    routed1 = _products(t1_ref, sol1, w1_ref)
    _fill_buckets(bucket0, routed1 + routed2[: routed1.shape[0]], 0)
    sends += spread_start(p, bucket0, got_b0, sb0, rb0)
    res0 = f0_ref[...] - spread_finish(p, bucket0, got_b0, sb0, rb0)
    x0[...] = jnp.stack([_mm(d0_ref[q].T, res0[q]) for q in range(res0.shape[0])], 0)
    sends += scatter_start(p, x0, got_x0, sx0, rx0)
    s0_ref[...] = scatter_finish(p, x0, got_x0, sx0, rx0)
    _wait_sends(sends)


def _f32(shape):
    return jax.ShapeDtypeStruct(shape, jnp.float32)


def _dma(k):
    return [pltpu.SemaphoreType.DMA((k,)), pltpu.SemaphoreType.DMA((k,))]


def _call(body, n, count, cid, args, outs, scratch):
    return pl.pallas_call(
        functools.partial(body, n, count),
        out_shape=tuple(_f32(o) for o in outs),
        in_specs=[_vmem() for a in args],
        out_specs=tuple(_vmem() for o in outs),
        scratch_shapes=scratch,
        compiler_params=_params(cid),
    )(*args)


def local(rhs, diag_inv, factor_tiles, tile_source, tile_count):
    levels = rhs.shape[0]
    owned_count = rhs.shape[1]
    share_rows = rhs.shape[2]
    columns = rhs.shape[3]
    slot_count = tile_source.shape[2]
    reach_dev = KDEV
    window_len = 2 * reach_dev + 1
    n = lax.axis_size("cols")
    count = lax.axis_size("rows")
    total_sup = count * owned_count
    row_place = lax.axis_index("rows")
    my_rows = lax.axis_index("cols") * share_rows
    highest = lax.Precision.HIGHEST
    slot_ids = jnp.arange(slot_count, dtype=jnp.int32)
    assert levels == 3 and count >= window_len
    blk = (owned_count, share_rows, columns)
    whole = (owned_count, n * share_rows, columns)
    dblk = diag_inv.shape[1:]
    dwhole = (owned_count, n * share_rows, diag_inv.shape[3])
    win = (window_len,) + blk
    slots = window_len

    def window_places(sources):
        src_level = sources // total_sup
        within = sources % total_sup
        return (
            src_level * window_len + within // owned_count - row_place + reach_dev
        ) * owned_count + within % owned_count

    def live_mask(counts):
        return (slot_ids[None, :] < counts[:, None]).astype(jnp.float32)

    def own_rows(block):
        return lax.dynamic_slice_in_dim(block, my_rows, share_rows, axis=1)

    def forward_share(height, windows):
        stacked = jnp.stack(windows, 0).reshape(height * window_len * owned_count, share_rows, columns)
        places = window_places(tile_source[height - 1])
        picked = jnp.take(stacked, places, axis=0) * live_mask(tile_count[height - 1])[:, :, None, None]
        partial_value = jnp.einsum(
            "skci,skcr->sir", factor_tiles[height - 1], picked, precision=highest
        )
        return lax.dynamic_update_slice_in_dim(
            -partial_value, rhs[height] - own_rows(partial_value), my_rows, axis=1
        )

    def buckets(height, whole_block):
        term_set = jnp.einsum(
            "skci,sir->skcr", factor_tiles[height - 1], whole_block, precision=highest
        )
        term_set = term_set * live_mask(tile_count[height - 1])[:, :, None, None]
        places = window_places(tile_source[height - 1]).reshape(-1)
        targets = height * window_len * owned_count
        one_hot = (jnp.arange(targets, dtype=jnp.int32)[:, None] == places[None, :]).astype(
            jnp.float32
        )
        outgoing = jnp.einsum(
            "ms,slg->mlg",
            one_hot,
            term_set.reshape(owned_count * slot_count, share_rows, columns),
            precision=highest,
        )
        push_outgoing = outgoing.reshape(height, window_len, owned_count, share_rows, columns)
        return push_outgoing.transpose(1, 0, 2, 3, 4)

    def vm(shape):
        return pltpu.VMEM(shape, jnp.float32)

    fv0, win0, d1 = _call(
        _first_kernel, n, count, 0, [rhs[0], diag_inv[0], diag_inv[1]], [blk, win, dwhole],
        [vm((n,) + blk)] + _dma(n) + [vm(whole)] + [vm(win)] + _dma(slots) + [vm((n,) + dblk)] + _dma(n),
    )
    fv1, win1, d2 = _call(
        _level1_kernel, n, count, 1, [forward_share(1, [win0]), d1, diag_inv[2]], [blk, win, dwhole],
        [vm(whole), vm((n,) + blk)] + _dma(n) + [vm(win)] + _dma(slots) + [vm((n,) + dblk)] + _dma(n),
    )
    def selection(height):
        places = window_places(tile_source[height - 1]).reshape(-1)
        live = live_mask(tile_count[height - 1]).reshape(-1)
        targets = height * window_len * owned_count
        pick = (jnp.arange(targets, dtype=jnp.int32)[:, None] == places[None, :]).astype(jnp.float32)
        pick = pick * live[None, :]
        eye = jnp.eye(share_rows, dtype=jnp.float32)
        return (pick[:, None, :, None] * eye[None, :, None, :]).reshape(
            targets * share_rows, places.shape[0] * share_rows
        )

    def flat_tiles(height):
        t = factor_tiles[height - 1]
        return t.reshape(t.shape[0], t.shape[1] * t.shape[2], t.shape[3])

    nblk = (n,) + blk
    sol0, sol1, sol2 = _call(
        _tail_kernel, n, count, 2,
        [forward_share(2, [win0, win1]), d2, d1, diag_inv[0], fv1, fv0, flat_tiles(2), flat_tiles(1),
         selection(2), selection(1)],
        [blk, blk, blk],
        [vm(whole), vm(nblk)] + _dma(n) + [vm(blk), vm(nblk)] + _dma(n) + [vm(whole), vm(whole)]
        + [vm(win), vm(win)] + _dma(slots) + [vm(blk), vm(nblk)] + _dma(n) + [vm(whole), vm(whole)]
        + [vm(win), vm(win)] + _dma(slots) + [vm(whole), vm(nblk)] + _dma(n),
    )
    return jnp.stack([sol0, sol1, sol2], 0)


def solution(mesh):
    placed = (
        P(None, "rows", "cols", None),
        P(None, "rows", "cols", None),
        P(None, "rows", None, "cols", None),
        P(None, "rows", None),
        P(None, "rows"),
    )
    return jax.shard_map(
        local, mesh=mesh, in_specs=placed, out_specs=P(None, "rows", "cols", None), check_vma=False
    )
```

```python
import functools

import jax
import jax.numpy as jnp
from jax import lax
from jax.experimental import pallas as pl
from jax.experimental.pallas import tpu as pltpu
from jax.sharding import PartitionSpec as P

KDEV = 7
MESH = pl.DeviceIdType.MESH
OFFSETS = [d for d in range(-KDEV, KDEV + 1) if d != 0]


def _params(cid):
    return pltpu.CompilerParams(collective_id=cid, has_side_effects=True)


def _vmem():
    return pl.BlockSpec(memory_space=pltpu.VMEM)


class Place:
    def __init__(self, n, count):
        self.n = n
        self.count = count
        self.col = lax.axis_index("cols")
        self.row = lax.axis_index("rows")

    def col_peer(self, k):
        return lax.rem(self.col + k, self.n)

    def row_peer(self, d):
        return lax.rem(self.row + d + self.count, self.count)

    def barrier(self, cols, rows):
        targets = []
        if cols:
            targets += [(self.row, self.col_peer(k)) for k in range(1, self.n)]
        if rows:
            targets += [(self.row_peer(d), self.col) for d in OFFSETS]
        barrier = pltpu.get_barrier_semaphore()
        for t in targets:
            pl.semaphore_signal(barrier, 1, device_id=t, device_id_type=MESH)
        pl.semaphore_wait(barrier, len(targets))


def _copy(src_ref, dst_ref, send, recv, device):
    return pltpu.make_async_remote_copy(
        src_ref=src_ref,
        dst_ref=dst_ref,
        send_sem=send,
        recv_sem=recv,
        device_id=device,
        device_id_type=MESH,
    )


def _rows_of(ref, index, chunk):
    return ref.at[:, pl.ds(pl.multiple_of(index * chunk, chunk), chunk), :]


def _start_all(copies):
    for c in copies:
        c.start()
    return copies


def _wait_sends(copies):
    for c in copies:
        c.wait_send()


def scatter_start(p, x_ref, got, send, recv):
    chunk = got.shape[2]
    out = []
    for k in range(1, p.n):
        peer = p.col_peer(k)
        out.append(
            _copy(_rows_of(x_ref, peer, chunk), got.at[p.col], send.at[peer], recv.at[p.col], (p.row, peer))
        )
    return _start_all(out)


def scatter_finish(p, x_ref, got, send, recv):
    chunk = got.shape[2]
    acc = _rows_of(x_ref, p.col, chunk)[...]
    for k in range(1, p.n):
        src = p.col_peer(p.n - k)
        _copy(_rows_of(x_ref, src, chunk), got.at[src], send.at[src], recv.at[src], (p.row, src)).wait_recv()
        acc = acc + got[src]
    return acc


def gather_start(p, y_ref, got, send, recv):
    out = []
    for k in range(1, p.n):
        peer = p.col_peer(k)
        out.append(_copy(y_ref, got.at[p.col], send.at[peer], recv.at[p.col], (p.row, peer)))
    return _start_all(out)


def gather_finish(p, y_ref, got, send, recv, full_ref):
    chunk = got.shape[2]
    _rows_of(full_ref, p.col, chunk)[...] = y_ref[...]
    for k in range(1, p.n):
        src = p.col_peer(p.n - k)
        _copy(y_ref, got.at[src], send.at[src], recv.at[src], (p.row, src)).wait_recv()
        _rows_of(full_ref, src, chunk)[...] = got[src]


def bcast_start(p, v_ref, got, send, recv):
    out = []
    for d in OFFSETS:
        out.append(_copy(v_ref, got.at[KDEV - d], send.at[KDEV + d], recv.at[KDEV - d], (p.row_peer(d), p.col)))
    return _start_all(out)


def bcast_finish(p, v_ref, got, send, recv, win_ref):
    win_ref[KDEV] = v_ref[...]
    for o in OFFSETS:
        w = KDEV + o
        _copy(v_ref, got.at[w], send.at[w], recv.at[w], (p.row_peer(o), p.col)).wait_recv()
        win_ref[w] = got[w]


def spread_start(p, x_ref, got, send, recv):
    out = []
    for d in OFFSETS:
        out.append(
            _copy(x_ref.at[KDEV + d], got.at[KDEV - d], send.at[KDEV + d], recv.at[KDEV - d], (p.row_peer(d), p.col))
        )
    return _start_all(out)


def spread_finish(p, x_ref, got, send, recv):
    acc = x_ref[KDEV]
    for o in OFFSETS:
        w = KDEV + o
        _copy(x_ref.at[w], got.at[w], send.at[w], recv.at[w], (p.row_peer(o), p.col)).wait_recv()
        acc = acc + got[w]
    return acc


def _gather_kernel(n, count, y_ref, full_ref, got, s, r):
    p = Place(n, count)
    p.barrier(True, False)
    sends = gather_start(p, y_ref, got, s, r)
    gather_finish(p, y_ref, got, s, r, full_ref)
    _wait_sends(sends)


def _scatter_kernel(n, count, x_ref, own_ref, got, s, r):
    p = Place(n, count)
    p.barrier(True, False)
    sends = scatter_start(p, x_ref, got, s, r)
    own_ref[...] = scatter_finish(p, x_ref, got, s, r)
    _wait_sends(sends)


def _bcast_gather_kernel(n, count, v_ref, d_ref, win_ref, dfull_ref, got_w, sw, rw, got_d, sd, rd):
    p = Place(n, count)
    p.barrier(True, True)
    sends = bcast_start(p, v_ref, got_w, sw, rw) + gather_start(p, d_ref, got_d, sd, rd)
    bcast_finish(p, v_ref, got_w, sw, rw, win_ref)
    gather_finish(p, d_ref, got_d, sd, rd, dfull_ref)
    _wait_sends(sends)


def _scatter_bcast_gather_kernel(
    n, count, x_ref, d_ref, own_ref, win_ref, dfull_ref, got_x, sx, rx, got_w, sw, rw, got_d, sd, rd
):
    p = Place(n, count)
    p.barrier(True, True)
    sends = scatter_start(p, x_ref, got_x, sx, rx)
    own_ref[...] = scatter_finish(p, x_ref, got_x, sx, rx)
    sends += bcast_start(p, own_ref, got_w, sw, rw) + gather_start(p, d_ref, got_d, sd, rd)
    bcast_finish(p, own_ref, got_w, sw, rw, win_ref)
    gather_finish(p, d_ref, got_d, sd, rd, dfull_ref)
    _wait_sends(sends)


def _scatter_gather_kernel(n, count, x_ref, own_ref, full_ref, got_x, sx, rx, got_y, sy, ry):
    p = Place(n, count)
    p.barrier(True, False)
    sends = scatter_start(p, x_ref, got_x, sx, rx)
    own_ref[...] = scatter_finish(p, x_ref, got_x, sx, rx)
    sends += gather_start(p, own_ref, got_y, sy, ry)
    gather_finish(p, own_ref, got_y, sy, ry, full_ref)
    _wait_sends(sends)


def _spread_gather_kernel(n, count, x_ref, f_ref, sum_ref, full_ref, got_b, sb, rb, res, got_y, sy, ry):
    p = Place(n, count)
    p.barrier(True, True)
    sends = spread_start(p, x_ref, got_b, sb, rb)
    acc = spread_finish(p, x_ref, got_b, sb, rb)
    sum_ref[...] = acc
    res[...] = f_ref[...] - acc[acc.shape[0] - 1]
    sends += gather_start(p, res, got_y, sy, ry)
    gather_finish(p, res, got_y, sy, ry, full_ref)
    _wait_sends(sends)


def _spread_kernel(n, count, x_ref, sum_ref, got_b, sb, rb):
    p = Place(n, count)
    p.barrier(False, True)
    sends = spread_start(p, x_ref, got_b, sb, rb)
    sum_ref[...] = spread_finish(p, x_ref, got_b, sb, rb)
    _wait_sends(sends)


def _dots(a_ref, b_ref, transpose_a=False):
    outs = []
    for s in range(a_ref.shape[0]):
        a = a_ref[s]
        if transpose_a:
            a = a.T
        outs.append(jnp.dot(a, b_ref[s], precision=lax.Precision.HIGHEST, preferred_element_type=jnp.float32))
    return jnp.stack(outs, 0)


def _first_kernel(n, count, rhs_ref, dinv_ref, fv_ref, win_ref, dfull_ref, got_y, sy, ry, whole, got_w, sw, rw, got_d, sd, rd):
    y_ref, d0_ref, d1_ref = rhs_ref.at[0], dinv_ref.at[0], dinv_ref.at[1]
    p = Place(n, count)
    p.barrier(True, True)
    sends = gather_start(p, y_ref, got_y, sy, ry)
    gather_finish(p, y_ref, got_y, sy, ry, whole)
    fv_ref[...] = _dots(d0_ref, whole)
    sends += bcast_start(p, fv_ref, got_w, sw, rw) + gather_start(p, d1_ref, got_d, sd, rd)
    bcast_finish(p, fv_ref, got_w, sw, rw, win_ref)
    gather_finish(p, d1_ref, got_d, sd, rd, dfull_ref)
    _wait_sends(sends)


def _level1_kernel(
    n, count, share_ref, dw_ref, dinv_ref, own_ref, win_ref, dfull_ref, x_ref, got_x, sx, rx, got_w, sw, rw, got_d, sd, rd
):
    d_ref = dinv_ref.at[2]
    p = Place(n, count)
    p.barrier(True, True)
    x_ref[...] = _dots(dw_ref, share_ref)
    sends = scatter_start(p, x_ref, got_x, sx, rx)
    own_ref[...] = scatter_finish(p, x_ref, got_x, sx, rx)
    sends += bcast_start(p, own_ref, got_w, sw, rw) + gather_start(p, d_ref, got_d, sd, rd)
    bcast_finish(p, own_ref, got_w, sw, rw, win_ref)
    gather_finish(p, d_ref, got_d, sd, rd, dfull_ref)
    _wait_sends(sends)


def _level2_kernel(n, count, share_ref, dw_ref, own_ref, sol_ref, mine_ref, x_ref, got_x, sx, rx, full, got_y, sy, ry):
    p = Place(n, count)
    p.barrier(True, False)
    x_ref[...] = _dots(dw_ref, share_ref)
    sends = scatter_start(p, x_ref, got_x, sx, rx)
    own_ref[...] = scatter_finish(p, x_ref, got_x, sx, rx)
    sends += gather_start(p, own_ref, got_y, sy, ry)
    gather_finish(p, own_ref, got_y, sy, ry, full)
    sol_ref[...] = _dots(dw_ref, full, transpose_a=True)
    mine_ref[...] = _rows_of(sol_ref, p.col, mine_ref.shape[1])[...]
    _wait_sends(sends)


def _back2_kernel(n, count, x_ref, f_ref, dw_ref, sum_ref, sol_ref, mine_ref, got_b, sb, rb, res, full, got_y, sy, ry):
    p = Place(n, count)
    p.barrier(True, True)
    sends = spread_start(p, x_ref, got_b, sb, rb)
    acc = spread_finish(p, x_ref, got_b, sb, rb)
    sum_ref[...] = acc
    res[...] = f_ref[...] - acc[acc.shape[0] - 1]
    sends += gather_start(p, res, got_y, sy, ry)
    gather_finish(p, res, got_y, sy, ry, full)
    sol_ref[...] = _dots(dw_ref, full, transpose_a=True)
    mine_ref[...] = _rows_of(sol_ref, p.col, mine_ref.shape[1])[...]
    _wait_sends(sends)


def _last_kernel(n, count, res_ref, d0_ref, own_ref, x_ref, got, s, r):
    p = Place(n, count)
    p.barrier(True, False)
    x_ref[...] = _dots(d0_ref, res_ref, transpose_a=True)
    sends = scatter_start(p, x_ref, got, s, r)
    own_ref[...] = scatter_finish(p, x_ref, got, s, r)
    _wait_sends(sends)


def _final_kernel(n, count, x_ref, f_ref, dinv_ref, own_ref, got_b, sb, rb, x2_ref, got, s, r):
    d0_ref = dinv_ref.at[0]
    p = Place(n, count)
    p.barrier(True, True)
    sends = spread_start(p, x_ref, got_b, sb, rb)
    acc = spread_finish(p, x_ref, got_b, sb, rb)
    res = f_ref[...] - acc[0]
    outs = []
    for q in range(d0_ref.shape[0]):
        outs.append(
            jnp.dot(d0_ref[q].T, res[q], precision=lax.Precision.HIGHEST, preferred_element_type=jnp.float32)
        )
    x2_ref[...] = jnp.stack(outs, 0)
    sends += scatter_start(p, x2_ref, got, s, r)
    own_ref[...] = scatter_finish(p, x2_ref, got, s, r)
    _wait_sends(sends)


def _f32(shape):
    return jax.ShapeDtypeStruct(shape, jnp.float32)


def _dma(k):
    return [pltpu.SemaphoreType.DMA((k,)), pltpu.SemaphoreType.DMA((k,))]


def _call(body, n, count, cid, args, outs, scratch):
    return pl.pallas_call(
        functools.partial(body, n, count),
        out_shape=tuple(_f32(o) for o in outs),
        in_specs=[_vmem() for a in args],
        out_specs=tuple(_vmem() for o in outs),
        scratch_shapes=scratch,
        compiler_params=_params(cid),
    )(*args)


def local(rhs, diag_inv, factor_tiles, tile_source, tile_count):
    levels = rhs.shape[0]
    owned_count = rhs.shape[1]
    share_rows = rhs.shape[2]
    columns = rhs.shape[3]
    slot_count = tile_source.shape[2]
    reach_dev = KDEV
    window_len = 2 * reach_dev + 1
    n = lax.axis_size("cols")
    count = lax.axis_size("rows")
    total_sup = count * owned_count
    row_place = lax.axis_index("rows")
    my_rows = lax.axis_index("cols") * share_rows
    highest = lax.Precision.HIGHEST
    slot_ids = jnp.arange(slot_count, dtype=jnp.int32)
    assert levels == 3 and count >= window_len
    blk = (owned_count, share_rows, columns)
    whole = (owned_count, n * share_rows, columns)
    dblk = diag_inv.shape[1:]
    dwhole = (owned_count, n * share_rows, diag_inv.shape[3])
    win = (window_len,) + blk
    slots = window_len

    def window_places(sources):
        src_level = sources // total_sup
        within = sources % total_sup
        return (
            src_level * window_len + within // owned_count - row_place + reach_dev
        ) * owned_count + within % owned_count

    def live_mask(counts):
        return (slot_ids[None, :] < counts[:, None]).astype(jnp.float32)

    def own_rows(block):
        return lax.dynamic_slice_in_dim(block, my_rows, share_rows, axis=1)

    def forward_share(height, windows):
        stacked = jnp.stack(windows, 0).reshape(height * window_len * owned_count, share_rows, columns)
        places = window_places(tile_source[height - 1])
        picked = jnp.take(stacked, places, axis=0) * live_mask(tile_count[height - 1])[:, :, None, None]
        partial_value = jnp.einsum(
            "skci,skcr->sir", factor_tiles[height - 1], picked, precision=highest
        )
        return lax.dynamic_update_slice_in_dim(
            -partial_value, rhs[height] - own_rows(partial_value), my_rows, axis=1
        )

    def buckets(height, whole_block):
        term_set = jnp.einsum(
            "skci,sir->skcr", factor_tiles[height - 1], whole_block, precision=highest
        )
        term_set = term_set * live_mask(tile_count[height - 1])[:, :, None, None]
        places = window_places(tile_source[height - 1]).reshape(-1)
        targets = height * window_len * owned_count
        one_hot = (jnp.arange(targets, dtype=jnp.int32)[:, None] == places[None, :]).astype(
            jnp.float32
        )
        outgoing = jnp.einsum(
            "ms,slg->mlg",
            one_hot,
            term_set.reshape(owned_count * slot_count, share_rows, columns),
            precision=highest,
        )
        push_outgoing = outgoing.reshape(height, window_len, owned_count, share_rows, columns)
        return push_outgoing.transpose(1, 0, 2, 3, 4)

    def vm(shape):
        return pltpu.VMEM(shape, jnp.float32)

    fv0, win0, d1 = _call(
        _first_kernel, n, count, 0, [rhs, diag_inv], [blk, win, dwhole],
        [vm((n,) + blk)] + _dma(n) + [vm(whole)] + [vm(win)] + _dma(slots) + [vm((n,) + dblk)] + _dma(n),
    )
    fv1, win1, d2 = _call(
        _level1_kernel, n, count, 1, [forward_share(1, [win0]), d1, diag_inv], [blk, win, dwhole],
        [vm(whole), vm((n,) + blk)] + _dma(n) + [vm(win)] + _dma(slots) + [vm((n,) + dblk)] + _dma(n),
    )
    fv2, sol2, mine2 = _call(
        _level2_kernel, n, count, 2, [forward_share(2, [win0, win1]), d2], [blk, whole, blk],
        [vm(whole), vm((n,) + blk)] + _dma(n) + [vm(whole), vm((n,) + blk)] + _dma(n),
    )
    out2 = buckets(2, sol2)
    got2, sol1, mine1 = _call(
        _back2_kernel, n, count, 3, [out2[:, 1:], fv1, d1], [out2[:, 1:].shape[1:], whole, blk],
        [vm(out2[:, 1:].shape)] + _dma(slots) + [vm(blk), vm(whole), vm((n,) + blk)] + _dma(n),
    )
    out1 = buckets(1, sol1) + out2[:, :1]
    (sol0,) = _call(
        _final_kernel, n, count, 4, [out1, fv0, diag_inv], [blk],
        [vm(out1.shape)] + _dma(slots) + [vm(whole), vm((n,) + blk)] + _dma(n),
    )
    return jnp.stack([sol0, mine1, mine2], 0)


def solution(mesh):
    placed = (
        P(None, "rows", "cols", None),
        P(None, "rows", "cols", None),
        P(None, "rows", None, "cols", None),
        P(None, "rows", None),
        P(None, "rows"),
    )
    return jax.shard_map(
        local, mesh=mesh, in_specs=placed, out_specs=P(None, "rows", "cols", None), check_vma=False
    )
```

```python
import functools

import jax
import jax.numpy as jnp
from jax import lax
from jax.experimental import pallas as pl
from jax.experimental.pallas import tpu as pltpu
from jax.sharding import PartitionSpec as P

KDEV = 7
MESH = pl.DeviceIdType.MESH
OFFSETS = [d for d in range(-KDEV, KDEV + 1) if d != 0]


def _params(cid):
    return pltpu.CompilerParams(collective_id=cid, has_side_effects=True)


def _vmem():
    return pl.BlockSpec(memory_space=pltpu.VMEM)


class Place:
    def __init__(self, n, count):
        self.n = n
        self.count = count
        self.col = lax.axis_index("cols")
        self.row = lax.axis_index("rows")

    def col_peer(self, k):
        return lax.rem(self.col + k, self.n)

    def row_peer(self, d):
        return lax.rem(self.row + d + self.count, self.count)

    def barrier(self, cols, rows):
        targets = []
        if cols:
            targets += [(self.row, self.col_peer(k)) for k in range(1, self.n)]
        if rows:
            targets += [(self.row_peer(d), self.col) for d in OFFSETS]
        barrier = pltpu.get_barrier_semaphore()
        for t in targets:
            pl.semaphore_signal(barrier, 1, device_id=t, device_id_type=MESH)
        pl.semaphore_wait(barrier, len(targets))


def _copy(src_ref, dst_ref, send, recv, device):
    return pltpu.make_async_remote_copy(
        src_ref=src_ref,
        dst_ref=dst_ref,
        send_sem=send,
        recv_sem=recv,
        device_id=device,
        device_id_type=MESH,
    )


def _rows_of(ref, index, chunk):
    return ref.at[:, pl.ds(pl.multiple_of(index * chunk, chunk), chunk), :]


def _start_all(copies):
    for c in copies:
        c.start()
    return copies


def _wait_sends(copies):
    for c in copies:
        c.wait_send()


def scatter_start(p, x_ref, got, send, recv):
    chunk = got.shape[2]
    out = []
    for k in range(1, p.n):
        peer = p.col_peer(k)
        out.append(
            _copy(_rows_of(x_ref, peer, chunk), got.at[p.col], send.at[peer], recv.at[p.col], (p.row, peer))
        )
    return _start_all(out)


def scatter_finish(p, x_ref, got, send, recv):
    chunk = got.shape[2]
    acc = _rows_of(x_ref, p.col, chunk)[...]
    for k in range(1, p.n):
        src = p.col_peer(p.n - k)
        _copy(_rows_of(x_ref, src, chunk), got.at[src], send.at[src], recv.at[src], (p.row, src)).wait_recv()
        acc = acc + got[src]
    return acc


def gather_start(p, y_ref, got, send, recv):
    out = []
    for k in range(1, p.n):
        peer = p.col_peer(k)
        out.append(_copy(y_ref, got.at[p.col], send.at[peer], recv.at[p.col], (p.row, peer)))
    return _start_all(out)


def gather_finish(p, y_ref, got, send, recv, full_ref):
    chunk = got.shape[2]
    _rows_of(full_ref, p.col, chunk)[...] = y_ref[...]
    for k in range(1, p.n):
        src = p.col_peer(p.n - k)
        _copy(y_ref, got.at[src], send.at[src], recv.at[src], (p.row, src)).wait_recv()
        _rows_of(full_ref, src, chunk)[...] = got[src]


def bcast_start(p, v_ref, got, send, recv):
    out = []
    for d in OFFSETS:
        out.append(_copy(v_ref, got.at[KDEV - d], send.at[KDEV + d], recv.at[KDEV - d], (p.row_peer(d), p.col)))
    return _start_all(out)


def bcast_finish(p, v_ref, got, send, recv, win_ref):
    win_ref[KDEV] = v_ref[...]
    for o in OFFSETS:
        w = KDEV + o
        _copy(v_ref, got.at[w], send.at[w], recv.at[w], (p.row_peer(o), p.col)).wait_recv()
        win_ref[w] = got[w]


def spread_start(p, x_ref, got, send, recv):
    out = []
    for d in OFFSETS:
        out.append(
            _copy(x_ref.at[KDEV + d], got.at[KDEV - d], send.at[KDEV + d], recv.at[KDEV - d], (p.row_peer(d), p.col))
        )
    return _start_all(out)


def spread_finish(p, x_ref, got, send, recv):
    acc = x_ref[KDEV]
    for o in OFFSETS:
        w = KDEV + o
        _copy(x_ref.at[w], got.at[w], send.at[w], recv.at[w], (p.row_peer(o), p.col)).wait_recv()
        acc = acc + got[w]
    return acc


def _gather_kernel(n, count, y_ref, full_ref, got, s, r):
    p = Place(n, count)
    p.barrier(True, False)
    sends = gather_start(p, y_ref, got, s, r)
    gather_finish(p, y_ref, got, s, r, full_ref)
    _wait_sends(sends)


def _scatter_kernel(n, count, x_ref, own_ref, got, s, r):
    p = Place(n, count)
    p.barrier(True, False)
    sends = scatter_start(p, x_ref, got, s, r)
    own_ref[...] = scatter_finish(p, x_ref, got, s, r)
    _wait_sends(sends)


def _bcast_gather_kernel(n, count, v_ref, d_ref, win_ref, dfull_ref, got_w, sw, rw, got_d, sd, rd):
    p = Place(n, count)
    p.barrier(True, True)
    sends = bcast_start(p, v_ref, got_w, sw, rw) + gather_start(p, d_ref, got_d, sd, rd)
    bcast_finish(p, v_ref, got_w, sw, rw, win_ref)
    gather_finish(p, d_ref, got_d, sd, rd, dfull_ref)
    _wait_sends(sends)


def _scatter_bcast_gather_kernel(
    n, count, x_ref, d_ref, own_ref, win_ref, dfull_ref, got_x, sx, rx, got_w, sw, rw, got_d, sd, rd
):
    p = Place(n, count)
    p.barrier(True, True)
    sends = scatter_start(p, x_ref, got_x, sx, rx)
    own_ref[...] = scatter_finish(p, x_ref, got_x, sx, rx)
    sends += bcast_start(p, own_ref, got_w, sw, rw) + gather_start(p, d_ref, got_d, sd, rd)
    bcast_finish(p, own_ref, got_w, sw, rw, win_ref)
    gather_finish(p, d_ref, got_d, sd, rd, dfull_ref)
    _wait_sends(sends)


def _scatter_gather_kernel(n, count, x_ref, own_ref, full_ref, got_x, sx, rx, got_y, sy, ry):
    p = Place(n, count)
    p.barrier(True, False)
    sends = scatter_start(p, x_ref, got_x, sx, rx)
    own_ref[...] = scatter_finish(p, x_ref, got_x, sx, rx)
    sends += gather_start(p, own_ref, got_y, sy, ry)
    gather_finish(p, own_ref, got_y, sy, ry, full_ref)
    _wait_sends(sends)


def _spread_gather_kernel(n, count, x_ref, f_ref, sum_ref, full_ref, got_b, sb, rb, res, got_y, sy, ry):
    p = Place(n, count)
    p.barrier(True, True)
    sends = spread_start(p, x_ref, got_b, sb, rb)
    acc = spread_finish(p, x_ref, got_b, sb, rb)
    sum_ref[...] = acc
    res[...] = f_ref[...] - acc[acc.shape[0] - 1]
    sends += gather_start(p, res, got_y, sy, ry)
    gather_finish(p, res, got_y, sy, ry, full_ref)
    _wait_sends(sends)


def _spread_kernel(n, count, x_ref, sum_ref, got_b, sb, rb):
    p = Place(n, count)
    p.barrier(False, True)
    sends = spread_start(p, x_ref, got_b, sb, rb)
    sum_ref[...] = spread_finish(p, x_ref, got_b, sb, rb)
    _wait_sends(sends)


def _dots(a_ref, b_ref, transpose_a=False):
    outs = []
    for s in range(a_ref.shape[0]):
        a = a_ref[s]
        if transpose_a:
            a = a.T
        outs.append(jnp.dot(a, b_ref[s], precision=lax.Precision.HIGHEST, preferred_element_type=jnp.float32))
    return jnp.stack(outs, 0)


def _first_kernel(n, count, rhs_ref, dinv_ref, fv_ref, win_ref, dfull_ref, got_y, sy, ry, whole, got_w, sw, rw, got_d, sd, rd):
    y_ref, d0_ref, d1_ref = rhs_ref.at[0], dinv_ref.at[0], dinv_ref.at[1]
    p = Place(n, count)
    p.barrier(True, True)
    sends = gather_start(p, y_ref, got_y, sy, ry)
    gather_finish(p, y_ref, got_y, sy, ry, whole)
    fv_ref[...] = _dots(d0_ref, whole)
    sends += bcast_start(p, fv_ref, got_w, sw, rw) + gather_start(p, d1_ref, got_d, sd, rd)
    bcast_finish(p, fv_ref, got_w, sw, rw, win_ref)
    gather_finish(p, d1_ref, got_d, sd, rd, dfull_ref)
    _wait_sends(sends)


def _level1_kernel(
    n, count, share_ref, dw_ref, dinv_ref, own_ref, win_ref, dfull_ref, x_ref, got_x, sx, rx, got_w, sw, rw, got_d, sd, rd
):
    d_ref = dinv_ref.at[2]
    p = Place(n, count)
    p.barrier(True, True)
    x_ref[...] = _dots(dw_ref, share_ref)
    sends = scatter_start(p, x_ref, got_x, sx, rx)
    own_ref[...] = scatter_finish(p, x_ref, got_x, sx, rx)
    sends += bcast_start(p, own_ref, got_w, sw, rw) + gather_start(p, d_ref, got_d, sd, rd)
    bcast_finish(p, own_ref, got_w, sw, rw, win_ref)
    gather_finish(p, d_ref, got_d, sd, rd, dfull_ref)
    _wait_sends(sends)


def _level2_kernel(n, count, share_ref, dw_ref, own_ref, sol_ref, mine_ref, x_ref, got_x, sx, rx, full, got_y, sy, ry):
    p = Place(n, count)
    p.barrier(True, False)
    x_ref[...] = _dots(dw_ref, share_ref)
    sends = scatter_start(p, x_ref, got_x, sx, rx)
    own_ref[...] = scatter_finish(p, x_ref, got_x, sx, rx)
    sends += gather_start(p, own_ref, got_y, sy, ry)
    gather_finish(p, own_ref, got_y, sy, ry, full)
    sol_ref[...] = _dots(dw_ref, full, transpose_a=True)
    mine_ref[...] = _rows_of(sol_ref, p.col, mine_ref.shape[1])[...]
    _wait_sends(sends)


def _back2_kernel(n, count, x_ref, f_ref, dw_ref, sum_ref, sol_ref, mine_ref, got_b, sb, rb, res, full, got_y, sy, ry):
    p = Place(n, count)
    p.barrier(True, True)
    sends = spread_start(p, x_ref, got_b, sb, rb)
    acc = spread_finish(p, x_ref, got_b, sb, rb)
    sum_ref[...] = acc
    res[...] = f_ref[...] - acc[acc.shape[0] - 1]
    sends += gather_start(p, res, got_y, sy, ry)
    gather_finish(p, res, got_y, sy, ry, full)
    sol_ref[...] = _dots(dw_ref, full, transpose_a=True)
    mine_ref[...] = _rows_of(sol_ref, p.col, mine_ref.shape[1])[...]
    _wait_sends(sends)


def _last_kernel(n, count, res_ref, d0_ref, own_ref, x_ref, got, s, r):
    p = Place(n, count)
    p.barrier(True, False)
    x_ref[...] = _dots(d0_ref, res_ref, transpose_a=True)
    sends = scatter_start(p, x_ref, got, s, r)
    own_ref[...] = scatter_finish(p, x_ref, got, s, r)
    _wait_sends(sends)


def _final_kernel(n, count, x_ref, f_ref, dinv_ref, own_ref, got_b, sb, rb, x2_ref, got, s, r):
    d0_ref = dinv_ref.at[0]
    p = Place(n, count)
    p.barrier(True, True)
    sends = spread_start(p, x_ref, got_b, sb, rb)
    acc = spread_finish(p, x_ref, got_b, sb, rb)
    res = f_ref[...] - acc[0]
    outs = []
    for q in range(d0_ref.shape[0]):
        outs.append(
            jnp.dot(d0_ref[q].T, res[q], precision=lax.Precision.HIGHEST, preferred_element_type=jnp.float32)
        )
    x2_ref[...] = jnp.stack(outs, 0)
    sends += scatter_start(p, x2_ref, got, s, r)
    own_ref[...] = scatter_finish(p, x2_ref, got, s, r)
    _wait_sends(sends)


def _mm(a, b):
    return jnp.dot(a, b, precision=lax.Precision.HIGHEST, preferred_element_type=jnp.float32)


def _smem():
    return pl.BlockSpec(memory_space=pltpu.SMEM)


def _share(p, wins, t_ref, lev_ref, slot_ref, sup_ref, live_ref, rhs_ref, out_ref):
    owned, share, r = rhs_ref.shape
    slots = lev_ref.shape[1]
    mine = pl.ds(pl.multiple_of(p.col * share, share), share)
    for s in range(owned):
        pieces = []
        for k in range(slots):
            w = slot_ref[s, k]
            q = sup_ref[s, k]
            v = wins[0][w, q]
            if len(wins) > 1:
                v = jnp.where(lev_ref[s, k] == 0, v, wins[1][w, q])
            pieces.append(v * live_ref[s, k])
        picked = jnp.concatenate(pieces, axis=0)
        out_ref[s] = -_mm(t_ref[s].T, picked)
        out_ref[s, mine, :] = rhs_ref[s] + out_ref[s, mine, :]


def _forward_kernel(
    n, count,
    rhs_ref, dinv_ref, t1_ref, t2_ref, lv1, sl1, su1, li1, lv2, sl2, su2, li2,
    fv0_ref, fv1_ref, sol2_ref, mine2_ref, d1_ref, d2_ref,
    got_y, sy, ry, whole, win0, got_w0, sw0, rw0, got_d1, sd1, rd1, got_d2, sd2, rd2,
    share1, x1, got_x1, sx1, rx1, win1, got_w1, sw1, rw1,
    share2, x2, got_x2, sx2, rx2, fv2, full2, got_y2, sy2, ry2,
):
    p = Place(n, count)
    p.barrier(True, True)
    sends = gather_start(p, rhs_ref.at[0], got_y, sy, ry)
    gather_finish(p, rhs_ref.at[0], got_y, sy, ry, whole)
    fv0_ref[...] = _dots(dinv_ref.at[0], whole)
    sends += bcast_start(p, fv0_ref, got_w0, sw0, rw0)
    sends += gather_start(p, dinv_ref.at[1], got_d1, sd1, rd1) + gather_start(p, dinv_ref.at[2], got_d2, sd2, rd2)
    bcast_finish(p, fv0_ref, got_w0, sw0, rw0, win0)
    gather_finish(p, dinv_ref.at[1], got_d1, sd1, rd1, d1_ref)
    _share(p, [win0], t1_ref, lv1, sl1, su1, li1, rhs_ref.at[1], share1)
    x1[...] = _dots(d1_ref, share1)
    sends += scatter_start(p, x1, got_x1, sx1, rx1)
    fv1_ref[...] = scatter_finish(p, x1, got_x1, sx1, rx1)
    sends += bcast_start(p, fv1_ref, got_w1, sw1, rw1)
    bcast_finish(p, fv1_ref, got_w1, sw1, rw1, win1)
    gather_finish(p, dinv_ref.at[2], got_d2, sd2, rd2, d2_ref)
    _share(p, [win0, win1], t2_ref, lv2, sl2, su2, li2, rhs_ref.at[2], share2)
    x2[...] = _dots(d2_ref, share2)
    sends += scatter_start(p, x2, got_x2, sx2, rx2)
    fv2[...] = scatter_finish(p, x2, got_x2, sx2, rx2)
    sends += gather_start(p, fv2, got_y2, sy2, ry2)
    gather_finish(p, fv2, got_y2, sy2, ry2, full2)
    sol2_ref[...] = _dots(d2_ref, full2, transpose_a=True)
    mine2_ref[...] = _rows_of(sol2_ref, p.col, mine2_ref.shape[1])[...]
    _wait_sends(sends)


def _f32(shape):
    return jax.ShapeDtypeStruct(shape, jnp.float32)


def _dma(k):
    return [pltpu.SemaphoreType.DMA((k,)), pltpu.SemaphoreType.DMA((k,))]


def _call(body, n, count, cid, args, outs, scratch):
    return pl.pallas_call(
        functools.partial(body, n, count),
        out_shape=tuple(_f32(o) for o in outs),
        in_specs=[_vmem() for a in args],
        out_specs=tuple(_vmem() for o in outs),
        scratch_shapes=scratch,
        compiler_params=_params(cid),
    )(*args)


def local(rhs, diag_inv, factor_tiles, tile_source, tile_count):
    levels = rhs.shape[0]
    owned_count = rhs.shape[1]
    share_rows = rhs.shape[2]
    columns = rhs.shape[3]
    slot_count = tile_source.shape[2]
    reach_dev = KDEV
    window_len = 2 * reach_dev + 1
    n = lax.axis_size("cols")
    count = lax.axis_size("rows")
    total_sup = count * owned_count
    row_place = lax.axis_index("rows")
    my_rows = lax.axis_index("cols") * share_rows
    highest = lax.Precision.HIGHEST
    slot_ids = jnp.arange(slot_count, dtype=jnp.int32)
    assert levels == 3 and count >= window_len
    blk = (owned_count, share_rows, columns)
    whole = (owned_count, n * share_rows, columns)
    dblk = diag_inv.shape[1:]
    dwhole = (owned_count, n * share_rows, diag_inv.shape[3])
    win = (window_len,) + blk
    slots = window_len

    def window_places(sources):
        src_level = sources // total_sup
        within = sources % total_sup
        return (
            src_level * window_len + within // owned_count - row_place + reach_dev
        ) * owned_count + within % owned_count

    def live_mask(counts):
        return (slot_ids[None, :] < counts[:, None]).astype(jnp.float32)

    def own_rows(block):
        return lax.dynamic_slice_in_dim(block, my_rows, share_rows, axis=1)

    def forward_share(height, windows):
        stacked = jnp.stack(windows, 0).reshape(height * window_len * owned_count, share_rows, columns)
        places = window_places(tile_source[height - 1])
        picked = jnp.take(stacked, places, axis=0) * live_mask(tile_count[height - 1])[:, :, None, None]
        partial_value = jnp.einsum(
            "skci,skcr->sir", factor_tiles[height - 1], picked, precision=highest
        )
        return lax.dynamic_update_slice_in_dim(
            -partial_value, rhs[height] - own_rows(partial_value), my_rows, axis=1
        )

    def buckets(height, whole_block):
        term_set = jnp.einsum(
            "skci,sir->skcr", factor_tiles[height - 1], whole_block, precision=highest
        )
        term_set = term_set * live_mask(tile_count[height - 1])[:, :, None, None]
        places = window_places(tile_source[height - 1]).reshape(-1)
        targets = height * window_len * owned_count
        one_hot = (jnp.arange(targets, dtype=jnp.int32)[:, None] == places[None, :]).astype(
            jnp.float32
        )
        outgoing = jnp.einsum(
            "ms,slg->mlg",
            one_hot,
            term_set.reshape(owned_count * slot_count, share_rows, columns),
            precision=highest,
        )
        push_outgoing = outgoing.reshape(height, window_len, owned_count, share_rows, columns)
        return push_outgoing.transpose(1, 0, 2, 3, 4)

    def vm(shape):
        return pltpu.VMEM(shape, jnp.float32)

    def source_tables(height):
        sources = tile_source[height - 1]
        src_level = jnp.clip(sources // total_sup, 0, height - 1)
        within = sources % total_sup
        slot = jnp.clip(within // owned_count - row_place + reach_dev, 0, window_len - 1)
        return [src_level, slot, within % owned_count, live_mask(tile_count[height - 1])]

    def flat_tiles(height):
        t = factor_tiles[height - 1]
        return t.reshape(t.shape[0], t.shape[1] * t.shape[2], t.shape[3])

    nblk = (n,) + blk
    fwd_args = [rhs, diag_inv, flat_tiles(1), flat_tiles(2)] + source_tables(1) + source_tables(2)
    fv0, fv1, sol2, mine2, d1, d2 = pl.pallas_call(
        functools.partial(_forward_kernel, n, count),
        out_shape=tuple(_f32(o) for o in [blk, blk, whole, blk, dwhole, dwhole]),
        in_specs=[_vmem()] * 4 + [_smem()] * 8,
        out_specs=tuple(_vmem() for o in range(6)),
        scratch_shapes=[vm(nblk)] + _dma(n) + [vm(whole)]
        + [vm(win), vm(win)] + _dma(slots)
        + [vm((n,) + dblk)] + _dma(n) + [vm((n,) + dblk)] + _dma(n)
        + [vm(whole), vm(whole), vm(nblk)] + _dma(n)
        + [vm(win), vm(win)] + _dma(slots)
        + [vm(whole), vm(whole), vm(nblk)] + _dma(n)
        + [vm(blk), vm(whole), vm(nblk)] + _dma(n),
        compiler_params=_params(0),
    )(*fwd_args)
    out2 = buckets(2, sol2)
    got2, sol1, mine1 = _call(
        _back2_kernel, n, count, 3, [out2[:, 1:], fv1, d1], [out2[:, 1:].shape[1:], whole, blk],
        [vm(out2[:, 1:].shape)] + _dma(slots) + [vm(blk), vm(whole), vm((n,) + blk)] + _dma(n),
    )
    out1 = buckets(1, sol1) + out2[:, :1]
    (sol0,) = _call(
        _final_kernel, n, count, 4, [out1, fv0, diag_inv], [blk],
        [vm(out1.shape)] + _dma(slots) + [vm(whole), vm((n,) + blk)] + _dma(n),
    )
    return jnp.stack([sol0, mine1, mine2], 0)


def solution(mesh):
    placed = (
        P(None, "rows", "cols", None),
        P(None, "rows", "cols", None),
        P(None, "rows", None, "cols", None),
        P(None, "rows", None),
        P(None, "rows"),
    )
    return jax.shard_map(
        local, mesh=mesh, in_specs=placed, out_specs=P(None, "rows", "cols", None), check_vma=False
    )
```

```python
import functools

import jax
import jax.numpy as jnp
from jax import lax
from jax.experimental import pallas as pl
from jax.experimental.pallas import tpu as pltpu
from jax.sharding import PartitionSpec as P

KDEV = 7
MESH = pl.DeviceIdType.MESH
OFFSETS = [d for d in range(-KDEV, KDEV + 1) if d != 0]


def _params(cid):
    return pltpu.CompilerParams(collective_id=cid, has_side_effects=True)


def _vmem():
    return pl.BlockSpec(memory_space=pltpu.VMEM)


class Place:
    def __init__(self, n, count):
        self.n = n
        self.count = count
        self.col = lax.axis_index("cols")
        self.row = lax.axis_index("rows")

    def col_peer(self, k):
        return lax.rem(self.col + k, self.n)

    def row_peer(self, d):
        return lax.rem(self.row + d + self.count, self.count)

    def barrier(self, cols, rows):
        targets = []
        if cols:
            targets += [(self.row, self.col_peer(k)) for k in range(1, self.n)]
        if rows:
            targets += [(self.row_peer(d), self.col) for d in OFFSETS]
        barrier = pltpu.get_barrier_semaphore()
        for t in targets:
            pl.semaphore_signal(barrier, 1, device_id=t, device_id_type=MESH)
        pl.semaphore_wait(barrier, len(targets))


def _copy(src_ref, dst_ref, send, recv, device):
    return pltpu.make_async_remote_copy(
        src_ref=src_ref,
        dst_ref=dst_ref,
        send_sem=send,
        recv_sem=recv,
        device_id=device,
        device_id_type=MESH,
    )


def _rows_of(ref, index, chunk):
    return ref.at[:, pl.ds(pl.multiple_of(index * chunk, chunk), chunk), :]


def _start_all(copies):
    for c in copies:
        c.start()
    return copies


def _wait_sends(copies):
    for c in copies:
        c.wait_send()


def scatter_start(p, x_ref, got, send, recv):
    chunk = got.shape[2]
    out = []
    for k in range(1, p.n):
        peer = p.col_peer(k)
        out.append(
            _copy(_rows_of(x_ref, peer, chunk), got.at[p.col], send.at[peer], recv.at[p.col], (p.row, peer))
        )
    return _start_all(out)


def scatter_finish(p, x_ref, got, send, recv):
    chunk = got.shape[2]
    acc = _rows_of(x_ref, p.col, chunk)[...]
    for k in range(1, p.n):
        src = p.col_peer(p.n - k)
        _copy(_rows_of(x_ref, src, chunk), got.at[src], send.at[src], recv.at[src], (p.row, src)).wait_recv()
        acc = acc + got[src]
    return acc


def gather_start(p, y_ref, got, send, recv):
    out = []
    for k in range(1, p.n):
        peer = p.col_peer(k)
        out.append(_copy(y_ref, got.at[p.col], send.at[peer], recv.at[p.col], (p.row, peer)))
    return _start_all(out)


def gather_finish(p, y_ref, got, send, recv, full_ref):
    chunk = got.shape[2]
    _rows_of(full_ref, p.col, chunk)[...] = y_ref[...]
    for k in range(1, p.n):
        src = p.col_peer(p.n - k)
        _copy(y_ref, got.at[src], send.at[src], recv.at[src], (p.row, src)).wait_recv()
        _rows_of(full_ref, src, chunk)[...] = got[src]


def bcast_start(p, v_ref, got, send, recv):
    out = []
    for d in OFFSETS:
        out.append(_copy(v_ref, got.at[KDEV - d], send.at[KDEV + d], recv.at[KDEV - d], (p.row_peer(d), p.col)))
    return _start_all(out)


def bcast_finish(p, v_ref, got, send, recv, win_ref):
    win_ref[KDEV] = v_ref[...]
    for o in OFFSETS:
        w = KDEV + o
        _copy(v_ref, got.at[w], send.at[w], recv.at[w], (p.row_peer(o), p.col)).wait_recv()
        win_ref[w] = got[w]


def spread_start(p, x_ref, got, send, recv):
    out = []
    for d in OFFSETS:
        out.append(
            _copy(x_ref.at[KDEV + d], got.at[KDEV - d], send.at[KDEV + d], recv.at[KDEV - d], (p.row_peer(d), p.col))
        )
    return _start_all(out)


def spread_finish(p, x_ref, got, send, recv):
    acc = x_ref[KDEV]
    for o in OFFSETS:
        w = KDEV + o
        _copy(x_ref.at[w], got.at[w], send.at[w], recv.at[w], (p.row_peer(o), p.col)).wait_recv()
        acc = acc + got[w]
    return acc


def _gather_kernel(n, count, y_ref, full_ref, got, s, r):
    p = Place(n, count)
    p.barrier(True, False)
    sends = gather_start(p, y_ref, got, s, r)
    gather_finish(p, y_ref, got, s, r, full_ref)
    _wait_sends(sends)


def _scatter_kernel(n, count, x_ref, own_ref, got, s, r):
    p = Place(n, count)
    p.barrier(True, False)
    sends = scatter_start(p, x_ref, got, s, r)
    own_ref[...] = scatter_finish(p, x_ref, got, s, r)
    _wait_sends(sends)


def _bcast_gather_kernel(n, count, v_ref, d_ref, win_ref, dfull_ref, got_w, sw, rw, got_d, sd, rd):
    p = Place(n, count)
    p.barrier(True, True)
    sends = bcast_start(p, v_ref, got_w, sw, rw) + gather_start(p, d_ref, got_d, sd, rd)
    bcast_finish(p, v_ref, got_w, sw, rw, win_ref)
    gather_finish(p, d_ref, got_d, sd, rd, dfull_ref)
    _wait_sends(sends)


def _scatter_bcast_gather_kernel(
    n, count, x_ref, d_ref, own_ref, win_ref, dfull_ref, got_x, sx, rx, got_w, sw, rw, got_d, sd, rd
):
    p = Place(n, count)
    p.barrier(True, True)
    sends = scatter_start(p, x_ref, got_x, sx, rx)
    own_ref[...] = scatter_finish(p, x_ref, got_x, sx, rx)
    sends += bcast_start(p, own_ref, got_w, sw, rw) + gather_start(p, d_ref, got_d, sd, rd)
    bcast_finish(p, own_ref, got_w, sw, rw, win_ref)
    gather_finish(p, d_ref, got_d, sd, rd, dfull_ref)
    _wait_sends(sends)


def _scatter_gather_kernel(n, count, x_ref, own_ref, full_ref, got_x, sx, rx, got_y, sy, ry):
    p = Place(n, count)
    p.barrier(True, False)
    sends = scatter_start(p, x_ref, got_x, sx, rx)
    own_ref[...] = scatter_finish(p, x_ref, got_x, sx, rx)
    sends += gather_start(p, own_ref, got_y, sy, ry)
    gather_finish(p, own_ref, got_y, sy, ry, full_ref)
    _wait_sends(sends)


def _spread_gather_kernel(n, count, x_ref, f_ref, sum_ref, full_ref, got_b, sb, rb, res, got_y, sy, ry):
    p = Place(n, count)
    p.barrier(True, True)
    sends = spread_start(p, x_ref, got_b, sb, rb)
    acc = spread_finish(p, x_ref, got_b, sb, rb)
    sum_ref[...] = acc
    res[...] = f_ref[...] - acc[acc.shape[0] - 1]
    sends += gather_start(p, res, got_y, sy, ry)
    gather_finish(p, res, got_y, sy, ry, full_ref)
    _wait_sends(sends)


def _spread_kernel(n, count, x_ref, sum_ref, got_b, sb, rb):
    p = Place(n, count)
    p.barrier(False, True)
    sends = spread_start(p, x_ref, got_b, sb, rb)
    sum_ref[...] = spread_finish(p, x_ref, got_b, sb, rb)
    _wait_sends(sends)


def _dots(a_ref, b_ref, transpose_a=False):
    outs = []
    for s in range(a_ref.shape[0]):
        a = a_ref[s]
        if transpose_a:
            a = a.T
        outs.append(jnp.dot(a, b_ref[s], precision=lax.Precision.HIGHEST, preferred_element_type=jnp.float32))
    return jnp.stack(outs, 0)


def _first_kernel(n, count, rhs_ref, dinv_ref, fv_ref, win_ref, dfull_ref, got_y, sy, ry, whole, got_w, sw, rw, got_d, sd, rd):
    y_ref, d0_ref, d1_ref = rhs_ref.at[0], dinv_ref.at[0], dinv_ref.at[1]
    p = Place(n, count)
    p.barrier(True, True)
    sends = gather_start(p, y_ref, got_y, sy, ry)
    gather_finish(p, y_ref, got_y, sy, ry, whole)
    fv_ref[...] = _dots(d0_ref, whole)
    sends += bcast_start(p, fv_ref, got_w, sw, rw) + gather_start(p, d1_ref, got_d, sd, rd)
    bcast_finish(p, fv_ref, got_w, sw, rw, win_ref)
    gather_finish(p, d1_ref, got_d, sd, rd, dfull_ref)
    _wait_sends(sends)


def _level1_kernel(
    n, count, share_ref, dw_ref, dinv_ref, own_ref, win_ref, dfull_ref, x_ref, got_x, sx, rx, got_w, sw, rw, got_d, sd, rd
):
    d_ref = dinv_ref.at[2]
    p = Place(n, count)
    p.barrier(True, True)
    x_ref[...] = _dots(dw_ref, share_ref)
    sends = scatter_start(p, x_ref, got_x, sx, rx)
    own_ref[...] = scatter_finish(p, x_ref, got_x, sx, rx)
    sends += bcast_start(p, own_ref, got_w, sw, rw) + gather_start(p, d_ref, got_d, sd, rd)
    bcast_finish(p, own_ref, got_w, sw, rw, win_ref)
    gather_finish(p, d_ref, got_d, sd, rd, dfull_ref)
    _wait_sends(sends)


def _level2_kernel(n, count, share_ref, dw_ref, own_ref, sol_ref, mine_ref, x_ref, got_x, sx, rx, full, got_y, sy, ry):
    p = Place(n, count)
    p.barrier(True, False)
    x_ref[...] = _dots(dw_ref, share_ref)
    sends = scatter_start(p, x_ref, got_x, sx, rx)
    own_ref[...] = scatter_finish(p, x_ref, got_x, sx, rx)
    sends += gather_start(p, own_ref, got_y, sy, ry)
    gather_finish(p, own_ref, got_y, sy, ry, full)
    sol_ref[...] = _dots(dw_ref, full, transpose_a=True)
    mine_ref[...] = _rows_of(sol_ref, p.col, mine_ref.shape[1])[...]
    _wait_sends(sends)


def _back2_kernel(n, count, x_ref, f_ref, dw_ref, sum_ref, sol_ref, mine_ref, got_b, sb, rb, res, full, got_y, sy, ry):
    p = Place(n, count)
    p.barrier(True, True)
    sends = spread_start(p, x_ref, got_b, sb, rb)
    acc = spread_finish(p, x_ref, got_b, sb, rb)
    sum_ref[...] = acc
    res[...] = f_ref[...] - acc[acc.shape[0] - 1]
    sends += gather_start(p, res, got_y, sy, ry)
    gather_finish(p, res, got_y, sy, ry, full)
    sol_ref[...] = _dots(dw_ref, full, transpose_a=True)
    mine_ref[...] = _rows_of(sol_ref, p.col, mine_ref.shape[1])[...]
    _wait_sends(sends)


def _last_kernel(n, count, res_ref, d0_ref, own_ref, x_ref, got, s, r):
    p = Place(n, count)
    p.barrier(True, False)
    x_ref[...] = _dots(d0_ref, res_ref, transpose_a=True)
    sends = scatter_start(p, x_ref, got, s, r)
    own_ref[...] = scatter_finish(p, x_ref, got, s, r)
    _wait_sends(sends)


def _final_kernel(n, count, x_ref, f_ref, dinv_ref, own_ref, got_b, sb, rb, x2_ref, got, s, r):
    d0_ref = dinv_ref.at[0]
    p = Place(n, count)
    p.barrier(True, True)
    sends = spread_start(p, x_ref, got_b, sb, rb)
    acc = spread_finish(p, x_ref, got_b, sb, rb)
    res = f_ref[...] - acc[0]
    outs = []
    for q in range(d0_ref.shape[0]):
        outs.append(
            jnp.dot(d0_ref[q].T, res[q], precision=lax.Precision.HIGHEST, preferred_element_type=jnp.float32)
        )
    x2_ref[...] = jnp.stack(outs, 0)
    sends += scatter_start(p, x2_ref, got, s, r)
    own_ref[...] = scatter_finish(p, x2_ref, got, s, r)
    _wait_sends(sends)


def _mm(a, b):
    return jnp.dot(a, b, precision=lax.Precision.HIGHEST, preferred_element_type=jnp.float32)


def _smem():
    return pl.BlockSpec(memory_space=pltpu.SMEM)


def _share(p, wins, t_ref, lev_ref, slot_ref, sup_ref, live_ref, rhs_ref, out_ref):
    owned, share, r = rhs_ref.shape
    slots = lev_ref.shape[1]
    mine = pl.ds(pl.multiple_of(p.col * share, share), share)
    for s in range(owned):
        pieces = []
        for k in range(slots):
            w = slot_ref[s, k]
            q = sup_ref[s, k]
            v = wins[0][w, q]
            if len(wins) > 1:
                v = jnp.where(lev_ref[s, k] == 0, v, wins[1][w, q])
            pieces.append(v * live_ref[s, k])
        picked = jnp.concatenate(pieces, axis=0)
        out_ref[s] = -_mm(t_ref[s].T, picked)
        out_ref[s, mine, :] = rhs_ref[s] + out_ref[s, mine, :]


def _terms(t_ref, sol_ref, terms_ref):
    owned, slots, share, r = terms_ref.shape
    for s in range(owned):
        full = _mm(t_ref[s], sol_ref[s])
        for k in range(slots):
            terms_ref[s, k] = full[k * share : (k + 1) * share]


def _route(bucket_ref, level, parts):
    slots, owned, share, r = bucket_ref.shape
    for w in range(slots):
        for q in range(owned):
            m = (level * slots + w) * owned + q
            acc = None
            for terms_ref, pick_ref, flag_ref in parts:
                for s in range(terms_ref.shape[0]):
                    v = terms_ref[s, pick_ref[m, s]] * flag_ref[m, s]
                    acc = v if acc is None else acc + v
            bucket_ref[w, q] = acc


def _forward_kernel(
    n, count,
    rhs_ref, dinv_ref, t1_ref, t2_ref, lv1, sl1, su1, li1, lv2, sl2, su2, li2, pk1, fl1, pk2, fl2,
    out_ref,
    fv0_ref, fv1_ref, sol2_ref, d1_ref, d2_ref,
    got_y, sy, ry, whole, win0, got_w0, sw0, rw0, got_d1, sd1, rd1, got_d2, sd2, rd2,
    share1, x1, got_x1, sx1, rx1, win1, got_w1, sw1, rw1,
    share2, x2, got_x2, sx2, rx2, fv2, full2, got_y2, sy2, ry2,
    terms2, bucket1, got_b1, sb1, rb1, res1, got_z1, sz1, rz1, full1, sol1,
    terms1, bucket0, got_b0, sb0, rb0, x0, got_x0, sx0, rx0,
):
    p = Place(n, count)
    p.barrier(True, True)
    sends = gather_start(p, rhs_ref.at[0], got_y, sy, ry)
    gather_finish(p, rhs_ref.at[0], got_y, sy, ry, whole)
    fv0_ref[...] = _dots(dinv_ref.at[0], whole)
    sends += bcast_start(p, fv0_ref, got_w0, sw0, rw0)
    sends += gather_start(p, dinv_ref.at[1], got_d1, sd1, rd1) + gather_start(p, dinv_ref.at[2], got_d2, sd2, rd2)
    bcast_finish(p, fv0_ref, got_w0, sw0, rw0, win0)
    gather_finish(p, dinv_ref.at[1], got_d1, sd1, rd1, d1_ref)
    _share(p, [win0], t1_ref, lv1, sl1, su1, li1, rhs_ref.at[1], share1)
    x1[...] = _dots(d1_ref, share1)
    sends += scatter_start(p, x1, got_x1, sx1, rx1)
    fv1_ref[...] = scatter_finish(p, x1, got_x1, sx1, rx1)
    sends += bcast_start(p, fv1_ref, got_w1, sw1, rw1)
    bcast_finish(p, fv1_ref, got_w1, sw1, rw1, win1)
    gather_finish(p, dinv_ref.at[2], got_d2, sd2, rd2, d2_ref)
    _share(p, [win0, win1], t2_ref, lv2, sl2, su2, li2, rhs_ref.at[2], share2)
    x2[...] = _dots(d2_ref, share2)
    sends += scatter_start(p, x2, got_x2, sx2, rx2)
    fv2[...] = scatter_finish(p, x2, got_x2, sx2, rx2)
    sends += gather_start(p, fv2, got_y2, sy2, ry2)
    gather_finish(p, fv2, got_y2, sy2, ry2, full2)
    sol2_ref[...] = _dots(d2_ref, full2, transpose_a=True)
    share = fv2.shape[1]
    out_ref[2] = _rows_of(sol2_ref, p.col, share)[...]
    _terms(t2_ref, sol2_ref, terms2)
    _route(bucket1, 1, [(terms2, pk2, fl2)])
    sends += spread_start(p, bucket1, got_b1, sb1, rb1)
    res1[...] = fv1_ref[...] - spread_finish(p, bucket1, got_b1, sb1, rb1)
    sends += gather_start(p, res1, got_z1, sz1, rz1)
    gather_finish(p, res1, got_z1, sz1, rz1, full1)
    sol1[...] = _dots(d1_ref, full1, transpose_a=True)
    out_ref[1] = _rows_of(sol1, p.col, share)[...]
    _terms(t1_ref, sol1, terms1)
    _route(bucket0, 0, [(terms2, pk2, fl2), (terms1, pk1, fl1)])
    sends += spread_start(p, bucket0, got_b0, sb0, rb0)
    res0 = fv0_ref[...] - spread_finish(p, bucket0, got_b0, sb0, rb0)
    d0 = dinv_ref.at[0]
    x0[...] = jnp.stack([_mm(d0[q].T, res0[q]) for q in range(res0.shape[0])], 0)
    sends += scatter_start(p, x0, got_x0, sx0, rx0)
    out_ref[0] = scatter_finish(p, x0, got_x0, sx0, rx0)
    _wait_sends(sends)


def _f32(shape):
    return jax.ShapeDtypeStruct(shape, jnp.float32)


def _dma(k):
    return [pltpu.SemaphoreType.DMA((k,)), pltpu.SemaphoreType.DMA((k,))]


def _call(body, n, count, cid, args, outs, scratch):
    return pl.pallas_call(
        functools.partial(body, n, count),
        out_shape=tuple(_f32(o) for o in outs),
        in_specs=[_vmem() for a in args],
        out_specs=tuple(_vmem() for o in outs),
        scratch_shapes=scratch,
        compiler_params=_params(cid),
    )(*args)


def local(rhs, diag_inv, factor_tiles, tile_source, tile_count):
    levels = rhs.shape[0]
    owned_count = rhs.shape[1]
    share_rows = rhs.shape[2]
    columns = rhs.shape[3]
    slot_count = tile_source.shape[2]
    reach_dev = KDEV
    window_len = 2 * reach_dev + 1
    n = lax.axis_size("cols")
    count = lax.axis_size("rows")
    total_sup = count * owned_count
    row_place = lax.axis_index("rows")
    my_rows = lax.axis_index("cols") * share_rows
    highest = lax.Precision.HIGHEST
    slot_ids = jnp.arange(slot_count, dtype=jnp.int32)
    assert levels == 3 and count >= window_len
    blk = (owned_count, share_rows, columns)
    whole = (owned_count, n * share_rows, columns)
    dblk = diag_inv.shape[1:]
    dwhole = (owned_count, n * share_rows, diag_inv.shape[3])
    win = (window_len,) + blk
    slots = window_len

    def window_places(sources):
        src_level = sources // total_sup
        within = sources % total_sup
        return (
            src_level * window_len + within // owned_count - row_place + reach_dev
        ) * owned_count + within % owned_count

    def live_mask(counts):
        return (slot_ids[None, :] < counts[:, None]).astype(jnp.float32)

    def own_rows(block):
        return lax.dynamic_slice_in_dim(block, my_rows, share_rows, axis=1)

    def forward_share(height, windows):
        stacked = jnp.stack(windows, 0).reshape(height * window_len * owned_count, share_rows, columns)
        places = window_places(tile_source[height - 1])
        picked = jnp.take(stacked, places, axis=0) * live_mask(tile_count[height - 1])[:, :, None, None]
        partial_value = jnp.einsum(
            "skci,skcr->sir", factor_tiles[height - 1], picked, precision=highest
        )
        return lax.dynamic_update_slice_in_dim(
            -partial_value, rhs[height] - own_rows(partial_value), my_rows, axis=1
        )

    def buckets(height, whole_block):
        term_set = jnp.einsum(
            "skci,sir->skcr", factor_tiles[height - 1], whole_block, precision=highest
        )
        term_set = term_set * live_mask(tile_count[height - 1])[:, :, None, None]
        places = window_places(tile_source[height - 1]).reshape(-1)
        targets = height * window_len * owned_count
        one_hot = (jnp.arange(targets, dtype=jnp.int32)[:, None] == places[None, :]).astype(
            jnp.float32
        )
        outgoing = jnp.einsum(
            "ms,slg->mlg",
            one_hot,
            term_set.reshape(owned_count * slot_count, share_rows, columns),
            precision=highest,
        )
        push_outgoing = outgoing.reshape(height, window_len, owned_count, share_rows, columns)
        return push_outgoing.transpose(1, 0, 2, 3, 4)

    def vm(shape):
        return pltpu.VMEM(shape, jnp.float32)

    def source_tables(height):
        sources = tile_source[height - 1]
        src_level = jnp.clip(sources // total_sup, 0, height - 1)
        within = sources % total_sup
        slot = jnp.clip(within // owned_count - row_place + reach_dev, 0, window_len - 1)
        return [src_level, slot, within % owned_count, live_mask(tile_count[height - 1])]

    def flat_tiles(height):
        t = factor_tiles[height - 1]
        return t.reshape(t.shape[0], t.shape[1] * t.shape[2], t.shape[3])

    def lookup(height):
        places = window_places(tile_source[height - 1])
        live = tile_count[height - 1][:, None] > slot_ids[None, :]
        targets = height * window_len * owned_count
        match = (places[None, :, :] == jnp.arange(targets, dtype=jnp.int32)[:, None, None]) & live[None]
        pick = jnp.sum(match.astype(jnp.int32) * slot_ids[None, None, :], axis=-1)
        return [pick, jnp.any(match, axis=-1).astype(jnp.float32)]

    nblk = (n,) + blk
    tiles = (owned_count, slot_count, share_rows, columns)
    args = (
        [rhs, diag_inv, flat_tiles(1), flat_tiles(2)] + source_tables(1) + source_tables(2)
        + lookup(1) + lookup(2)
    )
    outs = pl.pallas_call(
        functools.partial(_forward_kernel, n, count),
        out_shape=tuple(_f32(o) for o in [rhs.shape, blk, blk, whole, dwhole, dwhole]),
        in_specs=[_vmem()] * 4 + [_smem()] * 12,
        out_specs=tuple(_vmem() for o in range(6)),
        scratch_shapes=[vm(nblk)] + _dma(n) + [vm(whole)]
        + [vm(win), vm(win)] + _dma(slots)
        + [vm((n,) + dblk)] + _dma(n) + [vm((n,) + dblk)] + _dma(n)
        + [vm(whole), vm(whole), vm(nblk)] + _dma(n)
        + [vm(win), vm(win)] + _dma(slots)
        + [vm(whole), vm(whole), vm(nblk)] + _dma(n)
        + [vm(blk), vm(whole), vm(nblk)] + _dma(n)
        + [vm(tiles), vm(win), vm(win)] + _dma(slots) + [vm(blk), vm(nblk)] + _dma(n) + [vm(whole), vm(whole)]
        + [vm(tiles), vm(win), vm(win)] + _dma(slots) + [vm(whole), vm(nblk)] + _dma(n),
        compiler_params=_params(0),
    )(*args)
    return outs[0]


def solution(mesh):
    placed = (
        P(None, "rows", "cols", None),
        P(None, "rows", "cols", None),
        P(None, "rows", None, "cols", None),
        P(None, "rows", None),
        P(None, "rows"),
    )
    return jax.shard_map(
        local, mesh=mesh, in_specs=placed, out_specs=P(None, "rows", "cols", None), check_vma=False
    )
```

```python
import functools

import jax
import jax.numpy as jnp
from jax import lax
from jax.experimental import pallas as pl
from jax.experimental.pallas import tpu as pltpu
from jax.sharding import PartitionSpec as P

KDEV = 7
MESH = pl.DeviceIdType.MESH
OFFSETS = [d for d in range(-KDEV, KDEV + 1) if d != 0]


def _params(cid):
    return pltpu.CompilerParams(collective_id=cid, has_side_effects=True)


def _vmem():
    return pl.BlockSpec(memory_space=pltpu.VMEM)


class Place:
    def __init__(self, n, count):
        self.n = n
        self.count = count
        self.col = lax.axis_index("cols")
        self.row = lax.axis_index("rows")

    def col_peer(self, k):
        return lax.rem(self.col + k, self.n)

    def row_peer(self, d):
        return lax.rem(self.row + d + self.count, self.count)

    def barrier(self, cols, rows):
        targets = []
        if cols:
            targets += [(self.row, self.col_peer(k)) for k in range(1, self.n)]
        if rows:
            targets += [(self.row_peer(d), self.col) for d in OFFSETS]
        barrier = pltpu.get_barrier_semaphore()
        for t in targets:
            pl.semaphore_signal(barrier, 1, device_id=t, device_id_type=MESH)
        pl.semaphore_wait(barrier, len(targets))


def _copy(src_ref, dst_ref, send, recv, device):
    return pltpu.make_async_remote_copy(
        src_ref=src_ref,
        dst_ref=dst_ref,
        send_sem=send,
        recv_sem=recv,
        device_id=device,
        device_id_type=MESH,
    )


def _rows_of(ref, index, chunk):
    return ref.at[:, pl.ds(pl.multiple_of(index * chunk, chunk), chunk), :]


def _start_all(copies):
    for c in copies:
        c.start()
    return copies


def _wait_sends(copies):
    for c in copies:
        c.wait_send()


def scatter_start(p, x_ref, got, send, recv):
    chunk = got.shape[2]
    out = []
    for k in range(1, p.n):
        peer = p.col_peer(k)
        out.append(
            _copy(_rows_of(x_ref, peer, chunk), got.at[p.col], send.at[peer], recv.at[p.col], (p.row, peer))
        )
    return _start_all(out)


def scatter_finish(p, x_ref, got, send, recv):
    chunk = got.shape[2]
    acc = _rows_of(x_ref, p.col, chunk)[...]
    for k in range(1, p.n):
        src = p.col_peer(p.n - k)
        _copy(_rows_of(x_ref, src, chunk), got.at[src], send.at[src], recv.at[src], (p.row, src)).wait_recv()
        acc = acc + got[src]
    return acc


def gather_start(p, y_ref, got, send, recv):
    out = []
    for k in range(1, p.n):
        peer = p.col_peer(k)
        out.append(_copy(y_ref, got.at[p.col], send.at[peer], recv.at[p.col], (p.row, peer)))
    return _start_all(out)


def gather_finish(p, y_ref, got, send, recv, full_ref):
    chunk = got.shape[2]
    _rows_of(full_ref, p.col, chunk)[...] = y_ref[...]
    for k in range(1, p.n):
        src = p.col_peer(p.n - k)
        _copy(y_ref, got.at[src], send.at[src], recv.at[src], (p.row, src)).wait_recv()
        _rows_of(full_ref, src, chunk)[...] = got[src]


def bcast_start(p, v_ref, got, send, recv):
    out = []
    for d in OFFSETS:
        out.append(_copy(v_ref, got.at[KDEV - d], send.at[KDEV + d], recv.at[KDEV - d], (p.row_peer(d), p.col)))
    return _start_all(out)


def bcast_finish(p, v_ref, got, send, recv, win_ref):
    win_ref[KDEV] = v_ref[...]
    for o in OFFSETS:
        w = KDEV + o
        _copy(v_ref, got.at[w], send.at[w], recv.at[w], (p.row_peer(o), p.col)).wait_recv()
        win_ref[w] = got[w]


def spread_start(p, x_ref, got, send, recv):
    out = []
    for d in OFFSETS:
        out.append(
            _copy(x_ref.at[KDEV + d], got.at[KDEV - d], send.at[KDEV + d], recv.at[KDEV - d], (p.row_peer(d), p.col))
        )
    return _start_all(out)


def spread_finish(p, x_ref, got, send, recv):
    acc = x_ref[KDEV]
    for o in OFFSETS:
        w = KDEV + o
        _copy(x_ref.at[w], got.at[w], send.at[w], recv.at[w], (p.row_peer(o), p.col)).wait_recv()
        acc = acc + got[w]
    return acc


def _gather_kernel(n, count, y_ref, full_ref, got, s, r):
    p = Place(n, count)
    p.barrier(True, False)
    sends = gather_start(p, y_ref, got, s, r)
    gather_finish(p, y_ref, got, s, r, full_ref)
    _wait_sends(sends)


def _scatter_kernel(n, count, x_ref, own_ref, got, s, r):
    p = Place(n, count)
    p.barrier(True, False)
    sends = scatter_start(p, x_ref, got, s, r)
    own_ref[...] = scatter_finish(p, x_ref, got, s, r)
    _wait_sends(sends)


def _bcast_gather_kernel(n, count, v_ref, d_ref, win_ref, dfull_ref, got_w, sw, rw, got_d, sd, rd):
    p = Place(n, count)
    p.barrier(True, True)
    sends = bcast_start(p, v_ref, got_w, sw, rw) + gather_start(p, d_ref, got_d, sd, rd)
    bcast_finish(p, v_ref, got_w, sw, rw, win_ref)
    gather_finish(p, d_ref, got_d, sd, rd, dfull_ref)
    _wait_sends(sends)


def _scatter_bcast_gather_kernel(
    n, count, x_ref, d_ref, own_ref, win_ref, dfull_ref, got_x, sx, rx, got_w, sw, rw, got_d, sd, rd
):
    p = Place(n, count)
    p.barrier(True, True)
    sends = scatter_start(p, x_ref, got_x, sx, rx)
    own_ref[...] = scatter_finish(p, x_ref, got_x, sx, rx)
    sends += bcast_start(p, own_ref, got_w, sw, rw) + gather_start(p, d_ref, got_d, sd, rd)
    bcast_finish(p, own_ref, got_w, sw, rw, win_ref)
    gather_finish(p, d_ref, got_d, sd, rd, dfull_ref)
    _wait_sends(sends)


def _scatter_gather_kernel(n, count, x_ref, own_ref, full_ref, got_x, sx, rx, got_y, sy, ry):
    p = Place(n, count)
    p.barrier(True, False)
    sends = scatter_start(p, x_ref, got_x, sx, rx)
    own_ref[...] = scatter_finish(p, x_ref, got_x, sx, rx)
    sends += gather_start(p, own_ref, got_y, sy, ry)
    gather_finish(p, own_ref, got_y, sy, ry, full_ref)
    _wait_sends(sends)


def _spread_gather_kernel(n, count, x_ref, f_ref, sum_ref, full_ref, got_b, sb, rb, res, got_y, sy, ry):
    p = Place(n, count)
    p.barrier(True, True)
    sends = spread_start(p, x_ref, got_b, sb, rb)
    acc = spread_finish(p, x_ref, got_b, sb, rb)
    sum_ref[...] = acc
    res[...] = f_ref[...] - acc[acc.shape[0] - 1]
    sends += gather_start(p, res, got_y, sy, ry)
    gather_finish(p, res, got_y, sy, ry, full_ref)
    _wait_sends(sends)


def _spread_kernel(n, count, x_ref, sum_ref, got_b, sb, rb):
    p = Place(n, count)
    p.barrier(False, True)
    sends = spread_start(p, x_ref, got_b, sb, rb)
    sum_ref[...] = spread_finish(p, x_ref, got_b, sb, rb)
    _wait_sends(sends)


def _dots(a_ref, b_ref, transpose_a=False):
    outs = []
    for s in range(a_ref.shape[0]):
        a = a_ref[s]
        if transpose_a:
            a = a.T
        outs.append(jnp.dot(a, b_ref[s], precision=lax.Precision.HIGHEST, preferred_element_type=jnp.float32))
    return jnp.stack(outs, 0)


def _first_kernel(n, count, rhs_ref, dinv_ref, fv_ref, win_ref, dfull_ref, got_y, sy, ry, whole, got_w, sw, rw, got_d, sd, rd):
    y_ref, d0_ref, d1_ref = rhs_ref.at[0], dinv_ref.at[0], dinv_ref.at[1]
    p = Place(n, count)
    p.barrier(True, True)
    sends = gather_start(p, y_ref, got_y, sy, ry)
    gather_finish(p, y_ref, got_y, sy, ry, whole)
    fv_ref[...] = _dots(d0_ref, whole)
    sends += bcast_start(p, fv_ref, got_w, sw, rw) + gather_start(p, d1_ref, got_d, sd, rd)
    bcast_finish(p, fv_ref, got_w, sw, rw, win_ref)
    gather_finish(p, d1_ref, got_d, sd, rd, dfull_ref)
    _wait_sends(sends)


def _level1_kernel(
    n, count, share_ref, dw_ref, dinv_ref, own_ref, win_ref, dfull_ref, x_ref, got_x, sx, rx, got_w, sw, rw, got_d, sd, rd
):
    d_ref = dinv_ref.at[2]
    p = Place(n, count)
    p.barrier(True, True)
    x_ref[...] = _dots(dw_ref, share_ref)
    sends = scatter_start(p, x_ref, got_x, sx, rx)
    own_ref[...] = scatter_finish(p, x_ref, got_x, sx, rx)
    sends += bcast_start(p, own_ref, got_w, sw, rw) + gather_start(p, d_ref, got_d, sd, rd)
    bcast_finish(p, own_ref, got_w, sw, rw, win_ref)
    gather_finish(p, d_ref, got_d, sd, rd, dfull_ref)
    _wait_sends(sends)


def _level2_kernel(n, count, share_ref, dw_ref, own_ref, sol_ref, mine_ref, x_ref, got_x, sx, rx, full, got_y, sy, ry):
    p = Place(n, count)
    p.barrier(True, False)
    x_ref[...] = _dots(dw_ref, share_ref)
    sends = scatter_start(p, x_ref, got_x, sx, rx)
    own_ref[...] = scatter_finish(p, x_ref, got_x, sx, rx)
    sends += gather_start(p, own_ref, got_y, sy, ry)
    gather_finish(p, own_ref, got_y, sy, ry, full)
    sol_ref[...] = _dots(dw_ref, full, transpose_a=True)
    mine_ref[...] = _rows_of(sol_ref, p.col, mine_ref.shape[1])[...]
    _wait_sends(sends)


def _back2_kernel(n, count, x_ref, f_ref, dw_ref, sum_ref, sol_ref, mine_ref, got_b, sb, rb, res, full, got_y, sy, ry):
    p = Place(n, count)
    p.barrier(True, True)
    sends = spread_start(p, x_ref, got_b, sb, rb)
    acc = spread_finish(p, x_ref, got_b, sb, rb)
    sum_ref[...] = acc
    res[...] = f_ref[...] - acc[acc.shape[0] - 1]
    sends += gather_start(p, res, got_y, sy, ry)
    gather_finish(p, res, got_y, sy, ry, full)
    sol_ref[...] = _dots(dw_ref, full, transpose_a=True)
    mine_ref[...] = _rows_of(sol_ref, p.col, mine_ref.shape[1])[...]
    _wait_sends(sends)


def _last_kernel(n, count, res_ref, d0_ref, own_ref, x_ref, got, s, r):
    p = Place(n, count)
    p.barrier(True, False)
    x_ref[...] = _dots(d0_ref, res_ref, transpose_a=True)
    sends = scatter_start(p, x_ref, got, s, r)
    own_ref[...] = scatter_finish(p, x_ref, got, s, r)
    _wait_sends(sends)


def _final_kernel(n, count, x_ref, f_ref, dinv_ref, own_ref, got_b, sb, rb, x2_ref, got, s, r):
    d0_ref = dinv_ref.at[0]
    p = Place(n, count)
    p.barrier(True, True)
    sends = spread_start(p, x_ref, got_b, sb, rb)
    acc = spread_finish(p, x_ref, got_b, sb, rb)
    res = f_ref[...] - acc[0]
    outs = []
    for q in range(d0_ref.shape[0]):
        outs.append(
            jnp.dot(d0_ref[q].T, res[q], precision=lax.Precision.HIGHEST, preferred_element_type=jnp.float32)
        )
    x2_ref[...] = jnp.stack(outs, 0)
    sends += scatter_start(p, x2_ref, got, s, r)
    own_ref[...] = scatter_finish(p, x2_ref, got, s, r)
    _wait_sends(sends)


def _mm(a, b):
    return jnp.dot(a, b, precision=lax.Precision.HIGHEST, preferred_element_type=jnp.float32)


def _smem():
    return pl.BlockSpec(memory_space=pltpu.SMEM)


def _share(p, wins, t_ref, table, base, slots, rhs_ref, out_ref):
    owned, share, r = rhs_ref.shape
    mine = pl.ds(pl.multiple_of(p.col * share, share), share)
    size = owned * slots
    for s in range(owned):
        pieces = []
        for k in range(slots):
            at = base + s * slots + k
            w = table[at + size]
            q = table[at + 2 * size]
            v = wins[0][w, q]
            if len(wins) > 1:
                v = jnp.where(table[at] == 0, v, wins[1][w, q])
            pieces.append(jnp.where(table[at + 3 * size] != 0, v, 0.0))
        picked = jnp.concatenate(pieces, axis=0)
        out_ref[s] = -_mm(t_ref[s].T, picked)
        out_ref[s, mine, :] = rhs_ref[s] + out_ref[s, mine, :]


def _terms(t_ref, sol_ref, terms_ref):
    owned, slots, share, r = terms_ref.shape
    for s in range(owned):
        full = _mm(t_ref[s], sol_ref[s])
        for k in range(slots):
            terms_ref[s, k] = full[k * share : (k + 1) * share]


def _route(bucket_ref, level, table, parts):
    slots, owned, share, r = bucket_ref.shape
    for w in range(slots):
        for q in range(owned):
            m = (level * slots + w) * owned + q
            acc = None
            for terms_ref, base in parts:
                count = terms_ref.shape[0]
                for s in range(count):
                    at = base + 2 * (m * count + s)
                    v = jnp.where(table[at + 1] != 0, terms_ref[s, table[at]], 0.0)
                    acc = v if acc is None else acc + v
            bucket_ref[w, q] = acc


def _forward_kernel(
    n, count,
    rhs_ref, dinv_ref, ft_ref, table,
    out_ref,
    fv0_ref, fv1_ref, sol2_ref, d1_ref, d2_ref,
    got_y, sy, ry, whole, win0, got_w0, sw0, rw0, got_d1, sd1, rd1, got_d2, sd2, rd2,
    share1, x1, got_x1, sx1, rx1, win1, got_w1, sw1, rw1,
    share2, x2, got_x2, sx2, rx2, fv2, full2, got_y2, sy2, ry2,
    terms2, bucket1, got_b1, sb1, rb1, res1, got_z1, sz1, rz1, full1, sol1,
    terms1, bucket0, got_b0, sb0, rb0, x0, got_x0, sx0, rx0,
):
    t1_ref, t2_ref = ft_ref.at[0], ft_ref.at[1]
    owned = rhs_ref.shape[1]
    slots = terms1.shape[1]
    size = owned * slots
    lookup1 = 8 * size
    lookup2 = lookup1 + (2 * KDEV + 1) * owned * owned * 2
    p = Place(n, count)
    p.barrier(True, True)
    sends = gather_start(p, rhs_ref.at[0], got_y, sy, ry)
    gather_finish(p, rhs_ref.at[0], got_y, sy, ry, whole)
    fv0_ref[...] = _dots(dinv_ref.at[0], whole)
    sends += bcast_start(p, fv0_ref, got_w0, sw0, rw0)
    sends += gather_start(p, dinv_ref.at[1], got_d1, sd1, rd1) + gather_start(p, dinv_ref.at[2], got_d2, sd2, rd2)
    bcast_finish(p, fv0_ref, got_w0, sw0, rw0, win0)
    gather_finish(p, dinv_ref.at[1], got_d1, sd1, rd1, d1_ref)
    _share(p, [win0], t1_ref, table, 0, slots, rhs_ref.at[1], share1)
    x1[...] = _dots(d1_ref, share1)
    sends += scatter_start(p, x1, got_x1, sx1, rx1)
    fv1_ref[...] = scatter_finish(p, x1, got_x1, sx1, rx1)
    sends += bcast_start(p, fv1_ref, got_w1, sw1, rw1)
    bcast_finish(p, fv1_ref, got_w1, sw1, rw1, win1)
    gather_finish(p, dinv_ref.at[2], got_d2, sd2, rd2, d2_ref)
    _share(p, [win0, win1], t2_ref, table, 4 * size, slots, rhs_ref.at[2], share2)
    x2[...] = _dots(d2_ref, share2)
    sends += scatter_start(p, x2, got_x2, sx2, rx2)
    fv2[...] = scatter_finish(p, x2, got_x2, sx2, rx2)
    sends += gather_start(p, fv2, got_y2, sy2, ry2)
    gather_finish(p, fv2, got_y2, sy2, ry2, full2)
    sol2_ref[...] = _dots(d2_ref, full2, transpose_a=True)
    share = fv2.shape[1]
    out_ref[2] = _rows_of(sol2_ref, p.col, share)[...]
    _terms(t2_ref, sol2_ref, terms2)
    _route(bucket1, 1, table, [(terms2, lookup2)])
    sends += spread_start(p, bucket1, got_b1, sb1, rb1)
    res1[...] = fv1_ref[...] - spread_finish(p, bucket1, got_b1, sb1, rb1)
    sends += gather_start(p, res1, got_z1, sz1, rz1)
    gather_finish(p, res1, got_z1, sz1, rz1, full1)
    sol1[...] = _dots(d1_ref, full1, transpose_a=True)
    out_ref[1] = _rows_of(sol1, p.col, share)[...]
    _terms(t1_ref, sol1, terms1)
    _route(bucket0, 0, table, [(terms2, lookup2), (terms1, lookup1)])
    sends += spread_start(p, bucket0, got_b0, sb0, rb0)
    res0 = fv0_ref[...] - spread_finish(p, bucket0, got_b0, sb0, rb0)
    d0 = dinv_ref.at[0]
    x0[...] = jnp.stack([_mm(d0[q].T, res0[q]) for q in range(res0.shape[0])], 0)
    sends += scatter_start(p, x0, got_x0, sx0, rx0)
    out_ref[0] = scatter_finish(p, x0, got_x0, sx0, rx0)
    _wait_sends(sends)


def _f32(shape):
    return jax.ShapeDtypeStruct(shape, jnp.float32)


def _dma(k):
    return [pltpu.SemaphoreType.DMA((k,)), pltpu.SemaphoreType.DMA((k,))]


def _call(body, n, count, cid, args, outs, scratch):
    return pl.pallas_call(
        functools.partial(body, n, count),
        out_shape=tuple(_f32(o) for o in outs),
        in_specs=[_vmem() for a in args],
        out_specs=tuple(_vmem() for o in outs),
        scratch_shapes=scratch,
        compiler_params=_params(cid),
    )(*args)


def local(rhs, diag_inv, factor_tiles, tile_source, tile_count):
    levels = rhs.shape[0]
    owned_count = rhs.shape[1]
    share_rows = rhs.shape[2]
    columns = rhs.shape[3]
    slot_count = tile_source.shape[2]
    reach_dev = KDEV
    window_len = 2 * reach_dev + 1
    n = lax.axis_size("cols")
    count = lax.axis_size("rows")
    total_sup = count * owned_count
    row_place = lax.axis_index("rows")
    my_rows = lax.axis_index("cols") * share_rows
    highest = lax.Precision.HIGHEST
    slot_ids = jnp.arange(slot_count, dtype=jnp.int32)
    assert levels == 3 and count >= window_len
    blk = (owned_count, share_rows, columns)
    whole = (owned_count, n * share_rows, columns)
    dblk = diag_inv.shape[1:]
    dwhole = (owned_count, n * share_rows, diag_inv.shape[3])
    win = (window_len,) + blk
    slots = window_len

    def window_places(sources):
        src_level = sources // total_sup
        within = sources % total_sup
        return (
            src_level * window_len + within // owned_count - row_place + reach_dev
        ) * owned_count + within % owned_count

    def live_mask(counts):
        return (slot_ids[None, :] < counts[:, None]).astype(jnp.float32)

    def own_rows(block):
        return lax.dynamic_slice_in_dim(block, my_rows, share_rows, axis=1)

    def forward_share(height, windows):
        stacked = jnp.stack(windows, 0).reshape(height * window_len * owned_count, share_rows, columns)
        places = window_places(tile_source[height - 1])
        picked = jnp.take(stacked, places, axis=0) * live_mask(tile_count[height - 1])[:, :, None, None]
        partial_value = jnp.einsum(
            "skci,skcr->sir", factor_tiles[height - 1], picked, precision=highest
        )
        return lax.dynamic_update_slice_in_dim(
            -partial_value, rhs[height] - own_rows(partial_value), my_rows, axis=1
        )

    def buckets(height, whole_block):
        term_set = jnp.einsum(
            "skci,sir->skcr", factor_tiles[height - 1], whole_block, precision=highest
        )
        term_set = term_set * live_mask(tile_count[height - 1])[:, :, None, None]
        places = window_places(tile_source[height - 1]).reshape(-1)
        targets = height * window_len * owned_count
        one_hot = (jnp.arange(targets, dtype=jnp.int32)[:, None] == places[None, :]).astype(
            jnp.float32
        )
        outgoing = jnp.einsum(
            "ms,slg->mlg",
            one_hot,
            term_set.reshape(owned_count * slot_count, share_rows, columns),
            precision=highest,
        )
        push_outgoing = outgoing.reshape(height, window_len, owned_count, share_rows, columns)
        return push_outgoing.transpose(1, 0, 2, 3, 4)

    def vm(shape):
        return pltpu.VMEM(shape, jnp.float32)

    def source_tables(height):
        sources = tile_source[height - 1]
        src_level = jnp.clip(sources // total_sup, 0, height - 1)
        within = sources % total_sup
        slot = jnp.clip(within // owned_count - row_place + reach_dev, 0, window_len - 1)
        live = (tile_count[height - 1][:, None] > slot_ids[None, :]).astype(jnp.int32)
        return [src_level, slot, within % owned_count, live]

    def flat_tiles(height):
        t = factor_tiles[height - 1]
        return t.reshape(t.shape[0], t.shape[1] * t.shape[2], t.shape[3])

    def lookup(height):
        places = window_places(tile_source[height - 1])
        live = tile_count[height - 1][:, None] > slot_ids[None, :]
        targets = height * window_len * owned_count
        match = (places[None, :, :] == jnp.arange(targets, dtype=jnp.int32)[:, None, None]) & live[None]
        pick = jnp.sum(match.astype(jnp.int32) * slot_ids[None, None, :], axis=-1)
        return [jnp.stack([pick, jnp.any(match, axis=-1).astype(jnp.int32)], -1)]

    nblk = (n,) + blk
    tiles = (owned_count, slot_count, share_rows, columns)
    args = (
        [rhs, diag_inv, factor_tiles.reshape(factor_tiles.shape[:2] + (slot_count * share_rows, -1))]
        + [jnp.concatenate([t.reshape(-1) for t in source_tables(1) + source_tables(2) + lookup(1) + lookup(2)])]
    )
    outs = pl.pallas_call(
        functools.partial(_forward_kernel, n, count),
        out_shape=tuple(_f32(o) for o in [rhs.shape, blk, blk, whole, dwhole, dwhole]),
        in_specs=[_vmem()] * 3 + [_smem()],
        out_specs=tuple(_vmem() for o in range(6)),
        scratch_shapes=[vm(nblk)] + _dma(n) + [vm(whole)]
        + [vm(win), vm(win)] + _dma(slots)
        + [vm((n,) + dblk)] + _dma(n) + [vm((n,) + dblk)] + _dma(n)
        + [vm(whole), vm(whole), vm(nblk)] + _dma(n)
        + [vm(win), vm(win)] + _dma(slots)
        + [vm(whole), vm(whole), vm(nblk)] + _dma(n)
        + [vm(blk), vm(whole), vm(nblk)] + _dma(n)
        + [vm(tiles), vm(win), vm(win)] + _dma(slots) + [vm(blk), vm(nblk)] + _dma(n) + [vm(whole), vm(whole)]
        + [vm(tiles), vm(win), vm(win)] + _dma(slots) + [vm(whole), vm(nblk)] + _dma(n),
        compiler_params=_params(0),
    )(*args)
    return outs[0]


def solution(mesh):
    placed = (
        P(None, "rows", "cols", None),
        P(None, "rows", "cols", None),
        P(None, "rows", None, "cols", None),
        P(None, "rows", None),
        P(None, "rows"),
    )
    return jax.shard_map(
        local, mesh=mesh, in_specs=placed, out_specs=P(None, "rows", "cols", None), check_vma=False
    )
```

```python
import functools

import jax
import jax.numpy as jnp
from jax import lax
from jax.experimental import pallas as pl
from jax.experimental.pallas import tpu as pltpu
from jax.sharding import PartitionSpec as P

KDEV = 7
MESH = pl.DeviceIdType.MESH
OFFSETS = [d for d in range(-KDEV, KDEV + 1) if d != 0]


def _params(cid):
    return pltpu.CompilerParams(collective_id=cid, has_side_effects=True)


def _vmem():
    return pl.BlockSpec(memory_space=pltpu.VMEM)


class Place:
    def __init__(self, n, count):
        self.n = n
        self.count = count
        self.col = lax.axis_index("cols")
        self.row = lax.axis_index("rows")

    def col_peer(self, k):
        return lax.rem(self.col + k, self.n)

    def row_peer(self, d):
        return lax.rem(self.row + d + self.count, self.count)

    def barrier(self, cols, rows):
        targets = []
        if cols:
            targets += [(self.row, self.col_peer(k)) for k in range(1, self.n)]
        if rows:
            targets += [(self.row_peer(d), self.col) for d in OFFSETS]
        barrier = pltpu.get_barrier_semaphore()
        for t in targets:
            pl.semaphore_signal(barrier, 1, device_id=t, device_id_type=MESH)
        pl.semaphore_wait(barrier, len(targets))


def _copy(src_ref, dst_ref, send, recv, device):
    return pltpu.make_async_remote_copy(
        src_ref=src_ref,
        dst_ref=dst_ref,
        send_sem=send,
        recv_sem=recv,
        device_id=device,
        device_id_type=MESH,
    )


def _rows_of(ref, index, chunk):
    return ref.at[:, pl.ds(pl.multiple_of(index * chunk, chunk), chunk), :]


def _start_all(copies):
    for c in copies:
        c.start()
    return copies


def _wait_sends(copies):
    for c in copies:
        c.wait_send()


def scatter_start(p, x_ref, got, send, recv):
    chunk = got.shape[2]
    out = []
    for k in range(1, p.n):
        peer = p.col_peer(k)
        out.append(
            _copy(_rows_of(x_ref, peer, chunk), got.at[p.col], send.at[peer], recv.at[p.col], (p.row, peer))
        )
    return _start_all(out)


def scatter_finish(p, x_ref, got, send, recv):
    chunk = got.shape[2]
    acc = _rows_of(x_ref, p.col, chunk)[...]
    for k in range(1, p.n):
        src = p.col_peer(p.n - k)
        _copy(_rows_of(x_ref, src, chunk), got.at[src], send.at[src], recv.at[src], (p.row, src)).wait_recv()
        acc = acc + got[src]
    return acc


def gather_start(p, y_ref, got, send, recv):
    out = []
    for k in range(1, p.n):
        peer = p.col_peer(k)
        out.append(_copy(y_ref, got.at[p.col], send.at[peer], recv.at[p.col], (p.row, peer)))
    return _start_all(out)


def gather_finish(p, y_ref, got, send, recv, full_ref):
    chunk = got.shape[2]
    _rows_of(full_ref, p.col, chunk)[...] = y_ref[...]
    for k in range(1, p.n):
        src = p.col_peer(p.n - k)
        _copy(y_ref, got.at[src], send.at[src], recv.at[src], (p.row, src)).wait_recv()
        _rows_of(full_ref, src, chunk)[...] = got[src]


def bcast_start(p, v_ref, got, send, recv):
    out = []
    for d in OFFSETS:
        out.append(_copy(v_ref, got.at[KDEV - d], send.at[KDEV + d], recv.at[KDEV - d], (p.row_peer(d), p.col)))
    return _start_all(out)


def bcast_finish(p, v_ref, got, send, recv, win_ref):
    win_ref[KDEV] = v_ref[...]
    for o in OFFSETS:
        w = KDEV + o
        _copy(v_ref, got.at[w], send.at[w], recv.at[w], (p.row_peer(o), p.col)).wait_recv()
        win_ref[w] = got[w]


def spread_start(p, x_ref, got, send, recv):
    out = []
    for d in OFFSETS:
        out.append(
            _copy(x_ref.at[KDEV + d], got.at[KDEV - d], send.at[KDEV + d], recv.at[KDEV - d], (p.row_peer(d), p.col))
        )
    return _start_all(out)


def spread_finish(p, x_ref, got, send, recv):
    acc = x_ref[KDEV]
    for o in OFFSETS:
        w = KDEV + o
        _copy(x_ref.at[w], got.at[w], send.at[w], recv.at[w], (p.row_peer(o), p.col)).wait_recv()
        acc = acc + got[w]
    return acc


def _gather_kernel(n, count, y_ref, full_ref, got, s, r):
    p = Place(n, count)
    p.barrier(True, False)
    sends = gather_start(p, y_ref, got, s, r)
    gather_finish(p, y_ref, got, s, r, full_ref)
    _wait_sends(sends)


def _scatter_kernel(n, count, x_ref, own_ref, got, s, r):
    p = Place(n, count)
    p.barrier(True, False)
    sends = scatter_start(p, x_ref, got, s, r)
    own_ref[...] = scatter_finish(p, x_ref, got, s, r)
    _wait_sends(sends)


def _bcast_gather_kernel(n, count, v_ref, d_ref, win_ref, dfull_ref, got_w, sw, rw, got_d, sd, rd):
    p = Place(n, count)
    p.barrier(True, True)
    sends = bcast_start(p, v_ref, got_w, sw, rw) + gather_start(p, d_ref, got_d, sd, rd)
    bcast_finish(p, v_ref, got_w, sw, rw, win_ref)
    gather_finish(p, d_ref, got_d, sd, rd, dfull_ref)
    _wait_sends(sends)


def _scatter_bcast_gather_kernel(
    n, count, x_ref, d_ref, own_ref, win_ref, dfull_ref, got_x, sx, rx, got_w, sw, rw, got_d, sd, rd
):
    p = Place(n, count)
    p.barrier(True, True)
    sends = scatter_start(p, x_ref, got_x, sx, rx)
    own_ref[...] = scatter_finish(p, x_ref, got_x, sx, rx)
    sends += bcast_start(p, own_ref, got_w, sw, rw) + gather_start(p, d_ref, got_d, sd, rd)
    bcast_finish(p, own_ref, got_w, sw, rw, win_ref)
    gather_finish(p, d_ref, got_d, sd, rd, dfull_ref)
    _wait_sends(sends)


def _scatter_gather_kernel(n, count, x_ref, own_ref, full_ref, got_x, sx, rx, got_y, sy, ry):
    p = Place(n, count)
    p.barrier(True, False)
    sends = scatter_start(p, x_ref, got_x, sx, rx)
    own_ref[...] = scatter_finish(p, x_ref, got_x, sx, rx)
    sends += gather_start(p, own_ref, got_y, sy, ry)
    gather_finish(p, own_ref, got_y, sy, ry, full_ref)
    _wait_sends(sends)


def _spread_gather_kernel(n, count, x_ref, f_ref, sum_ref, full_ref, got_b, sb, rb, res, got_y, sy, ry):
    p = Place(n, count)
    p.barrier(True, True)
    sends = spread_start(p, x_ref, got_b, sb, rb)
    acc = spread_finish(p, x_ref, got_b, sb, rb)
    sum_ref[...] = acc
    res[...] = f_ref[...] - acc[acc.shape[0] - 1]
    sends += gather_start(p, res, got_y, sy, ry)
    gather_finish(p, res, got_y, sy, ry, full_ref)
    _wait_sends(sends)


def _spread_kernel(n, count, x_ref, sum_ref, got_b, sb, rb):
    p = Place(n, count)
    p.barrier(False, True)
    sends = spread_start(p, x_ref, got_b, sb, rb)
    sum_ref[...] = spread_finish(p, x_ref, got_b, sb, rb)
    _wait_sends(sends)


def _dots(a_ref, b_ref, transpose_a=False):
    outs = []
    for s in range(a_ref.shape[0]):
        a = a_ref[s]
        if transpose_a:
            a = a.T
        outs.append(jnp.dot(a, b_ref[s], precision=lax.Precision.HIGHEST, preferred_element_type=jnp.float32))
    return jnp.stack(outs, 0)


def _first_kernel(n, count, rhs_ref, dinv_ref, fv_ref, win_ref, dfull_ref, got_y, sy, ry, whole, got_w, sw, rw, got_d, sd, rd):
    y_ref, d0_ref, d1_ref = rhs_ref.at[0], dinv_ref.at[0], dinv_ref.at[1]
    p = Place(n, count)
    p.barrier(True, True)
    sends = gather_start(p, y_ref, got_y, sy, ry)
    gather_finish(p, y_ref, got_y, sy, ry, whole)
    fv_ref[...] = _dots(d0_ref, whole)
    sends += bcast_start(p, fv_ref, got_w, sw, rw) + gather_start(p, d1_ref, got_d, sd, rd)
    bcast_finish(p, fv_ref, got_w, sw, rw, win_ref)
    gather_finish(p, d1_ref, got_d, sd, rd, dfull_ref)
    _wait_sends(sends)


def _level1_kernel(
    n, count, share_ref, dw_ref, dinv_ref, own_ref, win_ref, dfull_ref, x_ref, got_x, sx, rx, got_w, sw, rw, got_d, sd, rd
):
    d_ref = dinv_ref.at[2]
    p = Place(n, count)
    p.barrier(True, True)
    x_ref[...] = _dots(dw_ref, share_ref)
    sends = scatter_start(p, x_ref, got_x, sx, rx)
    own_ref[...] = scatter_finish(p, x_ref, got_x, sx, rx)
    sends += bcast_start(p, own_ref, got_w, sw, rw) + gather_start(p, d_ref, got_d, sd, rd)
    bcast_finish(p, own_ref, got_w, sw, rw, win_ref)
    gather_finish(p, d_ref, got_d, sd, rd, dfull_ref)
    _wait_sends(sends)


def _level2_kernel(n, count, share_ref, dw_ref, own_ref, sol_ref, mine_ref, x_ref, got_x, sx, rx, full, got_y, sy, ry):
    p = Place(n, count)
    p.barrier(True, False)
    x_ref[...] = _dots(dw_ref, share_ref)
    sends = scatter_start(p, x_ref, got_x, sx, rx)
    own_ref[...] = scatter_finish(p, x_ref, got_x, sx, rx)
    sends += gather_start(p, own_ref, got_y, sy, ry)
    gather_finish(p, own_ref, got_y, sy, ry, full)
    sol_ref[...] = _dots(dw_ref, full, transpose_a=True)
    mine_ref[...] = _rows_of(sol_ref, p.col, mine_ref.shape[1])[...]
    _wait_sends(sends)


def _back2_kernel(n, count, x_ref, f_ref, dw_ref, sum_ref, sol_ref, mine_ref, got_b, sb, rb, res, full, got_y, sy, ry):
    p = Place(n, count)
    p.barrier(True, True)
    sends = spread_start(p, x_ref, got_b, sb, rb)
    acc = spread_finish(p, x_ref, got_b, sb, rb)
    sum_ref[...] = acc
    res[...] = f_ref[...] - acc[acc.shape[0] - 1]
    sends += gather_start(p, res, got_y, sy, ry)
    gather_finish(p, res, got_y, sy, ry, full)
    sol_ref[...] = _dots(dw_ref, full, transpose_a=True)
    mine_ref[...] = _rows_of(sol_ref, p.col, mine_ref.shape[1])[...]
    _wait_sends(sends)


def _last_kernel(n, count, res_ref, d0_ref, own_ref, x_ref, got, s, r):
    p = Place(n, count)
    p.barrier(True, False)
    x_ref[...] = _dots(d0_ref, res_ref, transpose_a=True)
    sends = scatter_start(p, x_ref, got, s, r)
    own_ref[...] = scatter_finish(p, x_ref, got, s, r)
    _wait_sends(sends)


def _final_kernel(n, count, x_ref, f_ref, dinv_ref, own_ref, got_b, sb, rb, x2_ref, got, s, r):
    d0_ref = dinv_ref.at[0]
    p = Place(n, count)
    p.barrier(True, True)
    sends = spread_start(p, x_ref, got_b, sb, rb)
    acc = spread_finish(p, x_ref, got_b, sb, rb)
    res = f_ref[...] - acc[0]
    outs = []
    for q in range(d0_ref.shape[0]):
        outs.append(
            jnp.dot(d0_ref[q].T, res[q], precision=lax.Precision.HIGHEST, preferred_element_type=jnp.float32)
        )
    x2_ref[...] = jnp.stack(outs, 0)
    sends += scatter_start(p, x2_ref, got, s, r)
    own_ref[...] = scatter_finish(p, x2_ref, got, s, r)
    _wait_sends(sends)


def _mm(a, b):
    return jnp.dot(a, b, precision=lax.Precision.HIGHEST, preferred_element_type=jnp.float32)


def _smem():
    return pl.BlockSpec(memory_space=pltpu.SMEM)


def _share(p, wins, t_ref, table, base, slots, rhs_ref, out_ref):
    owned, share, r = rhs_ref.shape
    mine = pl.ds(pl.multiple_of(p.col * share, share), share)
    size = owned * slots
    for s in range(owned):
        pieces = []
        for k in range(slots):
            at = base + s * slots + k
            w = table[at + size]
            q = table[at + 2 * size]
            v = wins[0][w, q]
            if len(wins) > 1:
                v = jnp.where(table[at] == 0, v, wins[1][w, q])
            pieces.append(jnp.where(table[at + 3 * size] != 0, v, 0.0))
        picked = jnp.concatenate(pieces, axis=0)
        out_ref[s] = -_mm(t_ref[s].T, picked)
        out_ref[s, mine, :] = rhs_ref[s] + out_ref[s, mine, :]


def _terms(t_ref, sol_ref, terms_ref):
    owned, slots, share, r = terms_ref.shape
    for s in range(owned):
        full = _mm(t_ref[s], sol_ref[s])
        for k in range(slots):
            terms_ref[s, k] = full[k * share : (k + 1) * share]


def _route(bucket_ref, level, table, parts):
    slots, owned, share, r = bucket_ref.shape
    for w in range(slots):
        for q in range(owned):
            m = (level * slots + w) * owned + q
            acc = None
            for terms_ref, base in parts:
                count = terms_ref.shape[0]
                for s in range(count):
                    at = base + 2 * (m * count + s)
                    v = jnp.where(table[at + 1] != 0, terms_ref[s, table[at]], 0.0)
                    acc = v if acc is None else acc + v
            bucket_ref[w, q] = acc


def _forward_kernel(
    n, count,
    rhs_ref, dinv_ref, ft_ref, table,
    out_ref,
    fv0_ref, fv1_ref, sol2_ref, d1_ref, d2_ref,
    got_y, sy, ry, whole, win0, got_w0, sw0, rw0, got_d1, sd1, rd1, got_d2, sd2, rd2,
    share1, x1, got_x1, sx1, rx1, win1, got_w1, sw1, rw1,
    share2, x2, got_x2, sx2, rx2, fv2, full2, got_y2, sy2, ry2,
    terms2, bucket1, got_b1, sb1, rb1, res1, got_z1, sz1, rz1, full1, sol1,
    terms1, bucket0, got_b0, sb0, rb0, x0, got_x0, sx0, rx0,
):
    t1_ref, t2_ref = ft_ref.at[0], ft_ref.at[1]
    owned = rhs_ref.shape[1]
    slots = terms1.shape[1]
    size = owned * slots
    lookup1 = 8 * size
    lookup2 = lookup1 + (2 * KDEV + 1) * owned * owned * 2
    p = Place(n, count)
    p.barrier(True, True)
    sends = gather_start(p, rhs_ref.at[0], got_y, sy, ry)
    gather_finish(p, rhs_ref.at[0], got_y, sy, ry, whole)
    fv0_ref[...] = _dots(dinv_ref.at[0], whole)
    sends += bcast_start(p, fv0_ref, got_w0, sw0, rw0)
    sends += gather_start(p, dinv_ref.at[1], got_d1, sd1, rd1)
    bcast_finish(p, fv0_ref, got_w0, sw0, rw0, win0)
    gather_finish(p, dinv_ref.at[1], got_d1, sd1, rd1, d1_ref)
    sends += gather_start(p, dinv_ref.at[2], got_d2, sd2, rd2)
    _share(p, [win0], t1_ref, table, 0, slots, rhs_ref.at[1], share1)
    x1[...] = _dots(d1_ref, share1)
    sends += scatter_start(p, x1, got_x1, sx1, rx1)
    fv1_ref[...] = scatter_finish(p, x1, got_x1, sx1, rx1)
    sends += bcast_start(p, fv1_ref, got_w1, sw1, rw1)
    bcast_finish(p, fv1_ref, got_w1, sw1, rw1, win1)
    gather_finish(p, dinv_ref.at[2], got_d2, sd2, rd2, d2_ref)
    _share(p, [win0, win1], t2_ref, table, 4 * size, slots, rhs_ref.at[2], share2)
    x2[...] = _dots(d2_ref, share2)
    sends += scatter_start(p, x2, got_x2, sx2, rx2)
    fv2[...] = scatter_finish(p, x2, got_x2, sx2, rx2)
    sends += gather_start(p, fv2, got_y2, sy2, ry2)
    gather_finish(p, fv2, got_y2, sy2, ry2, full2)
    sol2_ref[...] = _dots(d2_ref, full2, transpose_a=True)
    share = fv2.shape[1]
    out_ref[2] = _rows_of(sol2_ref, p.col, share)[...]
    _terms(t2_ref, sol2_ref, terms2)
    _route(bucket1, 1, table, [(terms2, lookup2)])
    sends += spread_start(p, bucket1, got_b1, sb1, rb1)
    res1[...] = fv1_ref[...] - spread_finish(p, bucket1, got_b1, sb1, rb1)
    sends += gather_start(p, res1, got_z1, sz1, rz1)
    gather_finish(p, res1, got_z1, sz1, rz1, full1)
    sol1[...] = _dots(d1_ref, full1, transpose_a=True)
    out_ref[1] = _rows_of(sol1, p.col, share)[...]
    _terms(t1_ref, sol1, terms1)
    _route(bucket0, 0, table, [(terms2, lookup2), (terms1, lookup1)])
    sends += spread_start(p, bucket0, got_b0, sb0, rb0)
    res0 = fv0_ref[...] - spread_finish(p, bucket0, got_b0, sb0, rb0)
    d0 = dinv_ref.at[0]
    x0[...] = jnp.stack([_mm(d0[q].T, res0[q]) for q in range(res0.shape[0])], 0)
    sends += scatter_start(p, x0, got_x0, sx0, rx0)
    out_ref[0] = scatter_finish(p, x0, got_x0, sx0, rx0)
    _wait_sends(sends)


def _f32(shape):
    return jax.ShapeDtypeStruct(shape, jnp.float32)


def _dma(k):
    return [pltpu.SemaphoreType.DMA((k,)), pltpu.SemaphoreType.DMA((k,))]


def _call(body, n, count, cid, args, outs, scratch):
    return pl.pallas_call(
        functools.partial(body, n, count),
        out_shape=tuple(_f32(o) for o in outs),
        in_specs=[_vmem() for a in args],
        out_specs=tuple(_vmem() for o in outs),
        scratch_shapes=scratch,
        compiler_params=_params(cid),
    )(*args)


def local(rhs, diag_inv, factor_tiles, tile_source, tile_count):
    levels = rhs.shape[0]
    owned_count = rhs.shape[1]
    share_rows = rhs.shape[2]
    columns = rhs.shape[3]
    slot_count = tile_source.shape[2]
    reach_dev = KDEV
    window_len = 2 * reach_dev + 1
    n = lax.axis_size("cols")
    count = lax.axis_size("rows")
    total_sup = count * owned_count
    row_place = lax.axis_index("rows")
    my_rows = lax.axis_index("cols") * share_rows
    highest = lax.Precision.HIGHEST
    slot_ids = jnp.arange(slot_count, dtype=jnp.int32)
    assert levels == 3 and count >= window_len
    blk = (owned_count, share_rows, columns)
    whole = (owned_count, n * share_rows, columns)
    dblk = diag_inv.shape[1:]
    dwhole = (owned_count, n * share_rows, diag_inv.shape[3])
    win = (window_len,) + blk
    slots = window_len

    def window_places(sources):
        src_level = sources // total_sup
        within = sources % total_sup
        return (
            src_level * window_len + within // owned_count - row_place + reach_dev
        ) * owned_count + within % owned_count

    def live_mask(counts):
        return (slot_ids[None, :] < counts[:, None]).astype(jnp.float32)

    def own_rows(block):
        return lax.dynamic_slice_in_dim(block, my_rows, share_rows, axis=1)

    def forward_share(height, windows):
        stacked = jnp.stack(windows, 0).reshape(height * window_len * owned_count, share_rows, columns)
        places = window_places(tile_source[height - 1])
        picked = jnp.take(stacked, places, axis=0) * live_mask(tile_count[height - 1])[:, :, None, None]
        partial_value = jnp.einsum(
            "skci,skcr->sir", factor_tiles[height - 1], picked, precision=highest
        )
        return lax.dynamic_update_slice_in_dim(
            -partial_value, rhs[height] - own_rows(partial_value), my_rows, axis=1
        )

    def buckets(height, whole_block):
        term_set = jnp.einsum(
            "skci,sir->skcr", factor_tiles[height - 1], whole_block, precision=highest
        )
        term_set = term_set * live_mask(tile_count[height - 1])[:, :, None, None]
        places = window_places(tile_source[height - 1]).reshape(-1)
        targets = height * window_len * owned_count
        one_hot = (jnp.arange(targets, dtype=jnp.int32)[:, None] == places[None, :]).astype(
            jnp.float32
        )
        outgoing = jnp.einsum(
            "ms,slg->mlg",
            one_hot,
            term_set.reshape(owned_count * slot_count, share_rows, columns),
            precision=highest,
        )
        push_outgoing = outgoing.reshape(height, window_len, owned_count, share_rows, columns)
        return push_outgoing.transpose(1, 0, 2, 3, 4)

    def vm(shape):
        return pltpu.VMEM(shape, jnp.float32)

    def source_tables(height):
        sources = tile_source[height - 1]
        src_level = jnp.clip(sources // total_sup, 0, height - 1)
        within = sources % total_sup
        slot = jnp.clip(within // owned_count - row_place + reach_dev, 0, window_len - 1)
        live = (tile_count[height - 1][:, None] > slot_ids[None, :]).astype(jnp.int32)
        return [src_level, slot, within % owned_count, live]

    def flat_tiles(height):
        t = factor_tiles[height - 1]
        return t.reshape(t.shape[0], t.shape[1] * t.shape[2], t.shape[3])

    def lookup(height):
        places = window_places(tile_source[height - 1])
        live = tile_count[height - 1][:, None] > slot_ids[None, :]
        targets = height * window_len * owned_count
        match = (places[None, :, :] == jnp.arange(targets, dtype=jnp.int32)[:, None, None]) & live[None]
        pick = jnp.sum(match.astype(jnp.int32) * slot_ids[None, None, :], axis=-1)
        return [jnp.stack([pick, jnp.any(match, axis=-1).astype(jnp.int32)], -1)]

    nblk = (n,) + blk
    tiles = (owned_count, slot_count, share_rows, columns)
    args = (
        [rhs, diag_inv, factor_tiles.reshape(factor_tiles.shape[:2] + (slot_count * share_rows, -1))]
        + [jnp.concatenate([t.reshape(-1) for t in source_tables(1) + source_tables(2) + lookup(1) + lookup(2)])]
    )
    outs = pl.pallas_call(
        functools.partial(_forward_kernel, n, count),
        out_shape=tuple(_f32(o) for o in [rhs.shape, blk, blk, whole, dwhole, dwhole]),
        in_specs=[_vmem()] * 3 + [_smem()],
        out_specs=tuple(_vmem() for o in range(6)),
        scratch_shapes=[vm(nblk)] + _dma(n) + [vm(whole)]
        + [vm(win), vm(win)] + _dma(slots)
        + [vm((n,) + dblk)] + _dma(n) + [vm((n,) + dblk)] + _dma(n)
        + [vm(whole), vm(whole), vm(nblk)] + _dma(n)
        + [vm(win), vm(win)] + _dma(slots)
        + [vm(whole), vm(whole), vm(nblk)] + _dma(n)
        + [vm(blk), vm(whole), vm(nblk)] + _dma(n)
        + [vm(tiles), vm(win), vm(win)] + _dma(slots) + [vm(blk), vm(nblk)] + _dma(n) + [vm(whole), vm(whole)]
        + [vm(tiles), vm(win), vm(win)] + _dma(slots) + [vm(whole), vm(nblk)] + _dma(n),
        compiler_params=_params(0),
    )(*args)
    return outs[0]


def solution(mesh):
    placed = (
        P(None, "rows", "cols", None),
        P(None, "rows", "cols", None),
        P(None, "rows", None, "cols", None),
        P(None, "rows", None),
        P(None, "rows"),
    )
    return jax.shard_map(
        local, mesh=mesh, in_specs=placed, out_specs=P(None, "rows", "cols", None), check_vma=False
    )
```

```python
import functools

import jax
import jax.numpy as jnp
from jax import lax
from jax.experimental import pallas as pl
from jax.experimental.pallas import tpu as pltpu
from jax.sharding import PartitionSpec as P

KDEV = 7
MESH = pl.DeviceIdType.MESH
OFFSETS = [d for d in range(-KDEV, KDEV + 1) if d != 0]
SEND_OFFSETS = sorted(OFFSETS, key=lambda d: (-abs(d), d))


def _send_order(n):
    return sorted(range(1, n), key=lambda k: (-min(k, n - k), k))


def _params(cid):
    return pltpu.CompilerParams(collective_id=cid, has_side_effects=True)


def _vmem():
    return pl.BlockSpec(memory_space=pltpu.VMEM)


class Place:
    def __init__(self, n, count):
        self.n = n
        self.count = count
        self.col = lax.axis_index("cols")
        self.row = lax.axis_index("rows")

    def col_peer(self, k):
        return lax.rem(self.col + k, self.n)

    def row_peer(self, d):
        return lax.rem(self.row + d + self.count, self.count)

    def barrier(self, cols, rows):
        targets = []
        if cols:
            targets += [(self.row, self.col_peer(k)) for k in range(1, self.n)]
        if rows:
            targets += [(self.row_peer(d), self.col) for d in OFFSETS]
        barrier = pltpu.get_barrier_semaphore()
        for t in targets:
            pl.semaphore_signal(barrier, 1, device_id=t, device_id_type=MESH)
        pl.semaphore_wait(barrier, len(targets))


def _copy(src_ref, dst_ref, send, recv, device):
    return pltpu.make_async_remote_copy(
        src_ref=src_ref,
        dst_ref=dst_ref,
        send_sem=send,
        recv_sem=recv,
        device_id=device,
        device_id_type=MESH,
    )


def _rows_of(ref, index, chunk):
    return ref.at[:, pl.ds(pl.multiple_of(index * chunk, chunk), chunk), :]


def _start_all(copies):
    for c in copies:
        c.start()
    return copies


def _wait_sends(copies):
    for c in copies:
        c.wait_send()


def scatter_start(p, x_ref, got, send, recv):
    chunk = got.shape[2]
    out = []
    for k in _send_order(p.n):
        peer = p.col_peer(k)
        out.append(
            _copy(_rows_of(x_ref, peer, chunk), got.at[p.col], send.at[peer], recv.at[p.col], (p.row, peer))
        )
    return _start_all(out)


def scatter_finish(p, x_ref, got, send, recv):
    chunk = got.shape[2]
    acc = _rows_of(x_ref, p.col, chunk)[...]
    for k in range(1, p.n):
        src = p.col_peer(p.n - k)
        _copy(_rows_of(x_ref, src, chunk), got.at[src], send.at[src], recv.at[src], (p.row, src)).wait_recv()
        acc = acc + got[src]
    return acc


def gather_start(p, y_ref, got, send, recv):
    out = []
    for k in _send_order(p.n):
        peer = p.col_peer(k)
        out.append(_copy(y_ref, got.at[p.col], send.at[peer], recv.at[p.col], (p.row, peer)))
    return _start_all(out)


def gather_finish(p, y_ref, got, send, recv, full_ref):
    chunk = got.shape[2]
    _rows_of(full_ref, p.col, chunk)[...] = y_ref[...]
    for k in range(1, p.n):
        src = p.col_peer(p.n - k)
        _copy(y_ref, got.at[src], send.at[src], recv.at[src], (p.row, src)).wait_recv()
        _rows_of(full_ref, src, chunk)[...] = got[src]


def bcast_start(p, v_ref, got, send, recv):
    out = []
    for d in SEND_OFFSETS:
        out.append(_copy(v_ref, got.at[KDEV - d], send.at[KDEV + d], recv.at[KDEV - d], (p.row_peer(d), p.col)))
    return _start_all(out)


def bcast_finish(p, v_ref, got, send, recv, win_ref):
    win_ref[KDEV] = v_ref[...]
    for o in OFFSETS:
        w = KDEV + o
        _copy(v_ref, got.at[w], send.at[w], recv.at[w], (p.row_peer(o), p.col)).wait_recv()
        win_ref[w] = got[w]


def spread_start(p, x_ref, got, send, recv):
    out = []
    for d in SEND_OFFSETS:
        out.append(
            _copy(x_ref.at[KDEV + d], got.at[KDEV - d], send.at[KDEV + d], recv.at[KDEV - d], (p.row_peer(d), p.col))
        )
    return _start_all(out)


def spread_finish(p, x_ref, got, send, recv):
    acc = x_ref[KDEV]
    for o in OFFSETS:
        w = KDEV + o
        _copy(x_ref.at[w], got.at[w], send.at[w], recv.at[w], (p.row_peer(o), p.col)).wait_recv()
        acc = acc + got[w]
    return acc


def _gather_kernel(n, count, y_ref, full_ref, got, s, r):
    p = Place(n, count)
    p.barrier(True, False)
    sends = gather_start(p, y_ref, got, s, r)
    gather_finish(p, y_ref, got, s, r, full_ref)
    _wait_sends(sends)


def _scatter_kernel(n, count, x_ref, own_ref, got, s, r):
    p = Place(n, count)
    p.barrier(True, False)
    sends = scatter_start(p, x_ref, got, s, r)
    own_ref[...] = scatter_finish(p, x_ref, got, s, r)
    _wait_sends(sends)


def _bcast_gather_kernel(n, count, v_ref, d_ref, win_ref, dfull_ref, got_w, sw, rw, got_d, sd, rd):
    p = Place(n, count)
    p.barrier(True, True)
    sends = bcast_start(p, v_ref, got_w, sw, rw) + gather_start(p, d_ref, got_d, sd, rd)
    bcast_finish(p, v_ref, got_w, sw, rw, win_ref)
    gather_finish(p, d_ref, got_d, sd, rd, dfull_ref)
    _wait_sends(sends)


def _scatter_bcast_gather_kernel(
    n, count, x_ref, d_ref, own_ref, win_ref, dfull_ref, got_x, sx, rx, got_w, sw, rw, got_d, sd, rd
):
    p = Place(n, count)
    p.barrier(True, True)
    sends = scatter_start(p, x_ref, got_x, sx, rx)
    own_ref[...] = scatter_finish(p, x_ref, got_x, sx, rx)
    sends += bcast_start(p, own_ref, got_w, sw, rw) + gather_start(p, d_ref, got_d, sd, rd)
    bcast_finish(p, own_ref, got_w, sw, rw, win_ref)
    gather_finish(p, d_ref, got_d, sd, rd, dfull_ref)
    _wait_sends(sends)


def _scatter_gather_kernel(n, count, x_ref, own_ref, full_ref, got_x, sx, rx, got_y, sy, ry):
    p = Place(n, count)
    p.barrier(True, False)
    sends = scatter_start(p, x_ref, got_x, sx, rx)
    own_ref[...] = scatter_finish(p, x_ref, got_x, sx, rx)
    sends += gather_start(p, own_ref, got_y, sy, ry)
    gather_finish(p, own_ref, got_y, sy, ry, full_ref)
    _wait_sends(sends)


def _spread_gather_kernel(n, count, x_ref, f_ref, sum_ref, full_ref, got_b, sb, rb, res, got_y, sy, ry):
    p = Place(n, count)
    p.barrier(True, True)
    sends = spread_start(p, x_ref, got_b, sb, rb)
    acc = spread_finish(p, x_ref, got_b, sb, rb)
    sum_ref[...] = acc
    res[...] = f_ref[...] - acc[acc.shape[0] - 1]
    sends += gather_start(p, res, got_y, sy, ry)
    gather_finish(p, res, got_y, sy, ry, full_ref)
    _wait_sends(sends)


def _spread_kernel(n, count, x_ref, sum_ref, got_b, sb, rb):
    p = Place(n, count)
    p.barrier(False, True)
    sends = spread_start(p, x_ref, got_b, sb, rb)
    sum_ref[...] = spread_finish(p, x_ref, got_b, sb, rb)
    _wait_sends(sends)


def _dots(a_ref, b_ref, transpose_a=False):
    outs = []
    for s in range(a_ref.shape[0]):
        a = a_ref[s]
        if transpose_a:
            a = a.T
        outs.append(jnp.dot(a, b_ref[s], precision=lax.Precision.HIGHEST, preferred_element_type=jnp.float32))
    return jnp.stack(outs, 0)


def _first_kernel(n, count, rhs_ref, dinv_ref, fv_ref, win_ref, dfull_ref, got_y, sy, ry, whole, got_w, sw, rw, got_d, sd, rd):
    y_ref, d0_ref, d1_ref = rhs_ref.at[0], dinv_ref.at[0], dinv_ref.at[1]
    p = Place(n, count)
    p.barrier(True, True)
    sends = gather_start(p, y_ref, got_y, sy, ry)
    gather_finish(p, y_ref, got_y, sy, ry, whole)
    fv_ref[...] = _dots(d0_ref, whole)
    sends += bcast_start(p, fv_ref, got_w, sw, rw) + gather_start(p, d1_ref, got_d, sd, rd)
    bcast_finish(p, fv_ref, got_w, sw, rw, win_ref)
    gather_finish(p, d1_ref, got_d, sd, rd, dfull_ref)
    _wait_sends(sends)


def _level1_kernel(
    n, count, share_ref, dw_ref, dinv_ref, own_ref, win_ref, dfull_ref, x_ref, got_x, sx, rx, got_w, sw, rw, got_d, sd, rd
):
    d_ref = dinv_ref.at[2]
    p = Place(n, count)
    p.barrier(True, True)
    x_ref[...] = _dots(dw_ref, share_ref)
    sends = scatter_start(p, x_ref, got_x, sx, rx)
    own_ref[...] = scatter_finish(p, x_ref, got_x, sx, rx)
    sends += bcast_start(p, own_ref, got_w, sw, rw) + gather_start(p, d_ref, got_d, sd, rd)
    bcast_finish(p, own_ref, got_w, sw, rw, win_ref)
    gather_finish(p, d_ref, got_d, sd, rd, dfull_ref)
    _wait_sends(sends)


def _level2_kernel(n, count, share_ref, dw_ref, own_ref, sol_ref, mine_ref, x_ref, got_x, sx, rx, full, got_y, sy, ry):
    p = Place(n, count)
    p.barrier(True, False)
    x_ref[...] = _dots(dw_ref, share_ref)
    sends = scatter_start(p, x_ref, got_x, sx, rx)
    own_ref[...] = scatter_finish(p, x_ref, got_x, sx, rx)
    sends += gather_start(p, own_ref, got_y, sy, ry)
    gather_finish(p, own_ref, got_y, sy, ry, full)
    sol_ref[...] = _dots(dw_ref, full, transpose_a=True)
    mine_ref[...] = _rows_of(sol_ref, p.col, mine_ref.shape[1])[...]
    _wait_sends(sends)


def _back2_kernel(n, count, x_ref, f_ref, dw_ref, sum_ref, sol_ref, mine_ref, got_b, sb, rb, res, full, got_y, sy, ry):
    p = Place(n, count)
    p.barrier(True, True)
    sends = spread_start(p, x_ref, got_b, sb, rb)
    acc = spread_finish(p, x_ref, got_b, sb, rb)
    sum_ref[...] = acc
    res[...] = f_ref[...] - acc[acc.shape[0] - 1]
    sends += gather_start(p, res, got_y, sy, ry)
    gather_finish(p, res, got_y, sy, ry, full)
    sol_ref[...] = _dots(dw_ref, full, transpose_a=True)
    mine_ref[...] = _rows_of(sol_ref, p.col, mine_ref.shape[1])[...]
    _wait_sends(sends)


def _last_kernel(n, count, res_ref, d0_ref, own_ref, x_ref, got, s, r):
    p = Place(n, count)
    p.barrier(True, False)
    x_ref[...] = _dots(d0_ref, res_ref, transpose_a=True)
    sends = scatter_start(p, x_ref, got, s, r)
    own_ref[...] = scatter_finish(p, x_ref, got, s, r)
    _wait_sends(sends)


def _final_kernel(n, count, x_ref, f_ref, dinv_ref, own_ref, got_b, sb, rb, x2_ref, got, s, r):
    d0_ref = dinv_ref.at[0]
    p = Place(n, count)
    p.barrier(True, True)
    sends = spread_start(p, x_ref, got_b, sb, rb)
    acc = spread_finish(p, x_ref, got_b, sb, rb)
    res = f_ref[...] - acc[0]
    outs = []
    for q in range(d0_ref.shape[0]):
        outs.append(
            jnp.dot(d0_ref[q].T, res[q], precision=lax.Precision.HIGHEST, preferred_element_type=jnp.float32)
        )
    x2_ref[...] = jnp.stack(outs, 0)
    sends += scatter_start(p, x2_ref, got, s, r)
    own_ref[...] = scatter_finish(p, x2_ref, got, s, r)
    _wait_sends(sends)


def _mm(a, b):
    return jnp.dot(a, b, precision=lax.Precision.HIGHEST, preferred_element_type=jnp.float32)


def _smem():
    return pl.BlockSpec(memory_space=pltpu.SMEM)


def _share(p, wins, t_ref, table, base, slots, rhs_ref, out_ref):
    owned, share, r = rhs_ref.shape
    mine = pl.ds(pl.multiple_of(p.col * share, share), share)
    size = owned * slots
    for s in range(owned):
        pieces = []
        for k in range(slots):
            at = base + s * slots + k
            w = table[at + size]
            q = table[at + 2 * size]
            v = wins[0][w, q]
            if len(wins) > 1:
                v = jnp.where(table[at] == 0, v, wins[1][w, q])
            pieces.append(jnp.where(table[at + 3 * size] != 0, v, 0.0))
        picked = jnp.concatenate(pieces, axis=0)
        out_ref[s] = -_mm(t_ref[s].T, picked)
        out_ref[s, mine, :] = rhs_ref[s] + out_ref[s, mine, :]


def _terms(t_ref, sol_ref, terms_ref):
    owned, slots, share, r = terms_ref.shape
    for s in range(owned):
        full = _mm(t_ref[s], sol_ref[s])
        for k in range(slots):
            terms_ref[s, k] = full[k * share : (k + 1) * share]


def _route(bucket_ref, level, table, parts):
    slots, owned, share, r = bucket_ref.shape
    for w in range(slots):
        for q in range(owned):
            m = (level * slots + w) * owned + q
            acc = None
            for terms_ref, base in parts:
                count = terms_ref.shape[0]
                for s in range(count):
                    at = base + 2 * (m * count + s)
                    v = jnp.where(table[at + 1] != 0, terms_ref[s, table[at]], 0.0)
                    acc = v if acc is None else acc + v
            bucket_ref[w, q] = acc


def _forward_kernel(
    n, count,
    rhs_ref, dinv_ref, ft_ref, table,
    out_ref,
    fv0_ref, fv1_ref, sol2_ref, d1_ref, d2_ref,
    got_y, sy, ry, whole, win0, got_w0, sw0, rw0, got_d1, sd1, rd1, got_d2, sd2, rd2,
    share1, x1, got_x1, sx1, rx1, win1, got_w1, sw1, rw1,
    share2, x2, got_x2, sx2, rx2, fv2, full2, got_y2, sy2, ry2,
    terms2, bucket1, got_b1, sb1, rb1, res1, got_z1, sz1, rz1, full1, sol1,
    terms1, bucket0, got_b0, sb0, rb0, x0, got_x0, sx0, rx0,
):
    t1_ref, t2_ref = ft_ref.at[0], ft_ref.at[1]
    owned = rhs_ref.shape[1]
    slots = terms1.shape[1]
    size = owned * slots
    lookup1 = 8 * size
    lookup2 = lookup1 + (2 * KDEV + 1) * owned * owned * 2
    p = Place(n, count)
    p.barrier(True, True)
    sends = gather_start(p, rhs_ref.at[0], got_y, sy, ry)
    gather_finish(p, rhs_ref.at[0], got_y, sy, ry, whole)
    fv0_ref[...] = _dots(dinv_ref.at[0], whole)
    sends += bcast_start(p, fv0_ref, got_w0, sw0, rw0)
    sends += gather_start(p, dinv_ref.at[1], got_d1, sd1, rd1) + gather_start(p, dinv_ref.at[2], got_d2, sd2, rd2)
    bcast_finish(p, fv0_ref, got_w0, sw0, rw0, win0)
    gather_finish(p, dinv_ref.at[1], got_d1, sd1, rd1, d1_ref)
    _share(p, [win0], t1_ref, table, 0, slots, rhs_ref.at[1], share1)
    x1[...] = _dots(d1_ref, share1)
    sends += scatter_start(p, x1, got_x1, sx1, rx1)
    fv1_ref[...] = scatter_finish(p, x1, got_x1, sx1, rx1)
    sends += bcast_start(p, fv1_ref, got_w1, sw1, rw1)
    bcast_finish(p, fv1_ref, got_w1, sw1, rw1, win1)
    gather_finish(p, dinv_ref.at[2], got_d2, sd2, rd2, d2_ref)
    _share(p, [win0, win1], t2_ref, table, 4 * size, slots, rhs_ref.at[2], share2)
    x2[...] = _dots(d2_ref, share2)
    sends += scatter_start(p, x2, got_x2, sx2, rx2)
    fv2[...] = scatter_finish(p, x2, got_x2, sx2, rx2)
    sends += gather_start(p, fv2, got_y2, sy2, ry2)
    gather_finish(p, fv2, got_y2, sy2, ry2, full2)
    sol2_ref[...] = _dots(d2_ref, full2, transpose_a=True)
    share = fv2.shape[1]
    out_ref[2] = _rows_of(sol2_ref, p.col, share)[...]
    _terms(t2_ref, sol2_ref, terms2)
    _route(bucket1, 1, table, [(terms2, lookup2)])
    sends += spread_start(p, bucket1, got_b1, sb1, rb1)
    res1[...] = fv1_ref[...] - spread_finish(p, bucket1, got_b1, sb1, rb1)
    sends += gather_start(p, res1, got_z1, sz1, rz1)
    gather_finish(p, res1, got_z1, sz1, rz1, full1)
    sol1[...] = _dots(d1_ref, full1, transpose_a=True)
    out_ref[1] = _rows_of(sol1, p.col, share)[...]
    _terms(t1_ref, sol1, terms1)
    _route(bucket0, 0, table, [(terms2, lookup2), (terms1, lookup1)])
    sends += spread_start(p, bucket0, got_b0, sb0, rb0)
    res0 = fv0_ref[...] - spread_finish(p, bucket0, got_b0, sb0, rb0)
    d0 = dinv_ref.at[0]
    x0[...] = jnp.stack([_mm(d0[q].T, res0[q]) for q in range(res0.shape[0])], 0)
    sends += scatter_start(p, x0, got_x0, sx0, rx0)
    out_ref[0] = scatter_finish(p, x0, got_x0, sx0, rx0)
    _wait_sends(sends)


def _f32(shape):
    return jax.ShapeDtypeStruct(shape, jnp.float32)


def _dma(k):
    return [pltpu.SemaphoreType.DMA((k,)), pltpu.SemaphoreType.DMA((k,))]


def _call(body, n, count, cid, args, outs, scratch):
    return pl.pallas_call(
        functools.partial(body, n, count),
        out_shape=tuple(_f32(o) for o in outs),
        in_specs=[_vmem() for a in args],
        out_specs=tuple(_vmem() for o in outs),
        scratch_shapes=scratch,
        compiler_params=_params(cid),
    )(*args)


def local(rhs, diag_inv, factor_tiles, tile_source, tile_count):
    levels = rhs.shape[0]
    owned_count = rhs.shape[1]
    share_rows = rhs.shape[2]
    columns = rhs.shape[3]
    slot_count = tile_source.shape[2]
    reach_dev = KDEV
    window_len = 2 * reach_dev + 1
    n = lax.axis_size("cols")
    count = lax.axis_size("rows")
    total_sup = count * owned_count
    row_place = lax.axis_index("rows")
    my_rows = lax.axis_index("cols") * share_rows
    highest = lax.Precision.HIGHEST
    slot_ids = jnp.arange(slot_count, dtype=jnp.int32)
    assert levels == 3 and count >= window_len
    blk = (owned_count, share_rows, columns)
    whole = (owned_count, n * share_rows, columns)
    dblk = diag_inv.shape[1:]
    dwhole = (owned_count, n * share_rows, diag_inv.shape[3])
    win = (window_len,) + blk
    slots = window_len

    def window_places(sources):
        src_level = sources // total_sup
        within = sources % total_sup
        return (
            src_level * window_len + within // owned_count - row_place + reach_dev
        ) * owned_count + within % owned_count

    def live_mask(counts):
        return (slot_ids[None, :] < counts[:, None]).astype(jnp.float32)

    def own_rows(block):
        return lax.dynamic_slice_in_dim(block, my_rows, share_rows, axis=1)

    def forward_share(height, windows):
        stacked = jnp.stack(windows, 0).reshape(height * window_len * owned_count, share_rows, columns)
        places = window_places(tile_source[height - 1])
        picked = jnp.take(stacked, places, axis=0) * live_mask(tile_count[height - 1])[:, :, None, None]
        partial_value = jnp.einsum(
            "skci,skcr->sir", factor_tiles[height - 1], picked, precision=highest
        )
        return lax.dynamic_update_slice_in_dim(
            -partial_value, rhs[height] - own_rows(partial_value), my_rows, axis=1
        )

    def buckets(height, whole_block):
        term_set = jnp.einsum(
            "skci,sir->skcr", factor_tiles[height - 1], whole_block, precision=highest
        )
        term_set = term_set * live_mask(tile_count[height - 1])[:, :, None, None]
        places = window_places(tile_source[height - 1]).reshape(-1)
        targets = height * window_len * owned_count
        one_hot = (jnp.arange(targets, dtype=jnp.int32)[:, None] == places[None, :]).astype(
            jnp.float32
        )
        outgoing = jnp.einsum(
            "ms,slg->mlg",
            one_hot,
            term_set.reshape(owned_count * slot_count, share_rows, columns),
            precision=highest,
        )
        push_outgoing = outgoing.reshape(height, window_len, owned_count, share_rows, columns)
        return push_outgoing.transpose(1, 0, 2, 3, 4)

    def vm(shape):
        return pltpu.VMEM(shape, jnp.float32)

    def source_tables(height):
        sources = tile_source[height - 1]
        src_level = jnp.clip(sources // total_sup, 0, height - 1)
        within = sources % total_sup
        slot = jnp.clip(within // owned_count - row_place + reach_dev, 0, window_len - 1)
        live = (tile_count[height - 1][:, None] > slot_ids[None, :]).astype(jnp.int32)
        return [src_level, slot, within % owned_count, live]

    def flat_tiles(height):
        t = factor_tiles[height - 1]
        return t.reshape(t.shape[0], t.shape[1] * t.shape[2], t.shape[3])

    def lookup(height):
        places = window_places(tile_source[height - 1])
        live = tile_count[height - 1][:, None] > slot_ids[None, :]
        targets = height * window_len * owned_count
        match = (places[None, :, :] == jnp.arange(targets, dtype=jnp.int32)[:, None, None]) & live[None]
        pick = jnp.sum(match.astype(jnp.int32) * slot_ids[None, None, :], axis=-1)
        return [jnp.stack([pick, jnp.any(match, axis=-1).astype(jnp.int32)], -1)]

    nblk = (n,) + blk
    tiles = (owned_count, slot_count, share_rows, columns)
    args = (
        [rhs, diag_inv, factor_tiles.reshape(factor_tiles.shape[:2] + (slot_count * share_rows, -1))]
        + [jnp.concatenate([t.reshape(-1) for t in source_tables(1) + source_tables(2) + lookup(1) + lookup(2)])]
    )
    outs = pl.pallas_call(
        functools.partial(_forward_kernel, n, count),
        out_shape=tuple(_f32(o) for o in [rhs.shape, blk, blk, whole, dwhole, dwhole]),
        in_specs=[_vmem()] * 3 + [_smem()],
        out_specs=tuple(_vmem() for o in range(6)),
        scratch_shapes=[vm(nblk)] + _dma(n) + [vm(whole)]
        + [vm(win), vm(win)] + _dma(slots)
        + [vm((n,) + dblk)] + _dma(n) + [vm((n,) + dblk)] + _dma(n)
        + [vm(whole), vm(whole), vm(nblk)] + _dma(n)
        + [vm(win), vm(win)] + _dma(slots)
        + [vm(whole), vm(whole), vm(nblk)] + _dma(n)
        + [vm(blk), vm(whole), vm(nblk)] + _dma(n)
        + [vm(tiles), vm(win), vm(win)] + _dma(slots) + [vm(blk), vm(nblk)] + _dma(n) + [vm(whole), vm(whole)]
        + [vm(tiles), vm(win), vm(win)] + _dma(slots) + [vm(whole), vm(nblk)] + _dma(n),
        compiler_params=_params(0),
    )(*args)
    return outs[0]


def solution(mesh):
    placed = (
        P(None, "rows", "cols", None),
        P(None, "rows", "cols", None),
        P(None, "rows", None, "cols", None),
        P(None, "rows", None),
        P(None, "rows"),
    )
    return jax.shard_map(
        local, mesh=mesh, in_specs=placed, out_specs=P(None, "rows", "cols", None), check_vma=False
    )
```

```python
import functools

import jax
import jax.numpy as jnp
from jax import lax
from jax.experimental import pallas as pl
from jax.experimental.pallas import tpu as pltpu
from jax.sharding import PartitionSpec as P

KDEV = 7
MESH = pl.DeviceIdType.MESH
OFFSETS = [d for d in range(-KDEV, KDEV + 1) if d != 0]
SEND_OFFSETS = sorted(OFFSETS, key=lambda d: (-abs(d), d))


def _send_order(n):
    return sorted(range(1, n), key=lambda k: (-min(k, n - k), k))


def _params(cid):
    return pltpu.CompilerParams(collective_id=cid, has_side_effects=True)


def _vmem():
    return pl.BlockSpec(memory_space=pltpu.VMEM)


class Place:
    def __init__(self, n, count):
        self.n = n
        self.count = count
        self.col = lax.axis_index("cols")
        self.row = lax.axis_index("rows")

    def col_peer(self, k):
        return lax.rem(self.col + k, self.n)

    def row_peer(self, d):
        return lax.rem(self.row + d + self.count, self.count)

    def barrier(self, cols, rows):
        targets = []
        if cols:
            targets += [(self.row, self.col_peer(k)) for k in range(1, self.n)]
        if rows:
            targets += [(self.row_peer(d), self.col) for d in OFFSETS]
        barrier = pltpu.get_barrier_semaphore()
        for t in targets:
            pl.semaphore_signal(barrier, 1, device_id=t, device_id_type=MESH)
        pl.semaphore_wait(barrier, len(targets))


def _copy(src_ref, dst_ref, send, recv, device):
    return pltpu.make_async_remote_copy(
        src_ref=src_ref,
        dst_ref=dst_ref,
        send_sem=send,
        recv_sem=recv,
        device_id=device,
        device_id_type=MESH,
    )


def _rows_of(ref, index, chunk):
    return ref.at[:, pl.ds(pl.multiple_of(index * chunk, chunk), chunk), :]


def _start_all(copies):
    for c in copies:
        c.start()
    return copies


def _wait_sends(copies):
    for c in copies:
        c.wait_send()


def scatter_start(p, x_ref, got, send, recv):
    chunk = got.shape[2]
    out = []
    for k in _send_order(p.n):
        peer = p.col_peer(k)
        out.append(
            _copy(_rows_of(x_ref, peer, chunk), got.at[p.col], send.at[peer], recv.at[p.col], (p.row, peer))
        )
    return _start_all(out)


def scatter_finish(p, x_ref, got, send, recv):
    chunk = got.shape[2]
    acc = _rows_of(x_ref, p.col, chunk)[...]
    for k in range(1, p.n):
        src = p.col_peer(p.n - k)
        _copy(_rows_of(x_ref, src, chunk), got.at[src], send.at[src], recv.at[src], (p.row, src)).wait_recv()
        acc = acc + got[src]
    return acc


def gather_start(p, y_ref, got, send, recv):
    out = []
    for k in _send_order(p.n):
        peer = p.col_peer(k)
        out.append(_copy(y_ref, got.at[p.col], send.at[peer], recv.at[p.col], (p.row, peer)))
    return _start_all(out)


def gather_finish(p, y_ref, got, send, recv, full_ref):
    chunk = got.shape[2]
    _rows_of(full_ref, p.col, chunk)[...] = y_ref[...]
    for k in range(1, p.n):
        src = p.col_peer(p.n - k)
        _copy(y_ref, got.at[src], send.at[src], recv.at[src], (p.row, src)).wait_recv()
        _rows_of(full_ref, src, chunk)[...] = got[src]


def _lane_block(ref, b):
    return ref.at[:, :, pl.ds(b * 128, 128)]


def tri_gather_start(p, d_ref, got, send, recv):
    share = d_ref.shape[1]
    blocks = d_ref.shape[2] // 128
    out = []
    for b in range(blocks):
        copies = [
            _copy(_lane_block(d_ref, b), _lane_block(got.at[p.col], b), send.at[b, p.col_peer(k)],
                  recv.at[b, p.col], (p.row, p.col_peer(k)))
            for k in _send_order(p.n)
        ]
        out.append((b, copies))

        @pl.when((p.col + 1) * share > b * 128)
        def _():
            for c in copies:
                c.start()
    return out


def tri_gather_finish(p, d_ref, got, send, recv, full_ref):
    share = d_ref.shape[1]
    blocks = d_ref.shape[2] // 128
    _rows_of(full_ref, p.col, share)[...] = d_ref[...]
    for k in range(1, p.n):
        src = p.col_peer(p.n - k)
        rows = pl.ds(pl.multiple_of(src * share, share), share)
        for b in range(blocks):
            lanes = pl.ds(b * 128, 128)

            @pl.when((src + 1) * share > b * 128)
            def _():
                _copy(_lane_block(d_ref, b), _lane_block(got.at[src], b), send.at[b, src], recv.at[b, src],
                      (p.row, src)).wait_recv()
                full_ref[:, rows, lanes] = got[src, :, :, lanes]

            @pl.when((src + 1) * share <= b * 128)
            def _():
                full_ref[:, rows, lanes] = jnp.zeros(full_ref.shape[:1] + (share, 128), jnp.float32)


def tri_wait_sends(p, share, started):
    for b, copies in started:

        @pl.when((p.col + 1) * share > b * 128)
        def _():
            for c in copies:
                c.wait_send()


def bcast_start(p, v_ref, got, send, recv):
    out = []
    for d in SEND_OFFSETS:
        out.append(_copy(v_ref, got.at[KDEV - d], send.at[KDEV + d], recv.at[KDEV - d], (p.row_peer(d), p.col)))
    return _start_all(out)


def bcast_finish(p, v_ref, got, send, recv, win_ref):
    win_ref[KDEV] = v_ref[...]
    for o in OFFSETS:
        w = KDEV + o
        _copy(v_ref, got.at[w], send.at[w], recv.at[w], (p.row_peer(o), p.col)).wait_recv()
        win_ref[w] = got[w]


def spread_start(p, x_ref, got, send, recv):
    out = []
    for d in SEND_OFFSETS:
        out.append(
            _copy(x_ref.at[KDEV + d], got.at[KDEV - d], send.at[KDEV + d], recv.at[KDEV - d], (p.row_peer(d), p.col))
        )
    return _start_all(out)


def spread_finish(p, x_ref, got, send, recv):
    acc = x_ref[KDEV]
    for o in OFFSETS:
        w = KDEV + o
        _copy(x_ref.at[w], got.at[w], send.at[w], recv.at[w], (p.row_peer(o), p.col)).wait_recv()
        acc = acc + got[w]
    return acc


def _gather_kernel(n, count, y_ref, full_ref, got, s, r):
    p = Place(n, count)
    p.barrier(True, False)
    sends = gather_start(p, y_ref, got, s, r)
    gather_finish(p, y_ref, got, s, r, full_ref)
    _wait_sends(sends)


def _scatter_kernel(n, count, x_ref, own_ref, got, s, r):
    p = Place(n, count)
    p.barrier(True, False)
    sends = scatter_start(p, x_ref, got, s, r)
    own_ref[...] = scatter_finish(p, x_ref, got, s, r)
    _wait_sends(sends)


def _bcast_gather_kernel(n, count, v_ref, d_ref, win_ref, dfull_ref, got_w, sw, rw, got_d, sd, rd):
    p = Place(n, count)
    p.barrier(True, True)
    sends = bcast_start(p, v_ref, got_w, sw, rw) + gather_start(p, d_ref, got_d, sd, rd)
    bcast_finish(p, v_ref, got_w, sw, rw, win_ref)
    gather_finish(p, d_ref, got_d, sd, rd, dfull_ref)
    _wait_sends(sends)


def _scatter_bcast_gather_kernel(
    n, count, x_ref, d_ref, own_ref, win_ref, dfull_ref, got_x, sx, rx, got_w, sw, rw, got_d, sd, rd
):
    p = Place(n, count)
    p.barrier(True, True)
    sends = scatter_start(p, x_ref, got_x, sx, rx)
    own_ref[...] = scatter_finish(p, x_ref, got_x, sx, rx)
    sends += bcast_start(p, own_ref, got_w, sw, rw) + gather_start(p, d_ref, got_d, sd, rd)
    bcast_finish(p, own_ref, got_w, sw, rw, win_ref)
    gather_finish(p, d_ref, got_d, sd, rd, dfull_ref)
    _wait_sends(sends)


def _scatter_gather_kernel(n, count, x_ref, own_ref, full_ref, got_x, sx, rx, got_y, sy, ry):
    p = Place(n, count)
    p.barrier(True, False)
    sends = scatter_start(p, x_ref, got_x, sx, rx)
    own_ref[...] = scatter_finish(p, x_ref, got_x, sx, rx)
    sends += gather_start(p, own_ref, got_y, sy, ry)
    gather_finish(p, own_ref, got_y, sy, ry, full_ref)
    _wait_sends(sends)


def _spread_gather_kernel(n, count, x_ref, f_ref, sum_ref, full_ref, got_b, sb, rb, res, got_y, sy, ry):
    p = Place(n, count)
    p.barrier(True, True)
    sends = spread_start(p, x_ref, got_b, sb, rb)
    acc = spread_finish(p, x_ref, got_b, sb, rb)
    sum_ref[...] = acc
    res[...] = f_ref[...] - acc[acc.shape[0] - 1]
    sends += gather_start(p, res, got_y, sy, ry)
    gather_finish(p, res, got_y, sy, ry, full_ref)
    _wait_sends(sends)


def _spread_kernel(n, count, x_ref, sum_ref, got_b, sb, rb):
    p = Place(n, count)
    p.barrier(False, True)
    sends = spread_start(p, x_ref, got_b, sb, rb)
    sum_ref[...] = spread_finish(p, x_ref, got_b, sb, rb)
    _wait_sends(sends)


def _dots(a_ref, b_ref, transpose_a=False):
    outs = []
    for s in range(a_ref.shape[0]):
        a = a_ref[s]
        if transpose_a:
            a = a.T
        outs.append(jnp.dot(a, b_ref[s], precision=lax.Precision.HIGHEST, preferred_element_type=jnp.float32))
    return jnp.stack(outs, 0)


def _first_kernel(n, count, rhs_ref, dinv_ref, fv_ref, win_ref, dfull_ref, got_y, sy, ry, whole, got_w, sw, rw, got_d, sd, rd):
    y_ref, d0_ref, d1_ref = rhs_ref.at[0], dinv_ref.at[0], dinv_ref.at[1]
    p = Place(n, count)
    p.barrier(True, True)
    sends = gather_start(p, y_ref, got_y, sy, ry)
    gather_finish(p, y_ref, got_y, sy, ry, whole)
    fv_ref[...] = _dots(d0_ref, whole)
    sends += bcast_start(p, fv_ref, got_w, sw, rw) + gather_start(p, d1_ref, got_d, sd, rd)
    bcast_finish(p, fv_ref, got_w, sw, rw, win_ref)
    gather_finish(p, d1_ref, got_d, sd, rd, dfull_ref)
    _wait_sends(sends)


def _level1_kernel(
    n, count, share_ref, dw_ref, dinv_ref, own_ref, win_ref, dfull_ref, x_ref, got_x, sx, rx, got_w, sw, rw, got_d, sd, rd
):
    d_ref = dinv_ref.at[2]
    p = Place(n, count)
    p.barrier(True, True)
    x_ref[...] = _dots(dw_ref, share_ref)
    sends = scatter_start(p, x_ref, got_x, sx, rx)
    own_ref[...] = scatter_finish(p, x_ref, got_x, sx, rx)
    sends += bcast_start(p, own_ref, got_w, sw, rw) + gather_start(p, d_ref, got_d, sd, rd)
    bcast_finish(p, own_ref, got_w, sw, rw, win_ref)
    gather_finish(p, d_ref, got_d, sd, rd, dfull_ref)
    _wait_sends(sends)


def _level2_kernel(n, count, share_ref, dw_ref, own_ref, sol_ref, mine_ref, x_ref, got_x, sx, rx, full, got_y, sy, ry):
    p = Place(n, count)
    p.barrier(True, False)
    x_ref[...] = _dots(dw_ref, share_ref)
    sends = scatter_start(p, x_ref, got_x, sx, rx)
    own_ref[...] = scatter_finish(p, x_ref, got_x, sx, rx)
    sends += gather_start(p, own_ref, got_y, sy, ry)
    gather_finish(p, own_ref, got_y, sy, ry, full)
    sol_ref[...] = _dots(dw_ref, full, transpose_a=True)
    mine_ref[...] = _rows_of(sol_ref, p.col, mine_ref.shape[1])[...]
    _wait_sends(sends)


def _back2_kernel(n, count, x_ref, f_ref, dw_ref, sum_ref, sol_ref, mine_ref, got_b, sb, rb, res, full, got_y, sy, ry):
    p = Place(n, count)
    p.barrier(True, True)
    sends = spread_start(p, x_ref, got_b, sb, rb)
    acc = spread_finish(p, x_ref, got_b, sb, rb)
    sum_ref[...] = acc
    res[...] = f_ref[...] - acc[acc.shape[0] - 1]
    sends += gather_start(p, res, got_y, sy, ry)
    gather_finish(p, res, got_y, sy, ry, full)
    sol_ref[...] = _dots(dw_ref, full, transpose_a=True)
    mine_ref[...] = _rows_of(sol_ref, p.col, mine_ref.shape[1])[...]
    _wait_sends(sends)


def _last_kernel(n, count, res_ref, d0_ref, own_ref, x_ref, got, s, r):
    p = Place(n, count)
    p.barrier(True, False)
    x_ref[...] = _dots(d0_ref, res_ref, transpose_a=True)
    sends = scatter_start(p, x_ref, got, s, r)
    own_ref[...] = scatter_finish(p, x_ref, got, s, r)
    _wait_sends(sends)


def _final_kernel(n, count, x_ref, f_ref, dinv_ref, own_ref, got_b, sb, rb, x2_ref, got, s, r):
    d0_ref = dinv_ref.at[0]
    p = Place(n, count)
    p.barrier(True, True)
    sends = spread_start(p, x_ref, got_b, sb, rb)
    acc = spread_finish(p, x_ref, got_b, sb, rb)
    res = f_ref[...] - acc[0]
    outs = []
    for q in range(d0_ref.shape[0]):
        outs.append(
            jnp.dot(d0_ref[q].T, res[q], precision=lax.Precision.HIGHEST, preferred_element_type=jnp.float32)
        )
    x2_ref[...] = jnp.stack(outs, 0)
    sends += scatter_start(p, x2_ref, got, s, r)
    own_ref[...] = scatter_finish(p, x2_ref, got, s, r)
    _wait_sends(sends)


def _mm(a, b):
    return jnp.dot(a, b, precision=lax.Precision.HIGHEST, preferred_element_type=jnp.float32)


def _smem():
    return pl.BlockSpec(memory_space=pltpu.SMEM)


def _share(p, wins, t_ref, table, base, slots, rhs_ref, out_ref):
    owned, share, r = rhs_ref.shape
    mine = pl.ds(pl.multiple_of(p.col * share, share), share)
    size = owned * slots
    for s in range(owned):
        pieces = []
        for k in range(slots):
            at = base + s * slots + k
            w = table[at + size]
            q = table[at + 2 * size]
            v = wins[0][w, q]
            if len(wins) > 1:
                v = jnp.where(table[at] == 0, v, wins[1][w, q])
            pieces.append(jnp.where(table[at + 3 * size] != 0, v, 0.0))
        picked = jnp.concatenate(pieces, axis=0)
        out_ref[s] = -_mm(t_ref[s].T, picked)
        out_ref[s, mine, :] = rhs_ref[s] + out_ref[s, mine, :]


def _terms(t_ref, sol_ref, terms_ref):
    owned, slots, share, r = terms_ref.shape
    for s in range(owned):
        full = _mm(t_ref[s], sol_ref[s])
        for k in range(slots):
            terms_ref[s, k] = full[k * share : (k + 1) * share]


def _route(bucket_ref, level, table, parts):
    slots, owned, share, r = bucket_ref.shape
    for w in range(slots):
        for q in range(owned):
            m = (level * slots + w) * owned + q
            acc = None
            for terms_ref, base in parts:
                count = terms_ref.shape[0]
                for s in range(count):
                    at = base + 2 * (m * count + s)
                    v = jnp.where(table[at + 1] != 0, terms_ref[s, table[at]], 0.0)
                    acc = v if acc is None else acc + v
            bucket_ref[w, q] = acc


def _forward_kernel(
    n, count,
    rhs_ref, dinv_ref, ft_ref, table,
    out_ref,
    fv0_ref, fv1_ref, sol2_ref, d1_ref, d2_ref,
    got_y, sy, ry, whole, win0, got_w0, sw0, rw0, got_d1, sd1, rd1, got_d2, sd2, rd2,
    share1, x1, got_x1, sx1, rx1, win1, got_w1, sw1, rw1,
    share2, x2, got_x2, sx2, rx2, fv2, full2, got_y2, sy2, ry2,
    terms2, bucket1, got_b1, sb1, rb1, res1, got_z1, sz1, rz1, full1, sol1,
    terms1, bucket0, got_b0, sb0, rb0, x0, got_x0, sx0, rx0,
):
    t1_ref, t2_ref = ft_ref.at[0], ft_ref.at[1]
    owned = rhs_ref.shape[1]
    slots = terms1.shape[1]
    size = owned * slots
    lookup1 = 8 * size
    lookup2 = lookup1 + (2 * KDEV + 1) * owned * owned * 2
    p = Place(n, count)
    p.barrier(True, True)
    sends = gather_start(p, rhs_ref.at[0], got_y, sy, ry)
    gather_finish(p, rhs_ref.at[0], got_y, sy, ry, whole)
    fv0_ref[...] = _dots(dinv_ref.at[0], whole)
    sends += bcast_start(p, fv0_ref, got_w0, sw0, rw0)
    tri = [tri_gather_start(p, dinv_ref.at[1], got_d1, sd1, rd1), tri_gather_start(p, dinv_ref.at[2], got_d2, sd2, rd2)]
    bcast_finish(p, fv0_ref, got_w0, sw0, rw0, win0)
    tri_gather_finish(p, dinv_ref.at[1], got_d1, sd1, rd1, d1_ref)
    _share(p, [win0], t1_ref, table, 0, slots, rhs_ref.at[1], share1)
    x1[...] = _dots(d1_ref, share1)
    sends += scatter_start(p, x1, got_x1, sx1, rx1)
    fv1_ref[...] = scatter_finish(p, x1, got_x1, sx1, rx1)
    sends += bcast_start(p, fv1_ref, got_w1, sw1, rw1)
    bcast_finish(p, fv1_ref, got_w1, sw1, rw1, win1)
    tri_gather_finish(p, dinv_ref.at[2], got_d2, sd2, rd2, d2_ref)
    _share(p, [win0, win1], t2_ref, table, 4 * size, slots, rhs_ref.at[2], share2)
    x2[...] = _dots(d2_ref, share2)
    sends += scatter_start(p, x2, got_x2, sx2, rx2)
    fv2[...] = scatter_finish(p, x2, got_x2, sx2, rx2)
    sends += gather_start(p, fv2, got_y2, sy2, ry2)
    gather_finish(p, fv2, got_y2, sy2, ry2, full2)
    sol2_ref[...] = _dots(d2_ref, full2, transpose_a=True)
    share = fv2.shape[1]
    out_ref[2] = _rows_of(sol2_ref, p.col, share)[...]
    _terms(t2_ref, sol2_ref, terms2)
    _route(bucket1, 1, table, [(terms2, lookup2)])
    sends += spread_start(p, bucket1, got_b1, sb1, rb1)
    res1[...] = fv1_ref[...] - spread_finish(p, bucket1, got_b1, sb1, rb1)
    sends += gather_start(p, res1, got_z1, sz1, rz1)
    gather_finish(p, res1, got_z1, sz1, rz1, full1)
    sol1[...] = _dots(d1_ref, full1, transpose_a=True)
    out_ref[1] = _rows_of(sol1, p.col, share)[...]
    _terms(t1_ref, sol1, terms1)
    _route(bucket0, 0, table, [(terms2, lookup2), (terms1, lookup1)])
    sends += spread_start(p, bucket0, got_b0, sb0, rb0)
    res0 = fv0_ref[...] - spread_finish(p, bucket0, got_b0, sb0, rb0)
    d0 = dinv_ref.at[0]
    x0[...] = jnp.stack([_mm(d0[q].T, res0[q]) for q in range(res0.shape[0])], 0)
    sends += scatter_start(p, x0, got_x0, sx0, rx0)
    out_ref[0] = scatter_finish(p, x0, got_x0, sx0, rx0)
    _wait_sends(sends)
    for started in tri:
        tri_wait_sends(p, share, started)


def _f32(shape):
    return jax.ShapeDtypeStruct(shape, jnp.float32)


def _dma(k):
    return [pltpu.SemaphoreType.DMA((k,)), pltpu.SemaphoreType.DMA((k,))]


def _call(body, n, count, cid, args, outs, scratch):
    return pl.pallas_call(
        functools.partial(body, n, count),
        out_shape=tuple(_f32(o) for o in outs),
        in_specs=[_vmem() for a in args],
        out_specs=tuple(_vmem() for o in outs),
        scratch_shapes=scratch,
        compiler_params=_params(cid),
    )(*args)


def local(rhs, diag_inv, factor_tiles, tile_source, tile_count):
    levels = rhs.shape[0]
    owned_count = rhs.shape[1]
    share_rows = rhs.shape[2]
    columns = rhs.shape[3]
    slot_count = tile_source.shape[2]
    reach_dev = KDEV
    window_len = 2 * reach_dev + 1
    n = lax.axis_size("cols")
    count = lax.axis_size("rows")
    total_sup = count * owned_count
    row_place = lax.axis_index("rows")
    my_rows = lax.axis_index("cols") * share_rows
    highest = lax.Precision.HIGHEST
    slot_ids = jnp.arange(slot_count, dtype=jnp.int32)
    assert levels == 3 and count >= window_len
    blk = (owned_count, share_rows, columns)
    whole = (owned_count, n * share_rows, columns)
    dblk = diag_inv.shape[1:]
    dwhole = (owned_count, n * share_rows, diag_inv.shape[3])
    win = (window_len,) + blk
    slots = window_len

    def window_places(sources):
        src_level = sources // total_sup
        within = sources % total_sup
        return (
            src_level * window_len + within // owned_count - row_place + reach_dev
        ) * owned_count + within % owned_count

    def live_mask(counts):
        return (slot_ids[None, :] < counts[:, None]).astype(jnp.float32)

    def own_rows(block):
        return lax.dynamic_slice_in_dim(block, my_rows, share_rows, axis=1)

    def forward_share(height, windows):
        stacked = jnp.stack(windows, 0).reshape(height * window_len * owned_count, share_rows, columns)
        places = window_places(tile_source[height - 1])
        picked = jnp.take(stacked, places, axis=0) * live_mask(tile_count[height - 1])[:, :, None, None]
        partial_value = jnp.einsum(
            "skci,skcr->sir", factor_tiles[height - 1], picked, precision=highest
        )
        return lax.dynamic_update_slice_in_dim(
            -partial_value, rhs[height] - own_rows(partial_value), my_rows, axis=1
        )

    def buckets(height, whole_block):
        term_set = jnp.einsum(
            "skci,sir->skcr", factor_tiles[height - 1], whole_block, precision=highest
        )
        term_set = term_set * live_mask(tile_count[height - 1])[:, :, None, None]
        places = window_places(tile_source[height - 1]).reshape(-1)
        targets = height * window_len * owned_count
        one_hot = (jnp.arange(targets, dtype=jnp.int32)[:, None] == places[None, :]).astype(
            jnp.float32
        )
        outgoing = jnp.einsum(
            "ms,slg->mlg",
            one_hot,
            term_set.reshape(owned_count * slot_count, share_rows, columns),
            precision=highest,
        )
        push_outgoing = outgoing.reshape(height, window_len, owned_count, share_rows, columns)
        return push_outgoing.transpose(1, 0, 2, 3, 4)

    def vm(shape):
        return pltpu.VMEM(shape, jnp.float32)

    def source_tables(height):
        sources = tile_source[height - 1]
        src_level = jnp.clip(sources // total_sup, 0, height - 1)
        within = sources % total_sup
        slot = jnp.clip(within // owned_count - row_place + reach_dev, 0, window_len - 1)
        live = (tile_count[height - 1][:, None] > slot_ids[None, :]).astype(jnp.int32)
        return [src_level, slot, within % owned_count, live]

    def flat_tiles(height):
        t = factor_tiles[height - 1]
        return t.reshape(t.shape[0], t.shape[1] * t.shape[2], t.shape[3])

    def lookup(height):
        places = window_places(tile_source[height - 1])
        live = tile_count[height - 1][:, None] > slot_ids[None, :]
        targets = height * window_len * owned_count
        match = (places[None, :, :] == jnp.arange(targets, dtype=jnp.int32)[:, None, None]) & live[None]
        pick = jnp.sum(match.astype(jnp.int32) * slot_ids[None, None, :], axis=-1)
        return [jnp.stack([pick, jnp.any(match, axis=-1).astype(jnp.int32)], -1)]

    nblk = (n,) + blk
    lane_blocks = diag_inv.shape[3] // 128
    tri_dma = [pltpu.SemaphoreType.DMA((lane_blocks, n)), pltpu.SemaphoreType.DMA((lane_blocks, n))]
    tiles = (owned_count, slot_count, share_rows, columns)
    args = (
        [rhs, diag_inv, factor_tiles.reshape(factor_tiles.shape[:2] + (slot_count * share_rows, -1))]
        + [jnp.concatenate([t.reshape(-1) for t in source_tables(1) + source_tables(2) + lookup(1) + lookup(2)])]
    )
    outs = pl.pallas_call(
        functools.partial(_forward_kernel, n, count),
        out_shape=tuple(_f32(o) for o in [rhs.shape, blk, blk, whole, dwhole, dwhole]),
        in_specs=[_vmem()] * 3 + [_smem()],
        out_specs=tuple(_vmem() for o in range(6)),
        scratch_shapes=[vm(nblk)] + _dma(n) + [vm(whole)]
        + [vm(win), vm(win)] + _dma(slots)
        + [vm((n,) + dblk)] + tri_dma + [vm((n,) + dblk)] + tri_dma
        + [vm(whole), vm(whole), vm(nblk)] + _dma(n)
        + [vm(win), vm(win)] + _dma(slots)
        + [vm(whole), vm(whole), vm(nblk)] + _dma(n)
        + [vm(blk), vm(whole), vm(nblk)] + _dma(n)
        + [vm(tiles), vm(win), vm(win)] + _dma(slots) + [vm(blk), vm(nblk)] + _dma(n) + [vm(whole), vm(whole)]
        + [vm(tiles), vm(win), vm(win)] + _dma(slots) + [vm(whole), vm(nblk)] + _dma(n),
        compiler_params=_params(0),
    )(*args)
    return outs[0]


def solution(mesh):
    placed = (
        P(None, "rows", "cols", None),
        P(None, "rows", "cols", None),
        P(None, "rows", None, "cols", None),
        P(None, "rows", None),
        P(None, "rows"),
    )
    return jax.shard_map(
        local, mesh=mesh, in_specs=placed, out_specs=P(None, "rows", "cols", None), check_vma=False
    )
```

```python
import functools

import jax
import jax.numpy as jnp
from jax import lax
from jax.experimental import pallas as pl
from jax.experimental.pallas import tpu as pltpu
from jax.sharding import PartitionSpec as P

KDEV = 7
MESH = pl.DeviceIdType.MESH
OFFSETS = [d for d in range(-KDEV, KDEV + 1) if d != 0]
SEND_OFFSETS = sorted(OFFSETS, key=lambda d: (-abs(d), d))


def _send_order(n):
    return sorted(range(1, n), key=lambda k: (-min(k, n - k), k))


def _params(cid):
    return pltpu.CompilerParams(collective_id=cid, has_side_effects=True)


def _vmem():
    return pl.BlockSpec(memory_space=pltpu.VMEM)


class Place:
    def __init__(self, n, count):
        self.n = n
        self.count = count
        self.col = lax.axis_index("cols")
        self.row = lax.axis_index("rows")

    def col_peer(self, k):
        return lax.rem(self.col + k, self.n)

    def row_peer(self, d):
        return lax.rem(self.row + d + self.count, self.count)

    def barrier(self, cols, rows):
        targets = []
        if cols:
            targets += [(self.row, self.col_peer(k)) for k in range(1, self.n)]
        if rows:
            targets += [(self.row_peer(d), self.col) for d in OFFSETS]
        barrier = pltpu.get_barrier_semaphore()
        for t in targets:
            pl.semaphore_signal(barrier, 1, device_id=t, device_id_type=MESH)
        pl.semaphore_wait(barrier, len(targets))


def _copy(src_ref, dst_ref, send, recv, device):
    return pltpu.make_async_remote_copy(
        src_ref=src_ref,
        dst_ref=dst_ref,
        send_sem=send,
        recv_sem=recv,
        device_id=device,
        device_id_type=MESH,
    )


def _rows_of(ref, index, chunk):
    return ref.at[:, pl.ds(pl.multiple_of(index * chunk, chunk), chunk), :]


def _start_all(copies):
    for c in copies:
        c.start()
    return copies


def _wait_sends(copies):
    for c in copies:
        c.wait_send()


def scatter_start(p, x_ref, got, send, recv):
    chunk = got.shape[2]
    out = []
    for k in _send_order(p.n):
        peer = p.col_peer(k)
        out.append(
            _copy(_rows_of(x_ref, peer, chunk), got.at[p.col], send.at[peer], recv.at[p.col], (p.row, peer))
        )
    return _start_all(out)


def scatter_finish(p, x_ref, got, send, recv):
    chunk = got.shape[2]
    acc = _rows_of(x_ref, p.col, chunk)[...]
    for k in range(1, p.n):
        src = p.col_peer(p.n - k)
        _copy(_rows_of(x_ref, src, chunk), got.at[src], send.at[src], recv.at[src], (p.row, src)).wait_recv()
        acc = acc + got[src]
    return acc


def gather_start(p, y_ref, got, send, recv):
    out = []
    for k in _send_order(p.n):
        peer = p.col_peer(k)
        out.append(_copy(y_ref, got.at[p.col], send.at[peer], recv.at[p.col], (p.row, peer)))
    return _start_all(out)


def gather_finish(p, y_ref, got, send, recv, full_ref):
    chunk = got.shape[2]
    _rows_of(full_ref, p.col, chunk)[...] = y_ref[...]
    for k in range(1, p.n):
        src = p.col_peer(p.n - k)
        _copy(y_ref, got.at[src], send.at[src], recv.at[src], (p.row, src)).wait_recv()
        _rows_of(full_ref, src, chunk)[...] = got[src]


def _when_start(cond, copy):
    pl.when(cond)(copy.start)
    return (cond, copy)


def _wait_sends_when(pairs):
    for cond, copy in pairs:
        pl.when(cond)(copy.wait_send)


def lower_gather_start(p, y_ref, got, send, recv):
    out = []
    for k in _send_order(p.n):
        peer = p.col_peer(k)
        out.append(_when_start(peer > p.col, _copy(y_ref, got.at[p.col], send.at[peer], recv.at[p.col], (p.row, peer))))
    return out


def lower_gather_finish(p, y_ref, got, send, recv, full_ref):
    chunk = got.shape[2]
    _rows_of(full_ref, p.col, chunk)[...] = y_ref[...]
    for k in range(1, p.n):
        src = p.col_peer(p.n - k)
        rows = _rows_of(full_ref, src, chunk)

        @pl.when(src < p.col)
        def _():
            _copy(y_ref, got.at[src], send.at[src], recv.at[src], (p.row, src)).wait_recv()
            rows[...] = got[src]

        @pl.when(src > p.col)
        def _():
            rows[...] = jnp.zeros(y_ref.shape, jnp.float32)


def upper_scatter_start(p, x_ref, got, send, recv):
    chunk = got.shape[2]
    out = []
    for k in _send_order(p.n):
        peer = p.col_peer(k)
        out.append(_when_start(
            peer < p.col,
            _copy(_rows_of(x_ref, peer, chunk), got.at[p.col], send.at[peer], recv.at[p.col], (p.row, peer)),
        ))
    return out


def upper_scatter_finish(p, x_ref, got, send, recv, acc_ref):
    chunk = got.shape[2]
    acc_ref[...] = _rows_of(x_ref, p.col, chunk)[...]
    for k in range(1, p.n):
        src = p.col_peer(p.n - k)

        @pl.when(src > p.col)
        def _():
            _copy(_rows_of(x_ref, src, chunk), got.at[src], send.at[src], recv.at[src], (p.row, src)).wait_recv()
            acc_ref[...] = acc_ref[...] + got[src]


def bcast_start(p, v_ref, got, send, recv):
    out = []
    for d in SEND_OFFSETS:
        out.append(_copy(v_ref, got.at[KDEV - d], send.at[KDEV + d], recv.at[KDEV - d], (p.row_peer(d), p.col)))
    return _start_all(out)


def bcast_finish(p, v_ref, got, send, recv, win_ref):
    win_ref[KDEV] = v_ref[...]
    for o in OFFSETS:
        w = KDEV + o
        _copy(v_ref, got.at[w], send.at[w], recv.at[w], (p.row_peer(o), p.col)).wait_recv()
        win_ref[w] = got[w]


def spread_start(p, x_ref, got, send, recv):
    out = []
    for d in SEND_OFFSETS:
        out.append(
            _copy(x_ref.at[KDEV + d], got.at[KDEV - d], send.at[KDEV + d], recv.at[KDEV - d], (p.row_peer(d), p.col))
        )
    return _start_all(out)


def spread_finish(p, x_ref, got, send, recv):
    acc = x_ref[KDEV]
    for o in OFFSETS:
        w = KDEV + o
        _copy(x_ref.at[w], got.at[w], send.at[w], recv.at[w], (p.row_peer(o), p.col)).wait_recv()
        acc = acc + got[w]
    return acc


def _gather_kernel(n, count, y_ref, full_ref, got, s, r):
    p = Place(n, count)
    p.barrier(True, False)
    sends = gather_start(p, y_ref, got, s, r)
    gather_finish(p, y_ref, got, s, r, full_ref)
    _wait_sends(sends)


def _scatter_kernel(n, count, x_ref, own_ref, got, s, r):
    p = Place(n, count)
    p.barrier(True, False)
    sends = scatter_start(p, x_ref, got, s, r)
    own_ref[...] = scatter_finish(p, x_ref, got, s, r)
    _wait_sends(sends)


def _bcast_gather_kernel(n, count, v_ref, d_ref, win_ref, dfull_ref, got_w, sw, rw, got_d, sd, rd):
    p = Place(n, count)
    p.barrier(True, True)
    sends = bcast_start(p, v_ref, got_w, sw, rw) + gather_start(p, d_ref, got_d, sd, rd)
    bcast_finish(p, v_ref, got_w, sw, rw, win_ref)
    gather_finish(p, d_ref, got_d, sd, rd, dfull_ref)
    _wait_sends(sends)


def _scatter_bcast_gather_kernel(
    n, count, x_ref, d_ref, own_ref, win_ref, dfull_ref, got_x, sx, rx, got_w, sw, rw, got_d, sd, rd
):
    p = Place(n, count)
    p.barrier(True, True)
    sends = scatter_start(p, x_ref, got_x, sx, rx)
    own_ref[...] = scatter_finish(p, x_ref, got_x, sx, rx)
    sends += bcast_start(p, own_ref, got_w, sw, rw) + gather_start(p, d_ref, got_d, sd, rd)
    bcast_finish(p, own_ref, got_w, sw, rw, win_ref)
    gather_finish(p, d_ref, got_d, sd, rd, dfull_ref)
    _wait_sends(sends)


def _scatter_gather_kernel(n, count, x_ref, own_ref, full_ref, got_x, sx, rx, got_y, sy, ry):
    p = Place(n, count)
    p.barrier(True, False)
    sends = scatter_start(p, x_ref, got_x, sx, rx)
    own_ref[...] = scatter_finish(p, x_ref, got_x, sx, rx)
    sends += gather_start(p, own_ref, got_y, sy, ry)
    gather_finish(p, own_ref, got_y, sy, ry, full_ref)
    _wait_sends(sends)


def _spread_gather_kernel(n, count, x_ref, f_ref, sum_ref, full_ref, got_b, sb, rb, res, got_y, sy, ry):
    p = Place(n, count)
    p.barrier(True, True)
    sends = spread_start(p, x_ref, got_b, sb, rb)
    acc = spread_finish(p, x_ref, got_b, sb, rb)
    sum_ref[...] = acc
    res[...] = f_ref[...] - acc[acc.shape[0] - 1]
    sends += gather_start(p, res, got_y, sy, ry)
    gather_finish(p, res, got_y, sy, ry, full_ref)
    _wait_sends(sends)


def _spread_kernel(n, count, x_ref, sum_ref, got_b, sb, rb):
    p = Place(n, count)
    p.barrier(False, True)
    sends = spread_start(p, x_ref, got_b, sb, rb)
    sum_ref[...] = spread_finish(p, x_ref, got_b, sb, rb)
    _wait_sends(sends)


def _dots(a_ref, b_ref, transpose_a=False):
    outs = []
    for s in range(a_ref.shape[0]):
        a = a_ref[s]
        if transpose_a:
            a = a.T
        outs.append(jnp.dot(a, b_ref[s], precision=lax.Precision.HIGHEST, preferred_element_type=jnp.float32))
    return jnp.stack(outs, 0)


def _first_kernel(n, count, rhs_ref, dinv_ref, fv_ref, win_ref, dfull_ref, got_y, sy, ry, whole, got_w, sw, rw, got_d, sd, rd):
    y_ref, d0_ref, d1_ref = rhs_ref.at[0], dinv_ref.at[0], dinv_ref.at[1]
    p = Place(n, count)
    p.barrier(True, True)
    sends = gather_start(p, y_ref, got_y, sy, ry)
    gather_finish(p, y_ref, got_y, sy, ry, whole)
    fv_ref[...] = _dots(d0_ref, whole)
    sends += bcast_start(p, fv_ref, got_w, sw, rw) + gather_start(p, d1_ref, got_d, sd, rd)
    bcast_finish(p, fv_ref, got_w, sw, rw, win_ref)
    gather_finish(p, d1_ref, got_d, sd, rd, dfull_ref)
    _wait_sends(sends)


def _level1_kernel(
    n, count, share_ref, dw_ref, dinv_ref, own_ref, win_ref, dfull_ref, x_ref, got_x, sx, rx, got_w, sw, rw, got_d, sd, rd
):
    d_ref = dinv_ref.at[2]
    p = Place(n, count)
    p.barrier(True, True)
    x_ref[...] = _dots(dw_ref, share_ref)
    sends = scatter_start(p, x_ref, got_x, sx, rx)
    own_ref[...] = scatter_finish(p, x_ref, got_x, sx, rx)
    sends += bcast_start(p, own_ref, got_w, sw, rw) + gather_start(p, d_ref, got_d, sd, rd)
    bcast_finish(p, own_ref, got_w, sw, rw, win_ref)
    gather_finish(p, d_ref, got_d, sd, rd, dfull_ref)
    _wait_sends(sends)


def _level2_kernel(n, count, share_ref, dw_ref, own_ref, sol_ref, mine_ref, x_ref, got_x, sx, rx, full, got_y, sy, ry):
    p = Place(n, count)
    p.barrier(True, False)
    x_ref[...] = _dots(dw_ref, share_ref)
    sends = scatter_start(p, x_ref, got_x, sx, rx)
    own_ref[...] = scatter_finish(p, x_ref, got_x, sx, rx)
    sends += gather_start(p, own_ref, got_y, sy, ry)
    gather_finish(p, own_ref, got_y, sy, ry, full)
    sol_ref[...] = _dots(dw_ref, full, transpose_a=True)
    mine_ref[...] = _rows_of(sol_ref, p.col, mine_ref.shape[1])[...]
    _wait_sends(sends)


def _back2_kernel(n, count, x_ref, f_ref, dw_ref, sum_ref, sol_ref, mine_ref, got_b, sb, rb, res, full, got_y, sy, ry):
    p = Place(n, count)
    p.barrier(True, True)
    sends = spread_start(p, x_ref, got_b, sb, rb)
    acc = spread_finish(p, x_ref, got_b, sb, rb)
    sum_ref[...] = acc
    res[...] = f_ref[...] - acc[acc.shape[0] - 1]
    sends += gather_start(p, res, got_y, sy, ry)
    gather_finish(p, res, got_y, sy, ry, full)
    sol_ref[...] = _dots(dw_ref, full, transpose_a=True)
    mine_ref[...] = _rows_of(sol_ref, p.col, mine_ref.shape[1])[...]
    _wait_sends(sends)


def _last_kernel(n, count, res_ref, d0_ref, own_ref, x_ref, got, s, r):
    p = Place(n, count)
    p.barrier(True, False)
    x_ref[...] = _dots(d0_ref, res_ref, transpose_a=True)
    sends = scatter_start(p, x_ref, got, s, r)
    own_ref[...] = scatter_finish(p, x_ref, got, s, r)
    _wait_sends(sends)


def _final_kernel(n, count, x_ref, f_ref, dinv_ref, own_ref, got_b, sb, rb, x2_ref, got, s, r):
    d0_ref = dinv_ref.at[0]
    p = Place(n, count)
    p.barrier(True, True)
    sends = spread_start(p, x_ref, got_b, sb, rb)
    acc = spread_finish(p, x_ref, got_b, sb, rb)
    res = f_ref[...] - acc[0]
    outs = []
    for q in range(d0_ref.shape[0]):
        outs.append(
            jnp.dot(d0_ref[q].T, res[q], precision=lax.Precision.HIGHEST, preferred_element_type=jnp.float32)
        )
    x2_ref[...] = jnp.stack(outs, 0)
    sends += scatter_start(p, x2_ref, got, s, r)
    own_ref[...] = scatter_finish(p, x2_ref, got, s, r)
    _wait_sends(sends)


def _mm(a, b):
    return jnp.dot(a, b, precision=lax.Precision.HIGHEST, preferred_element_type=jnp.float32)


def _smem():
    return pl.BlockSpec(memory_space=pltpu.SMEM)


def _share(p, wins, t_ref, table, base, slots, rhs_ref, out_ref):
    owned, share, r = rhs_ref.shape
    mine = pl.ds(pl.multiple_of(p.col * share, share), share)
    size = owned * slots
    for s in range(owned):
        pieces = []
        for k in range(slots):
            at = base + s * slots + k
            w = table[at + size]
            q = table[at + 2 * size]
            v = wins[0][w, q]
            if len(wins) > 1:
                v = jnp.where(table[at] == 0, v, wins[1][w, q])
            pieces.append(jnp.where(table[at + 3 * size] != 0, v, 0.0))
        picked = jnp.concatenate(pieces, axis=0)
        out_ref[s] = -_mm(t_ref[s].T, picked)
        out_ref[s, mine, :] = rhs_ref[s] + out_ref[s, mine, :]


def _terms(t_ref, sol_ref, terms_ref):
    owned, slots, share, r = terms_ref.shape
    for s in range(owned):
        full = _mm(t_ref[s], sol_ref[s])
        for k in range(slots):
            terms_ref[s, k] = full[k * share : (k + 1) * share]


def _route(bucket_ref, level, table, parts):
    slots, owned, share, r = bucket_ref.shape
    for w in range(slots):
        for q in range(owned):
            m = (level * slots + w) * owned + q
            acc = None
            for terms_ref, base in parts:
                count = terms_ref.shape[0]
                for s in range(count):
                    at = base + 2 * (m * count + s)
                    v = jnp.where(table[at + 1] != 0, terms_ref[s, table[at]], 0.0)
                    acc = v if acc is None else acc + v
            bucket_ref[w, q] = acc


def _forward_kernel(
    n, count,
    rhs_ref, dinv_ref, ft_ref, table,
    out_ref,
    fv0_ref, fv1_ref, sol2_ref, d1_ref, d2_ref,
    got_y, sy, ry, whole, win0, got_w0, sw0, rw0, got_d1, sd1, rd1, got_d2, sd2, rd2,
    share1, x1, got_x1, sx1, rx1, win1, got_w1, sw1, rw1,
    share2, x2, got_x2, sx2, rx2, fv2, full2, got_y2, sy2, ry2,
    terms2, bucket1, got_b1, sb1, rb1, res1, got_z1, sz1, rz1, full1, sol1,
    terms1, bucket0, got_b0, sb0, rb0, x0, got_x0, sx0, rx0,
):
    t1_ref, t2_ref = ft_ref.at[0], ft_ref.at[1]
    owned = rhs_ref.shape[1]
    slots = terms1.shape[1]
    size = owned * slots
    lookup1 = 8 * size
    lookup2 = lookup1 + (2 * KDEV + 1) * owned * owned * 2
    p = Place(n, count)
    p.barrier(True, True)
    lower = lower_gather_start(p, rhs_ref.at[0], got_y, sy, ry)
    lower_gather_finish(p, rhs_ref.at[0], got_y, sy, ry, whole)
    sends = []
    fv0_ref[...] = _dots(dinv_ref.at[0], whole)
    sends += bcast_start(p, fv0_ref, got_w0, sw0, rw0)
    sends += gather_start(p, dinv_ref.at[1], got_d1, sd1, rd1) + gather_start(p, dinv_ref.at[2], got_d2, sd2, rd2)
    bcast_finish(p, fv0_ref, got_w0, sw0, rw0, win0)
    gather_finish(p, dinv_ref.at[1], got_d1, sd1, rd1, d1_ref)
    _share(p, [win0], t1_ref, table, 0, slots, rhs_ref.at[1], share1)
    x1[...] = _dots(d1_ref, share1)
    sends += scatter_start(p, x1, got_x1, sx1, rx1)
    fv1_ref[...] = scatter_finish(p, x1, got_x1, sx1, rx1)
    sends += bcast_start(p, fv1_ref, got_w1, sw1, rw1)
    bcast_finish(p, fv1_ref, got_w1, sw1, rw1, win1)
    gather_finish(p, dinv_ref.at[2], got_d2, sd2, rd2, d2_ref)
    _share(p, [win0, win1], t2_ref, table, 4 * size, slots, rhs_ref.at[2], share2)
    x2[...] = _dots(d2_ref, share2)
    sends += scatter_start(p, x2, got_x2, sx2, rx2)
    fv2[...] = scatter_finish(p, x2, got_x2, sx2, rx2)
    sends += gather_start(p, fv2, got_y2, sy2, ry2)
    gather_finish(p, fv2, got_y2, sy2, ry2, full2)
    sol2_ref[...] = _dots(d2_ref, full2, transpose_a=True)
    share = fv2.shape[1]
    out_ref[2] = _rows_of(sol2_ref, p.col, share)[...]
    _terms(t2_ref, sol2_ref, terms2)
    _route(bucket1, 1, table, [(terms2, lookup2)])
    sends += spread_start(p, bucket1, got_b1, sb1, rb1)
    res1[...] = fv1_ref[...] - spread_finish(p, bucket1, got_b1, sb1, rb1)
    sends += gather_start(p, res1, got_z1, sz1, rz1)
    gather_finish(p, res1, got_z1, sz1, rz1, full1)
    sol1[...] = _dots(d1_ref, full1, transpose_a=True)
    out_ref[1] = _rows_of(sol1, p.col, share)[...]
    _terms(t1_ref, sol1, terms1)
    _route(bucket0, 0, table, [(terms2, lookup2), (terms1, lookup1)])
    sends += spread_start(p, bucket0, got_b0, sb0, rb0)
    res0 = fv0_ref[...] - spread_finish(p, bucket0, got_b0, sb0, rb0)
    d0 = dinv_ref.at[0]
    x0[...] = jnp.stack([_mm(d0[q].T, res0[q]) for q in range(res0.shape[0])], 0)
    upper = upper_scatter_start(p, x0, got_x0, sx0, rx0)
    upper_scatter_finish(p, x0, got_x0, sx0, rx0, out_ref.at[0])
    _wait_sends(sends)
    _wait_sends_when(lower + upper)


def _f32(shape):
    return jax.ShapeDtypeStruct(shape, jnp.float32)


def _dma(k):
    return [pltpu.SemaphoreType.DMA((k,)), pltpu.SemaphoreType.DMA((k,))]


def _call(body, n, count, cid, args, outs, scratch):
    return pl.pallas_call(
        functools.partial(body, n, count),
        out_shape=tuple(_f32(o) for o in outs),
        in_specs=[_vmem() for a in args],
        out_specs=tuple(_vmem() for o in outs),
        scratch_shapes=scratch,
        compiler_params=_params(cid),
    )(*args)


def local(rhs, diag_inv, factor_tiles, tile_source, tile_count):
    levels = rhs.shape[0]
    owned_count = rhs.shape[1]
    share_rows = rhs.shape[2]
    columns = rhs.shape[3]
    slot_count = tile_source.shape[2]
    reach_dev = KDEV
    window_len = 2 * reach_dev + 1
    n = lax.axis_size("cols")
    count = lax.axis_size("rows")
    total_sup = count * owned_count
    row_place = lax.axis_index("rows")
    my_rows = lax.axis_index("cols") * share_rows
    highest = lax.Precision.HIGHEST
    slot_ids = jnp.arange(slot_count, dtype=jnp.int32)
    assert levels == 3 and count >= window_len
    blk = (owned_count, share_rows, columns)
    whole = (owned_count, n * share_rows, columns)
    dblk = diag_inv.shape[1:]
    dwhole = (owned_count, n * share_rows, diag_inv.shape[3])
    win = (window_len,) + blk
    slots = window_len

    def window_places(sources):
        src_level = sources // total_sup
        within = sources % total_sup
        return (
            src_level * window_len + within // owned_count - row_place + reach_dev
        ) * owned_count + within % owned_count

    def live_mask(counts):
        return (slot_ids[None, :] < counts[:, None]).astype(jnp.float32)

    def own_rows(block):
        return lax.dynamic_slice_in_dim(block, my_rows, share_rows, axis=1)

    def forward_share(height, windows):
        stacked = jnp.stack(windows, 0).reshape(height * window_len * owned_count, share_rows, columns)
        places = window_places(tile_source[height - 1])
        picked = jnp.take(stacked, places, axis=0) * live_mask(tile_count[height - 1])[:, :, None, None]
        partial_value = jnp.einsum(
            "skci,skcr->sir", factor_tiles[height - 1], picked, precision=highest
        )
        return lax.dynamic_update_slice_in_dim(
            -partial_value, rhs[height] - own_rows(partial_value), my_rows, axis=1
        )

    def buckets(height, whole_block):
        term_set = jnp.einsum(
            "skci,sir->skcr", factor_tiles[height - 1], whole_block, precision=highest
        )
        term_set = term_set * live_mask(tile_count[height - 1])[:, :, None, None]
        places = window_places(tile_source[height - 1]).reshape(-1)
        targets = height * window_len * owned_count
        one_hot = (jnp.arange(targets, dtype=jnp.int32)[:, None] == places[None, :]).astype(
            jnp.float32
        )
        outgoing = jnp.einsum(
            "ms,slg->mlg",
            one_hot,
            term_set.reshape(owned_count * slot_count, share_rows, columns),
            precision=highest,
        )
        push_outgoing = outgoing.reshape(height, window_len, owned_count, share_rows, columns)
        return push_outgoing.transpose(1, 0, 2, 3, 4)

    def vm(shape):
        return pltpu.VMEM(shape, jnp.float32)

    def source_tables(height):
        sources = tile_source[height - 1]
        src_level = jnp.clip(sources // total_sup, 0, height - 1)
        within = sources % total_sup
        slot = jnp.clip(within // owned_count - row_place + reach_dev, 0, window_len - 1)
        live = (tile_count[height - 1][:, None] > slot_ids[None, :]).astype(jnp.int32)
        return [src_level, slot, within % owned_count, live]

    def flat_tiles(height):
        t = factor_tiles[height - 1]
        return t.reshape(t.shape[0], t.shape[1] * t.shape[2], t.shape[3])

    def lookup(height):
        places = window_places(tile_source[height - 1])
        live = tile_count[height - 1][:, None] > slot_ids[None, :]
        targets = height * window_len * owned_count
        match = (places[None, :, :] == jnp.arange(targets, dtype=jnp.int32)[:, None, None]) & live[None]
        pick = jnp.sum(match.astype(jnp.int32) * slot_ids[None, None, :], axis=-1)
        return [jnp.stack([pick, jnp.any(match, axis=-1).astype(jnp.int32)], -1)]

    nblk = (n,) + blk
    tiles = (owned_count, slot_count, share_rows, columns)
    args = (
        [rhs, diag_inv, factor_tiles.reshape(factor_tiles.shape[:2] + (slot_count * share_rows, -1))]
        + [jnp.concatenate([t.reshape(-1) for t in source_tables(1) + source_tables(2) + lookup(1) + lookup(2)])]
    )
    outs = pl.pallas_call(
        functools.partial(_forward_kernel, n, count),
        out_shape=tuple(_f32(o) for o in [rhs.shape, blk, blk, whole, dwhole, dwhole]),
        in_specs=[_vmem()] * 3 + [_smem()],
        out_specs=tuple(_vmem() for o in range(6)),
        scratch_shapes=[vm(nblk)] + _dma(n) + [vm(whole)]
        + [vm(win), vm(win)] + _dma(slots)
        + [vm((n,) + dblk)] + _dma(n) + [vm((n,) + dblk)] + _dma(n)
        + [vm(whole), vm(whole), vm(nblk)] + _dma(n)
        + [vm(win), vm(win)] + _dma(slots)
        + [vm(whole), vm(whole), vm(nblk)] + _dma(n)
        + [vm(blk), vm(whole), vm(nblk)] + _dma(n)
        + [vm(tiles), vm(win), vm(win)] + _dma(slots) + [vm(blk), vm(nblk)] + _dma(n) + [vm(whole), vm(whole)]
        + [vm(tiles), vm(win), vm(win)] + _dma(slots) + [vm(whole), vm(nblk)] + _dma(n),
        compiler_params=_params(0),
    )(*args)
    return outs[0]


def solution(mesh):
    placed = (
        P(None, "rows", "cols", None),
        P(None, "rows", "cols", None),
        P(None, "rows", None, "cols", None),
        P(None, "rows", None),
        P(None, "rows"),
    )
    return jax.shard_map(
        local, mesh=mesh, in_specs=placed, out_specs=P(None, "rows", "cols", None), check_vma=False
    )
```

```python
import functools

import jax
import jax.numpy as jnp
from jax import lax
from jax.experimental import pallas as pl
from jax.experimental.pallas import tpu as pltpu
from jax.sharding import PartitionSpec as P

KDEV = 7
MESH = pl.DeviceIdType.MESH
OFFSETS = [d for d in range(-KDEV, KDEV + 1) if d != 0]
SEND_OFFSETS = sorted(OFFSETS, key=lambda d: (-abs(d), d))


WAIT_OFFSETS = sorted(OFFSETS, key=lambda d: (abs(d), d))


def _wait_order(n):
    return sorted(range(1, n), key=lambda k: (min(k, n - k), k))


def _send_order(n):
    return sorted(range(1, n), key=lambda k: (-min(k, n - k), k))


def _params(cid):
    return pltpu.CompilerParams(collective_id=cid, has_side_effects=True)


def _vmem():
    return pl.BlockSpec(memory_space=pltpu.VMEM)


class Place:
    def __init__(self, n, count):
        self.n = n
        self.count = count
        self.col = lax.axis_index("cols")
        self.row = lax.axis_index("rows")

    def col_peer(self, k):
        return lax.rem(self.col + k, self.n)

    def row_peer(self, d):
        return lax.rem(self.row + d + self.count, self.count)

    def barrier(self, cols, rows):
        targets = []
        if cols:
            targets += [(self.row, self.col_peer(k)) for k in range(1, self.n)]
        if rows:
            targets += [(self.row_peer(d), self.col) for d in OFFSETS]
        barrier = pltpu.get_barrier_semaphore()
        for t in targets:
            pl.semaphore_signal(barrier, 1, device_id=t, device_id_type=MESH)
        pl.semaphore_wait(barrier, len(targets))


def _copy(src_ref, dst_ref, send, recv, device):
    return pltpu.make_async_remote_copy(
        src_ref=src_ref,
        dst_ref=dst_ref,
        send_sem=send,
        recv_sem=recv,
        device_id=device,
        device_id_type=MESH,
    )


def _rows_of(ref, index, chunk):
    return ref.at[:, pl.ds(pl.multiple_of(index * chunk, chunk), chunk), :]


def _start_all(copies):
    for c in copies:
        c.start()
    return copies


def _wait_sends(copies):
    for c in copies:
        c.wait_send()


def scatter_start(p, x_ref, got, send, recv):
    chunk = got.shape[2]
    out = []
    for k in _send_order(p.n):
        peer = p.col_peer(k)
        out.append(
            _copy(_rows_of(x_ref, peer, chunk), got.at[p.col], send.at[peer], recv.at[p.col], (p.row, peer))
        )
    return _start_all(out)


def scatter_finish(p, x_ref, got, send, recv):
    chunk = got.shape[2]
    acc = _rows_of(x_ref, p.col, chunk)[...]
    for k in _wait_order(p.n):
        src = p.col_peer(p.n - k)
        _copy(_rows_of(x_ref, src, chunk), got.at[src], send.at[src], recv.at[src], (p.row, src)).wait_recv()
        acc = acc + got[src]
    return acc


def gather_start(p, y_ref, got, send, recv):
    out = []
    for k in _send_order(p.n):
        peer = p.col_peer(k)
        out.append(_copy(y_ref, got.at[p.col], send.at[peer], recv.at[p.col], (p.row, peer)))
    return _start_all(out)


def gather_finish(p, y_ref, got, send, recv, full_ref):
    chunk = got.shape[2]
    _rows_of(full_ref, p.col, chunk)[...] = y_ref[...]
    for k in _wait_order(p.n):
        src = p.col_peer(p.n - k)
        _copy(y_ref, got.at[src], send.at[src], recv.at[src], (p.row, src)).wait_recv()
        _rows_of(full_ref, src, chunk)[...] = got[src]


def bcast_start(p, v_ref, got, send, recv):
    out = []
    for d in SEND_OFFSETS:
        out.append(_copy(v_ref, got.at[KDEV - d], send.at[KDEV + d], recv.at[KDEV - d], (p.row_peer(d), p.col)))
    return _start_all(out)


def bcast_finish(p, v_ref, got, send, recv, win_ref):
    win_ref[KDEV] = v_ref[...]
    for o in WAIT_OFFSETS:
        w = KDEV + o
        _copy(v_ref, got.at[w], send.at[w], recv.at[w], (p.row_peer(o), p.col)).wait_recv()
        win_ref[w] = got[w]


def spread_start(p, x_ref, got, send, recv):
    out = []
    for d in SEND_OFFSETS:
        out.append(
            _copy(x_ref.at[KDEV + d], got.at[KDEV - d], send.at[KDEV + d], recv.at[KDEV - d], (p.row_peer(d), p.col))
        )
    return _start_all(out)


def spread_finish(p, x_ref, got, send, recv):
    acc = x_ref[KDEV]
    for o in WAIT_OFFSETS:
        w = KDEV + o
        _copy(x_ref.at[w], got.at[w], send.at[w], recv.at[w], (p.row_peer(o), p.col)).wait_recv()
        acc = acc + got[w]
    return acc


def _gather_kernel(n, count, y_ref, full_ref, got, s, r):
    p = Place(n, count)
    p.barrier(True, False)
    sends = gather_start(p, y_ref, got, s, r)
    gather_finish(p, y_ref, got, s, r, full_ref)
    _wait_sends(sends)


def _scatter_kernel(n, count, x_ref, own_ref, got, s, r):
    p = Place(n, count)
    p.barrier(True, False)
    sends = scatter_start(p, x_ref, got, s, r)
    own_ref[...] = scatter_finish(p, x_ref, got, s, r)
    _wait_sends(sends)


def _bcast_gather_kernel(n, count, v_ref, d_ref, win_ref, dfull_ref, got_w, sw, rw, got_d, sd, rd):
    p = Place(n, count)
    p.barrier(True, True)
    sends = bcast_start(p, v_ref, got_w, sw, rw) + gather_start(p, d_ref, got_d, sd, rd)
    bcast_finish(p, v_ref, got_w, sw, rw, win_ref)
    gather_finish(p, d_ref, got_d, sd, rd, dfull_ref)
    _wait_sends(sends)


def _scatter_bcast_gather_kernel(
    n, count, x_ref, d_ref, own_ref, win_ref, dfull_ref, got_x, sx, rx, got_w, sw, rw, got_d, sd, rd
):
    p = Place(n, count)
    p.barrier(True, True)
    sends = scatter_start(p, x_ref, got_x, sx, rx)
    own_ref[...] = scatter_finish(p, x_ref, got_x, sx, rx)
    sends += bcast_start(p, own_ref, got_w, sw, rw) + gather_start(p, d_ref, got_d, sd, rd)
    bcast_finish(p, own_ref, got_w, sw, rw, win_ref)
    gather_finish(p, d_ref, got_d, sd, rd, dfull_ref)
    _wait_sends(sends)


def _scatter_gather_kernel(n, count, x_ref, own_ref, full_ref, got_x, sx, rx, got_y, sy, ry):
    p = Place(n, count)
    p.barrier(True, False)
    sends = scatter_start(p, x_ref, got_x, sx, rx)
    own_ref[...] = scatter_finish(p, x_ref, got_x, sx, rx)
    sends += gather_start(p, own_ref, got_y, sy, ry)
    gather_finish(p, own_ref, got_y, sy, ry, full_ref)
    _wait_sends(sends)


def _spread_gather_kernel(n, count, x_ref, f_ref, sum_ref, full_ref, got_b, sb, rb, res, got_y, sy, ry):
    p = Place(n, count)
    p.barrier(True, True)
    sends = spread_start(p, x_ref, got_b, sb, rb)
    acc = spread_finish(p, x_ref, got_b, sb, rb)
    sum_ref[...] = acc
    res[...] = f_ref[...] - acc[acc.shape[0] - 1]
    sends += gather_start(p, res, got_y, sy, ry)
    gather_finish(p, res, got_y, sy, ry, full_ref)
    _wait_sends(sends)


def _spread_kernel(n, count, x_ref, sum_ref, got_b, sb, rb):
    p = Place(n, count)
    p.barrier(False, True)
    sends = spread_start(p, x_ref, got_b, sb, rb)
    sum_ref[...] = spread_finish(p, x_ref, got_b, sb, rb)
    _wait_sends(sends)


def _dots(a_ref, b_ref, transpose_a=False):
    outs = []
    for s in range(a_ref.shape[0]):
        a = a_ref[s]
        if transpose_a:
            a = a.T
        outs.append(jnp.dot(a, b_ref[s], precision=lax.Precision.HIGHEST, preferred_element_type=jnp.float32))
    return jnp.stack(outs, 0)


def _first_kernel(n, count, rhs_ref, dinv_ref, fv_ref, win_ref, dfull_ref, got_y, sy, ry, whole, got_w, sw, rw, got_d, sd, rd):
    y_ref, d0_ref, d1_ref = rhs_ref.at[0], dinv_ref.at[0], dinv_ref.at[1]
    p = Place(n, count)
    p.barrier(True, True)
    sends = gather_start(p, y_ref, got_y, sy, ry)
    gather_finish(p, y_ref, got_y, sy, ry, whole)
    fv_ref[...] = _dots(d0_ref, whole)
    sends += bcast_start(p, fv_ref, got_w, sw, rw) + gather_start(p, d1_ref, got_d, sd, rd)
    bcast_finish(p, fv_ref, got_w, sw, rw, win_ref)
    gather_finish(p, d1_ref, got_d, sd, rd, dfull_ref)
    _wait_sends(sends)


def _level1_kernel(
    n, count, share_ref, dw_ref, dinv_ref, own_ref, win_ref, dfull_ref, x_ref, got_x, sx, rx, got_w, sw, rw, got_d, sd, rd
):
    d_ref = dinv_ref.at[2]
    p = Place(n, count)
    p.barrier(True, True)
    x_ref[...] = _dots(dw_ref, share_ref)
    sends = scatter_start(p, x_ref, got_x, sx, rx)
    own_ref[...] = scatter_finish(p, x_ref, got_x, sx, rx)
    sends += bcast_start(p, own_ref, got_w, sw, rw) + gather_start(p, d_ref, got_d, sd, rd)
    bcast_finish(p, own_ref, got_w, sw, rw, win_ref)
    gather_finish(p, d_ref, got_d, sd, rd, dfull_ref)
    _wait_sends(sends)


def _level2_kernel(n, count, share_ref, dw_ref, own_ref, sol_ref, mine_ref, x_ref, got_x, sx, rx, full, got_y, sy, ry):
    p = Place(n, count)
    p.barrier(True, False)
    x_ref[...] = _dots(dw_ref, share_ref)
    sends = scatter_start(p, x_ref, got_x, sx, rx)
    own_ref[...] = scatter_finish(p, x_ref, got_x, sx, rx)
    sends += gather_start(p, own_ref, got_y, sy, ry)
    gather_finish(p, own_ref, got_y, sy, ry, full)
    sol_ref[...] = _dots(dw_ref, full, transpose_a=True)
    mine_ref[...] = _rows_of(sol_ref, p.col, mine_ref.shape[1])[...]
    _wait_sends(sends)


def _back2_kernel(n, count, x_ref, f_ref, dw_ref, sum_ref, sol_ref, mine_ref, got_b, sb, rb, res, full, got_y, sy, ry):
    p = Place(n, count)
    p.barrier(True, True)
    sends = spread_start(p, x_ref, got_b, sb, rb)
    acc = spread_finish(p, x_ref, got_b, sb, rb)
    sum_ref[...] = acc
    res[...] = f_ref[...] - acc[acc.shape[0] - 1]
    sends += gather_start(p, res, got_y, sy, ry)
    gather_finish(p, res, got_y, sy, ry, full)
    sol_ref[...] = _dots(dw_ref, full, transpose_a=True)
    mine_ref[...] = _rows_of(sol_ref, p.col, mine_ref.shape[1])[...]
    _wait_sends(sends)


def _last_kernel(n, count, res_ref, d0_ref, own_ref, x_ref, got, s, r):
    p = Place(n, count)
    p.barrier(True, False)
    x_ref[...] = _dots(d0_ref, res_ref, transpose_a=True)
    sends = scatter_start(p, x_ref, got, s, r)
    own_ref[...] = scatter_finish(p, x_ref, got, s, r)
    _wait_sends(sends)


def _final_kernel(n, count, x_ref, f_ref, dinv_ref, own_ref, got_b, sb, rb, x2_ref, got, s, r):
    d0_ref = dinv_ref.at[0]
    p = Place(n, count)
    p.barrier(True, True)
    sends = spread_start(p, x_ref, got_b, sb, rb)
    acc = spread_finish(p, x_ref, got_b, sb, rb)
    res = f_ref[...] - acc[0]
    outs = []
    for q in range(d0_ref.shape[0]):
        outs.append(
            jnp.dot(d0_ref[q].T, res[q], precision=lax.Precision.HIGHEST, preferred_element_type=jnp.float32)
        )
    x2_ref[...] = jnp.stack(outs, 0)
    sends += scatter_start(p, x2_ref, got, s, r)
    own_ref[...] = scatter_finish(p, x2_ref, got, s, r)
    _wait_sends(sends)


def _mm(a, b):
    return jnp.dot(a, b, precision=lax.Precision.HIGHEST, preferred_element_type=jnp.float32)


def _smem():
    return pl.BlockSpec(memory_space=pltpu.SMEM)


def _share(p, wins, t_ref, table, base, slots, rhs_ref, out_ref):
    owned, share, r = rhs_ref.shape
    mine = pl.ds(pl.multiple_of(p.col * share, share), share)
    size = owned * slots
    for s in range(owned):
        pieces = []
        for k in range(slots):
            at = base + s * slots + k
            w = table[at + size]
            q = table[at + 2 * size]
            v = wins[0][w, q]
            if len(wins) > 1:
                v = jnp.where(table[at] == 0, v, wins[1][w, q])
            pieces.append(jnp.where(table[at + 3 * size] != 0, v, 0.0))
        picked = jnp.concatenate(pieces, axis=0)
        out_ref[s] = -_mm(t_ref[s].T, picked)
        out_ref[s, mine, :] = rhs_ref[s] + out_ref[s, mine, :]


def _terms(t_ref, sol_ref, terms_ref):
    owned, slots, share, r = terms_ref.shape
    for s in range(owned):
        full = _mm(t_ref[s], sol_ref[s])
        for k in range(slots):
            terms_ref[s, k] = full[k * share : (k + 1) * share]


def _route(bucket_ref, level, table, parts):
    slots, owned, share, r = bucket_ref.shape
    for w in range(slots):
        for q in range(owned):
            m = (level * slots + w) * owned + q
            acc = None
            for terms_ref, base in parts:
                count = terms_ref.shape[0]
                for s in range(count):
                    at = base + 2 * (m * count + s)
                    v = jnp.where(table[at + 1] != 0, terms_ref[s, table[at]], 0.0)
                    acc = v if acc is None else acc + v
            bucket_ref[w, q] = acc


def _forward_kernel(
    n, count,
    rhs_ref, dinv_ref, ft_ref, table,
    out_ref,
    fv0_ref, fv1_ref, sol2_ref, d1_ref, d2_ref,
    got_y, sy, ry, whole, win0, got_w0, sw0, rw0, got_d1, sd1, rd1, got_d2, sd2, rd2,
    share1, x1, got_x1, sx1, rx1, win1, got_w1, sw1, rw1,
    share2, x2, got_x2, sx2, rx2, fv2, full2, got_y2, sy2, ry2,
    terms2, bucket1, got_b1, sb1, rb1, res1, got_z1, sz1, rz1, full1, sol1,
    terms1, bucket0, got_b0, sb0, rb0, x0, got_x0, sx0, rx0,
):
    t1_ref, t2_ref = ft_ref.at[0], ft_ref.at[1]
    owned = rhs_ref.shape[1]
    slots = terms1.shape[1]
    size = owned * slots
    lookup1 = 8 * size
    lookup2 = lookup1 + (2 * KDEV + 1) * owned * owned * 2
    p = Place(n, count)
    p.barrier(True, True)
    sends = gather_start(p, rhs_ref.at[0], got_y, sy, ry)
    gather_finish(p, rhs_ref.at[0], got_y, sy, ry, whole)
    fv0_ref[...] = _dots(dinv_ref.at[0], whole)
    sends += bcast_start(p, fv0_ref, got_w0, sw0, rw0)
    sends += gather_start(p, dinv_ref.at[1], got_d1, sd1, rd1) + gather_start(p, dinv_ref.at[2], got_d2, sd2, rd2)
    bcast_finish(p, fv0_ref, got_w0, sw0, rw0, win0)
    gather_finish(p, dinv_ref.at[1], got_d1, sd1, rd1, d1_ref)
    _share(p, [win0], t1_ref, table, 0, slots, rhs_ref.at[1], share1)
    x1[...] = _dots(d1_ref, share1)
    sends += scatter_start(p, x1, got_x1, sx1, rx1)
    fv1_ref[...] = scatter_finish(p, x1, got_x1, sx1, rx1)
    sends += bcast_start(p, fv1_ref, got_w1, sw1, rw1)
    bcast_finish(p, fv1_ref, got_w1, sw1, rw1, win1)
    gather_finish(p, dinv_ref.at[2], got_d2, sd2, rd2, d2_ref)
    _share(p, [win0, win1], t2_ref, table, 4 * size, slots, rhs_ref.at[2], share2)
    x2[...] = _dots(d2_ref, share2)
    sends += scatter_start(p, x2, got_x2, sx2, rx2)
    fv2[...] = scatter_finish(p, x2, got_x2, sx2, rx2)
    sends += gather_start(p, fv2, got_y2, sy2, ry2)
    gather_finish(p, fv2, got_y2, sy2, ry2, full2)
    sol2_ref[...] = _dots(d2_ref, full2, transpose_a=True)
    share = fv2.shape[1]
    out_ref[2] = _rows_of(sol2_ref, p.col, share)[...]
    _terms(t2_ref, sol2_ref, terms2)
    _route(bucket1, 1, table, [(terms2, lookup2)])
    sends += spread_start(p, bucket1, got_b1, sb1, rb1)
    res1[...] = fv1_ref[...] - spread_finish(p, bucket1, got_b1, sb1, rb1)
    sends += gather_start(p, res1, got_z1, sz1, rz1)
    gather_finish(p, res1, got_z1, sz1, rz1, full1)
    sol1[...] = _dots(d1_ref, full1, transpose_a=True)
    out_ref[1] = _rows_of(sol1, p.col, share)[...]
    _terms(t1_ref, sol1, terms1)
    _route(bucket0, 0, table, [(terms2, lookup2), (terms1, lookup1)])
    sends += spread_start(p, bucket0, got_b0, sb0, rb0)
    res0 = fv0_ref[...] - spread_finish(p, bucket0, got_b0, sb0, rb0)
    d0 = dinv_ref.at[0]
    x0[...] = jnp.stack([_mm(d0[q].T, res0[q]) for q in range(res0.shape[0])], 0)
    sends += scatter_start(p, x0, got_x0, sx0, rx0)
    out_ref[0] = scatter_finish(p, x0, got_x0, sx0, rx0)
    _wait_sends(sends)


def _f32(shape):
    return jax.ShapeDtypeStruct(shape, jnp.float32)


def _dma(k):
    return [pltpu.SemaphoreType.DMA((k,)), pltpu.SemaphoreType.DMA((k,))]


def _call(body, n, count, cid, args, outs, scratch):
    return pl.pallas_call(
        functools.partial(body, n, count),
        out_shape=tuple(_f32(o) for o in outs),
        in_specs=[_vmem() for a in args],
        out_specs=tuple(_vmem() for o in outs),
        scratch_shapes=scratch,
        compiler_params=_params(cid),
    )(*args)


def local(rhs, diag_inv, factor_tiles, tile_source, tile_count):
    levels = rhs.shape[0]
    owned_count = rhs.shape[1]
    share_rows = rhs.shape[2]
    columns = rhs.shape[3]
    slot_count = tile_source.shape[2]
    reach_dev = KDEV
    window_len = 2 * reach_dev + 1
    n = lax.axis_size("cols")
    count = lax.axis_size("rows")
    total_sup = count * owned_count
    row_place = lax.axis_index("rows")
    my_rows = lax.axis_index("cols") * share_rows
    highest = lax.Precision.HIGHEST
    slot_ids = jnp.arange(slot_count, dtype=jnp.int32)
    assert levels == 3 and count >= window_len
    blk = (owned_count, share_rows, columns)
    whole = (owned_count, n * share_rows, columns)
    dblk = diag_inv.shape[1:]
    dwhole = (owned_count, n * share_rows, diag_inv.shape[3])
    win = (window_len,) + blk
    slots = window_len

    def window_places(sources):
        src_level = sources // total_sup
        within = sources % total_sup
        return (
            src_level * window_len + within // owned_count - row_place + reach_dev
        ) * owned_count + within % owned_count

    def live_mask(counts):
        return (slot_ids[None, :] < counts[:, None]).astype(jnp.float32)

    def own_rows(block):
        return lax.dynamic_slice_in_dim(block, my_rows, share_rows, axis=1)

    def forward_share(height, windows):
        stacked = jnp.stack(windows, 0).reshape(height * window_len * owned_count, share_rows, columns)
        places = window_places(tile_source[height - 1])
        picked = jnp.take(stacked, places, axis=0) * live_mask(tile_count[height - 1])[:, :, None, None]
        partial_value = jnp.einsum(
            "skci,skcr->sir", factor_tiles[height - 1], picked, precision=highest
        )
        return lax.dynamic_update_slice_in_dim(
            -partial_value, rhs[height] - own_rows(partial_value), my_rows, axis=1
        )

    def buckets(height, whole_block):
        term_set = jnp.einsum(
            "skci,sir->skcr", factor_tiles[height - 1], whole_block, precision=highest
        )
        term_set = term_set * live_mask(tile_count[height - 1])[:, :, None, None]
        places = window_places(tile_source[height - 1]).reshape(-1)
        targets = height * window_len * owned_count
        one_hot = (jnp.arange(targets, dtype=jnp.int32)[:, None] == places[None, :]).astype(
            jnp.float32
        )
        outgoing = jnp.einsum(
            "ms,slg->mlg",
            one_hot,
            term_set.reshape(owned_count * slot_count, share_rows, columns),
            precision=highest,
        )
        push_outgoing = outgoing.reshape(height, window_len, owned_count, share_rows, columns)
        return push_outgoing.transpose(1, 0, 2, 3, 4)

    def vm(shape):
        return pltpu.VMEM(shape, jnp.float32)

    def source_tables(height):
        sources = tile_source[height - 1]
        src_level = jnp.clip(sources // total_sup, 0, height - 1)
        within = sources % total_sup
        slot = jnp.clip(within // owned_count - row_place + reach_dev, 0, window_len - 1)
        live = (tile_count[height - 1][:, None] > slot_ids[None, :]).astype(jnp.int32)
        return [src_level, slot, within % owned_count, live]

    def flat_tiles(height):
        t = factor_tiles[height - 1]
        return t.reshape(t.shape[0], t.shape[1] * t.shape[2], t.shape[3])

    def lookup(height):
        places = window_places(tile_source[height - 1])
        live = tile_count[height - 1][:, None] > slot_ids[None, :]
        targets = height * window_len * owned_count
        match = (places[None, :, :] == jnp.arange(targets, dtype=jnp.int32)[:, None, None]) & live[None]
        pick = jnp.sum(match.astype(jnp.int32) * slot_ids[None, None, :], axis=-1)
        return [jnp.stack([pick, jnp.any(match, axis=-1).astype(jnp.int32)], -1)]

    nblk = (n,) + blk
    tiles = (owned_count, slot_count, share_rows, columns)
    args = (
        [rhs, diag_inv, factor_tiles.reshape(factor_tiles.shape[:2] + (slot_count * share_rows, -1))]
        + [jnp.concatenate([t.reshape(-1) for t in source_tables(1) + source_tables(2) + lookup(1) + lookup(2)])]
    )
    outs = pl.pallas_call(
        functools.partial(_forward_kernel, n, count),
        out_shape=tuple(_f32(o) for o in [rhs.shape, blk, blk, whole, dwhole, dwhole]),
        in_specs=[_vmem()] * 3 + [_smem()],
        out_specs=tuple(_vmem() for o in range(6)),
        scratch_shapes=[vm(nblk)] + _dma(n) + [vm(whole)]
        + [vm(win), vm(win)] + _dma(slots)
        + [vm((n,) + dblk)] + _dma(n) + [vm((n,) + dblk)] + _dma(n)
        + [vm(whole), vm(whole), vm(nblk)] + _dma(n)
        + [vm(win), vm(win)] + _dma(slots)
        + [vm(whole), vm(whole), vm(nblk)] + _dma(n)
        + [vm(blk), vm(whole), vm(nblk)] + _dma(n)
        + [vm(tiles), vm(win), vm(win)] + _dma(slots) + [vm(blk), vm(nblk)] + _dma(n) + [vm(whole), vm(whole)]
        + [vm(tiles), vm(win), vm(win)] + _dma(slots) + [vm(whole), vm(nblk)] + _dma(n),
        compiler_params=_params(0),
    )(*args)
    return outs[0]


def solution(mesh):
    placed = (
        P(None, "rows", "cols", None),
        P(None, "rows", "cols", None),
        P(None, "rows", None, "cols", None),
        P(None, "rows", None),
        P(None, "rows"),
    )
    return jax.shard_map(
        local, mesh=mesh, in_specs=placed, out_specs=P(None, "rows", "cols", None), check_vma=False
    )
```

```python
import functools

import jax
import jax.numpy as jnp
from jax import lax
from jax.experimental import pallas as pl
from jax.experimental.pallas import tpu as pltpu
from jax.sharding import PartitionSpec as P

KDEV = 7
MESH = pl.DeviceIdType.MESH
OFFSETS = [d for d in range(-KDEV, KDEV + 1) if d != 0]
SEND_OFFSETS = sorted(OFFSETS, key=lambda d: (-abs(d), d))


def _send_order(n):
    return sorted(range(1, n), key=lambda k: (-min(k, n - k), k))


def _params(cid):
    return pltpu.CompilerParams(collective_id=cid, has_side_effects=True)


def _vmem():
    return pl.BlockSpec(memory_space=pltpu.VMEM)


class Place:
    def __init__(self, n, count):
        self.n = n
        self.count = count
        self.col = lax.axis_index("cols")
        self.row = lax.axis_index("rows")

    def col_peer(self, k):
        return lax.rem(self.col + k, self.n)

    def row_peer(self, d):
        return lax.rem(self.row + d + self.count, self.count)

    def barrier(self, cols, rows):
        targets = []
        if cols:
            targets += [(self.row, self.col_peer(k)) for k in range(1, self.n)]
        if rows:
            targets += [(self.row_peer(d), self.col) for d in OFFSETS]
        barrier = pltpu.get_barrier_semaphore()
        for t in targets:
            pl.semaphore_signal(barrier, 1, device_id=t, device_id_type=MESH)
        pl.semaphore_wait(barrier, len(targets))


def _copy(src_ref, dst_ref, send, recv, device):
    return pltpu.make_async_remote_copy(
        src_ref=src_ref,
        dst_ref=dst_ref,
        send_sem=send,
        recv_sem=recv,
        device_id=device,
        device_id_type=MESH,
    )


def _rows_of(ref, index, chunk):
    return ref.at[:, pl.ds(pl.multiple_of(index * chunk, chunk), chunk), :]


def _start_all(copies):
    for c in copies:
        c.start()
    return copies


def _wait_sends(copies):
    for c in copies:
        c.wait_send()


def scatter_start(p, x_ref, got, send, recv):
    chunk = got.shape[2]
    out = []
    for k in _send_order(p.n):
        peer = p.col_peer(k)
        out.append(
            _copy(_rows_of(x_ref, peer, chunk), got.at[p.col], send.at[peer], recv.at[p.col], (p.row, peer))
        )
    return _start_all(out)


def scatter_finish(p, x_ref, got, send, recv):
    chunk = got.shape[2]
    acc = _rows_of(x_ref, p.col, chunk)[...]
    for k in range(1, p.n):
        src = p.col_peer(p.n - k)
        _copy(_rows_of(x_ref, src, chunk), got.at[src], send.at[src], recv.at[src], (p.row, src)).wait_recv()
        acc = acc + got[src]
    return acc


def gather_start(p, y_ref, got, send, recv):
    out = []
    for k in _send_order(p.n):
        peer = p.col_peer(k)
        out.append(_copy(y_ref, got.at[p.col], send.at[peer], recv.at[p.col], (p.row, peer)))
    return _start_all(out)


def gather_finish(p, y_ref, got, send, recv, full_ref):
    chunk = got.shape[2]
    _rows_of(full_ref, p.col, chunk)[...] = y_ref[...]
    for k in range(1, p.n):
        src = p.col_peer(p.n - k)
        _copy(y_ref, got.at[src], send.at[src], recv.at[src], (p.row, src)).wait_recv()
        _rows_of(full_ref, src, chunk)[...] = got[src]


def bcast_start(p, v_ref, got, send, recv):
    out = []
    for d in SEND_OFFSETS:
        out.append(_copy(v_ref, got.at[KDEV - d], send.at[KDEV + d], recv.at[KDEV - d], (p.row_peer(d), p.col)))
    return _start_all(out)


def bcast_finish(p, v_ref, got, send, recv, win_ref):
    win_ref[KDEV] = v_ref[...]
    for o in OFFSETS:
        w = KDEV + o
        _copy(v_ref, got.at[w], send.at[w], recv.at[w], (p.row_peer(o), p.col)).wait_recv()
        if win_ref is not got:
            win_ref[w] = got[w]


def spread_start(p, x_ref, got, send, recv):
    out = []
    for d in SEND_OFFSETS:
        out.append(
            _copy(x_ref.at[KDEV + d], got.at[KDEV - d], send.at[KDEV + d], recv.at[KDEV - d], (p.row_peer(d), p.col))
        )
    return _start_all(out)


def spread_finish(p, x_ref, got, send, recv):
    acc = x_ref[KDEV]
    for o in OFFSETS:
        w = KDEV + o
        _copy(x_ref.at[w], got.at[w], send.at[w], recv.at[w], (p.row_peer(o), p.col)).wait_recv()
        acc = acc + got[w]
    return acc


def _gather_kernel(n, count, y_ref, full_ref, got, s, r):
    p = Place(n, count)
    p.barrier(True, False)
    sends = gather_start(p, y_ref, got, s, r)
    gather_finish(p, y_ref, got, s, r, full_ref)
    _wait_sends(sends)


def _scatter_kernel(n, count, x_ref, own_ref, got, s, r):
    p = Place(n, count)
    p.barrier(True, False)
    sends = scatter_start(p, x_ref, got, s, r)
    own_ref[...] = scatter_finish(p, x_ref, got, s, r)
    _wait_sends(sends)


def _bcast_gather_kernel(n, count, v_ref, d_ref, win_ref, dfull_ref, got_w, sw, rw, got_d, sd, rd):
    p = Place(n, count)
    p.barrier(True, True)
    sends = bcast_start(p, v_ref, got_w, sw, rw) + gather_start(p, d_ref, got_d, sd, rd)
    bcast_finish(p, v_ref, got_w, sw, rw, win_ref)
    gather_finish(p, d_ref, got_d, sd, rd, dfull_ref)
    _wait_sends(sends)


def _scatter_bcast_gather_kernel(
    n, count, x_ref, d_ref, own_ref, win_ref, dfull_ref, got_x, sx, rx, got_w, sw, rw, got_d, sd, rd
):
    p = Place(n, count)
    p.barrier(True, True)
    sends = scatter_start(p, x_ref, got_x, sx, rx)
    own_ref[...] = scatter_finish(p, x_ref, got_x, sx, rx)
    sends += bcast_start(p, own_ref, got_w, sw, rw) + gather_start(p, d_ref, got_d, sd, rd)
    bcast_finish(p, own_ref, got_w, sw, rw, win_ref)
    gather_finish(p, d_ref, got_d, sd, rd, dfull_ref)
    _wait_sends(sends)


def _scatter_gather_kernel(n, count, x_ref, own_ref, full_ref, got_x, sx, rx, got_y, sy, ry):
    p = Place(n, count)
    p.barrier(True, False)
    sends = scatter_start(p, x_ref, got_x, sx, rx)
    own_ref[...] = scatter_finish(p, x_ref, got_x, sx, rx)
    sends += gather_start(p, own_ref, got_y, sy, ry)
    gather_finish(p, own_ref, got_y, sy, ry, full_ref)
    _wait_sends(sends)


def _spread_gather_kernel(n, count, x_ref, f_ref, sum_ref, full_ref, got_b, sb, rb, res, got_y, sy, ry):
    p = Place(n, count)
    p.barrier(True, True)
    sends = spread_start(p, x_ref, got_b, sb, rb)
    acc = spread_finish(p, x_ref, got_b, sb, rb)
    sum_ref[...] = acc
    res[...] = f_ref[...] - acc[acc.shape[0] - 1]
    sends += gather_start(p, res, got_y, sy, ry)
    gather_finish(p, res, got_y, sy, ry, full_ref)
    _wait_sends(sends)


def _spread_kernel(n, count, x_ref, sum_ref, got_b, sb, rb):
    p = Place(n, count)
    p.barrier(False, True)
    sends = spread_start(p, x_ref, got_b, sb, rb)
    sum_ref[...] = spread_finish(p, x_ref, got_b, sb, rb)
    _wait_sends(sends)


def _dots(a_ref, b_ref, transpose_a=False):
    outs = []
    for s in range(a_ref.shape[0]):
        a = a_ref[s]
        if transpose_a:
            a = a.T
        outs.append(jnp.dot(a, b_ref[s], precision=lax.Precision.HIGHEST, preferred_element_type=jnp.float32))
    return jnp.stack(outs, 0)


def _first_kernel(n, count, rhs_ref, dinv_ref, fv_ref, win_ref, dfull_ref, got_y, sy, ry, whole, got_w, sw, rw, got_d, sd, rd):
    y_ref, d0_ref, d1_ref = rhs_ref.at[0], dinv_ref.at[0], dinv_ref.at[1]
    p = Place(n, count)
    p.barrier(True, True)
    sends = gather_start(p, y_ref, got_y, sy, ry)
    gather_finish(p, y_ref, got_y, sy, ry, whole)
    fv_ref[...] = _dots(d0_ref, whole)
    sends += bcast_start(p, fv_ref, got_w, sw, rw) + gather_start(p, d1_ref, got_d, sd, rd)
    bcast_finish(p, fv_ref, got_w, sw, rw, win_ref)
    gather_finish(p, d1_ref, got_d, sd, rd, dfull_ref)
    _wait_sends(sends)


def _level1_kernel(
    n, count, share_ref, dw_ref, dinv_ref, own_ref, win_ref, dfull_ref, x_ref, got_x, sx, rx, got_w, sw, rw, got_d, sd, rd
):
    d_ref = dinv_ref.at[2]
    p = Place(n, count)
    p.barrier(True, True)
    x_ref[...] = _dots(dw_ref, share_ref)
    sends = scatter_start(p, x_ref, got_x, sx, rx)
    own_ref[...] = scatter_finish(p, x_ref, got_x, sx, rx)
    sends += bcast_start(p, own_ref, got_w, sw, rw) + gather_start(p, d_ref, got_d, sd, rd)
    bcast_finish(p, own_ref, got_w, sw, rw, win_ref)
    gather_finish(p, d_ref, got_d, sd, rd, dfull_ref)
    _wait_sends(sends)


def _level2_kernel(n, count, share_ref, dw_ref, own_ref, sol_ref, mine_ref, x_ref, got_x, sx, rx, full, got_y, sy, ry):
    p = Place(n, count)
    p.barrier(True, False)
    x_ref[...] = _dots(dw_ref, share_ref)
    sends = scatter_start(p, x_ref, got_x, sx, rx)
    own_ref[...] = scatter_finish(p, x_ref, got_x, sx, rx)
    sends += gather_start(p, own_ref, got_y, sy, ry)
    gather_finish(p, own_ref, got_y, sy, ry, full)
    sol_ref[...] = _dots(dw_ref, full, transpose_a=True)
    mine_ref[...] = _rows_of(sol_ref, p.col, mine_ref.shape[1])[...]
    _wait_sends(sends)


def _back2_kernel(n, count, x_ref, f_ref, dw_ref, sum_ref, sol_ref, mine_ref, got_b, sb, rb, res, full, got_y, sy, ry):
    p = Place(n, count)
    p.barrier(True, True)
    sends = spread_start(p, x_ref, got_b, sb, rb)
    acc = spread_finish(p, x_ref, got_b, sb, rb)
    sum_ref[...] = acc
    res[...] = f_ref[...] - acc[acc.shape[0] - 1]
    sends += gather_start(p, res, got_y, sy, ry)
    gather_finish(p, res, got_y, sy, ry, full)
    sol_ref[...] = _dots(dw_ref, full, transpose_a=True)
    mine_ref[...] = _rows_of(sol_ref, p.col, mine_ref.shape[1])[...]
    _wait_sends(sends)


def _last_kernel(n, count, res_ref, d0_ref, own_ref, x_ref, got, s, r):
    p = Place(n, count)
    p.barrier(True, False)
    x_ref[...] = _dots(d0_ref, res_ref, transpose_a=True)
    sends = scatter_start(p, x_ref, got, s, r)
    own_ref[...] = scatter_finish(p, x_ref, got, s, r)
    _wait_sends(sends)


def _final_kernel(n, count, x_ref, f_ref, dinv_ref, own_ref, got_b, sb, rb, x2_ref, got, s, r):
    d0_ref = dinv_ref.at[0]
    p = Place(n, count)
    p.barrier(True, True)
    sends = spread_start(p, x_ref, got_b, sb, rb)
    acc = spread_finish(p, x_ref, got_b, sb, rb)
    res = f_ref[...] - acc[0]
    outs = []
    for q in range(d0_ref.shape[0]):
        outs.append(
            jnp.dot(d0_ref[q].T, res[q], precision=lax.Precision.HIGHEST, preferred_element_type=jnp.float32)
        )
    x2_ref[...] = jnp.stack(outs, 0)
    sends += scatter_start(p, x2_ref, got, s, r)
    own_ref[...] = scatter_finish(p, x2_ref, got, s, r)
    _wait_sends(sends)


def _mm(a, b):
    return jnp.dot(a, b, precision=lax.Precision.HIGHEST, preferred_element_type=jnp.float32)


def _smem():
    return pl.BlockSpec(memory_space=pltpu.SMEM)


def _share(p, wins, t_ref, table, base, slots, rhs_ref, out_ref):
    owned, share, r = rhs_ref.shape
    mine = pl.ds(pl.multiple_of(p.col * share, share), share)
    size = owned * slots
    for s in range(owned):
        pieces = []
        for k in range(slots):
            at = base + s * slots + k
            w = table[at + size]
            q = table[at + 2 * size]
            v = wins[0][w, q]
            if len(wins) > 1:
                v = jnp.where(table[at] == 0, v, wins[1][w, q])
            pieces.append(jnp.where(table[at + 3 * size] != 0, v, 0.0))
        picked = jnp.concatenate(pieces, axis=0)
        out_ref[s] = -_mm(t_ref[s].T, picked)
        out_ref[s, mine, :] = rhs_ref[s] + out_ref[s, mine, :]


def _terms(t_ref, sol_ref, terms_ref):
    owned, slots, share, r = terms_ref.shape
    for s in range(owned):
        full = _mm(t_ref[s], sol_ref[s])
        for k in range(slots):
            terms_ref[s, k] = full[k * share : (k + 1) * share]


def _route(bucket_ref, level, table, parts):
    slots, owned, share, r = bucket_ref.shape
    for w in range(slots):
        for q in range(owned):
            m = (level * slots + w) * owned + q
            acc = None
            for terms_ref, base in parts:
                count = terms_ref.shape[0]
                for s in range(count):
                    at = base + 2 * (m * count + s)
                    v = jnp.where(table[at + 1] != 0, terms_ref[s, table[at]], 0.0)
                    acc = v if acc is None else acc + v
            bucket_ref[w, q] = acc


def _forward_kernel(
    n, count,
    rhs_ref, dinv_ref, ft_ref, table,
    out_ref,
    fv0_ref, fv1_ref, sol2_ref, d1_ref, d2_ref,
    got_y, sy, ry, whole, win0, got_w0, sw0, rw0, got_d1, sd1, rd1, got_d2, sd2, rd2,
    share1, x1, got_x1, sx1, rx1, win1, got_w1, sw1, rw1,
    share2, x2, got_x2, sx2, rx2, fv2, full2, got_y2, sy2, ry2,
    terms2, bucket1, got_b1, sb1, rb1, res1, got_z1, sz1, rz1, full1, sol1,
    terms1, bucket0, got_b0, sb0, rb0, x0, got_x0, sx0, rx0,
):
    t1_ref, t2_ref = ft_ref.at[0], ft_ref.at[1]
    owned = rhs_ref.shape[1]
    slots = terms1.shape[1]
    size = owned * slots
    lookup1 = 8 * size
    lookup2 = lookup1 + (2 * KDEV + 1) * owned * owned * 2
    p = Place(n, count)
    p.barrier(True, True)
    sends = gather_start(p, rhs_ref.at[0], got_y, sy, ry)
    gather_finish(p, rhs_ref.at[0], got_y, sy, ry, whole)
    fv0_ref[...] = _dots(dinv_ref.at[0], whole)
    sends += bcast_start(p, fv0_ref, got_w0, sw0, rw0)
    sends += gather_start(p, dinv_ref.at[1], got_d1, sd1, rd1) + gather_start(p, dinv_ref.at[2], got_d2, sd2, rd2)
    bcast_finish(p, fv0_ref, got_w0, sw0, rw0, got_w0)
    gather_finish(p, dinv_ref.at[1], got_d1, sd1, rd1, d1_ref)
    _share(p, [got_w0], t1_ref, table, 0, slots, rhs_ref.at[1], share1)
    x1[...] = _dots(d1_ref, share1)
    sends += scatter_start(p, x1, got_x1, sx1, rx1)
    fv1_ref[...] = scatter_finish(p, x1, got_x1, sx1, rx1)
    sends += bcast_start(p, fv1_ref, got_w1, sw1, rw1)
    bcast_finish(p, fv1_ref, got_w1, sw1, rw1, got_w1)
    gather_finish(p, dinv_ref.at[2], got_d2, sd2, rd2, d2_ref)
    _share(p, [got_w0, got_w1], t2_ref, table, 4 * size, slots, rhs_ref.at[2], share2)
    x2[...] = _dots(d2_ref, share2)
    sends += scatter_start(p, x2, got_x2, sx2, rx2)
    fv2[...] = scatter_finish(p, x2, got_x2, sx2, rx2)
    sends += gather_start(p, fv2, got_y2, sy2, ry2)
    gather_finish(p, fv2, got_y2, sy2, ry2, full2)
    sol2_ref[...] = _dots(d2_ref, full2, transpose_a=True)
    share = fv2.shape[1]
    out_ref[2] = _rows_of(sol2_ref, p.col, share)[...]
    _terms(t2_ref, sol2_ref, terms2)
    _route(bucket1, 1, table, [(terms2, lookup2)])
    sends += spread_start(p, bucket1, got_b1, sb1, rb1)
    res1[...] = fv1_ref[...] - spread_finish(p, bucket1, got_b1, sb1, rb1)
    sends += gather_start(p, res1, got_z1, sz1, rz1)
    gather_finish(p, res1, got_z1, sz1, rz1, full1)
    sol1[...] = _dots(d1_ref, full1, transpose_a=True)
    out_ref[1] = _rows_of(sol1, p.col, share)[...]
    _terms(t1_ref, sol1, terms1)
    _route(bucket0, 0, table, [(terms2, lookup2), (terms1, lookup1)])
    sends += spread_start(p, bucket0, got_b0, sb0, rb0)
    res0 = fv0_ref[...] - spread_finish(p, bucket0, got_b0, sb0, rb0)
    d0 = dinv_ref.at[0]
    x0[...] = jnp.stack([_mm(d0[q].T, res0[q]) for q in range(res0.shape[0])], 0)
    sends += scatter_start(p, x0, got_x0, sx0, rx0)
    out_ref[0] = scatter_finish(p, x0, got_x0, sx0, rx0)
    _wait_sends(sends)


def _f32(shape):
    return jax.ShapeDtypeStruct(shape, jnp.float32)


def _dma(k):
    return [pltpu.SemaphoreType.DMA((k,)), pltpu.SemaphoreType.DMA((k,))]


def _call(body, n, count, cid, args, outs, scratch):
    return pl.pallas_call(
        functools.partial(body, n, count),
        out_shape=tuple(_f32(o) for o in outs),
        in_specs=[_vmem() for a in args],
        out_specs=tuple(_vmem() for o in outs),
        scratch_shapes=scratch,
        compiler_params=_params(cid),
    )(*args)


def local(rhs, diag_inv, factor_tiles, tile_source, tile_count):
    levels = rhs.shape[0]
    owned_count = rhs.shape[1]
    share_rows = rhs.shape[2]
    columns = rhs.shape[3]
    slot_count = tile_source.shape[2]
    reach_dev = KDEV
    window_len = 2 * reach_dev + 1
    n = lax.axis_size("cols")
    count = lax.axis_size("rows")
    total_sup = count * owned_count
    row_place = lax.axis_index("rows")
    my_rows = lax.axis_index("cols") * share_rows
    highest = lax.Precision.HIGHEST
    slot_ids = jnp.arange(slot_count, dtype=jnp.int32)
    assert levels == 3 and count >= window_len
    blk = (owned_count, share_rows, columns)
    whole = (owned_count, n * share_rows, columns)
    dblk = diag_inv.shape[1:]
    dwhole = (owned_count, n * share_rows, diag_inv.shape[3])
    win = (window_len,) + blk
    slots = window_len

    def window_places(sources):
        src_level = sources // total_sup
        within = sources % total_sup
        return (
            src_level * window_len + within // owned_count - row_place + reach_dev
        ) * owned_count + within % owned_count

    def live_mask(counts):
        return (slot_ids[None, :] < counts[:, None]).astype(jnp.float32)

    def own_rows(block):
        return lax.dynamic_slice_in_dim(block, my_rows, share_rows, axis=1)

    def forward_share(height, windows):
        stacked = jnp.stack(windows, 0).reshape(height * window_len * owned_count, share_rows, columns)
        places = window_places(tile_source[height - 1])
        picked = jnp.take(stacked, places, axis=0) * live_mask(tile_count[height - 1])[:, :, None, None]
        partial_value = jnp.einsum(
            "skci,skcr->sir", factor_tiles[height - 1], picked, precision=highest
        )
        return lax.dynamic_update_slice_in_dim(
            -partial_value, rhs[height] - own_rows(partial_value), my_rows, axis=1
        )

    def buckets(height, whole_block):
        term_set = jnp.einsum(
            "skci,sir->skcr", factor_tiles[height - 1], whole_block, precision=highest
        )
        term_set = term_set * live_mask(tile_count[height - 1])[:, :, None, None]
        places = window_places(tile_source[height - 1]).reshape(-1)
        targets = height * window_len * owned_count
        one_hot = (jnp.arange(targets, dtype=jnp.int32)[:, None] == places[None, :]).astype(
            jnp.float32
        )
        outgoing = jnp.einsum(
            "ms,slg->mlg",
            one_hot,
            term_set.reshape(owned_count * slot_count, share_rows, columns),
            precision=highest,
        )
        push_outgoing = outgoing.reshape(height, window_len, owned_count, share_rows, columns)
        return push_outgoing.transpose(1, 0, 2, 3, 4)

    def vm(shape):
        return pltpu.VMEM(shape, jnp.float32)

    def source_tables(height):
        sources = tile_source[height - 1]
        src_level = jnp.clip(sources // total_sup, 0, height - 1)
        within = sources % total_sup
        slot = jnp.clip(within // owned_count - row_place + reach_dev, 0, window_len - 1)
        live = (tile_count[height - 1][:, None] > slot_ids[None, :]).astype(jnp.int32)
        return [src_level, slot, within % owned_count, live]

    def flat_tiles(height):
        t = factor_tiles[height - 1]
        return t.reshape(t.shape[0], t.shape[1] * t.shape[2], t.shape[3])

    def lookup(height):
        places = window_places(tile_source[height - 1])
        live = tile_count[height - 1][:, None] > slot_ids[None, :]
        targets = height * window_len * owned_count
        match = (places[None, :, :] == jnp.arange(targets, dtype=jnp.int32)[:, None, None]) & live[None]
        pick = jnp.sum(match.astype(jnp.int32) * slot_ids[None, None, :], axis=-1)
        return [jnp.stack([pick, jnp.any(match, axis=-1).astype(jnp.int32)], -1)]

    nblk = (n,) + blk
    tiles = (owned_count, slot_count, share_rows, columns)
    args = (
        [rhs, diag_inv, factor_tiles.reshape(factor_tiles.shape[:2] + (slot_count * share_rows, -1))]
        + [jnp.concatenate([t.reshape(-1) for t in source_tables(1) + source_tables(2) + lookup(1) + lookup(2)])]
    )
    outs = pl.pallas_call(
        functools.partial(_forward_kernel, n, count),
        out_shape=tuple(_f32(o) for o in [rhs.shape, blk, blk, whole, dwhole, dwhole]),
        in_specs=[_vmem()] * 3 + [_smem()],
        out_specs=tuple(_vmem() for o in range(6)),
        scratch_shapes=[vm(nblk)] + _dma(n) + [vm(whole)]
        + [vm(win), vm(win)] + _dma(slots)
        + [vm((n,) + dblk)] + _dma(n) + [vm((n,) + dblk)] + _dma(n)
        + [vm(whole), vm(whole), vm(nblk)] + _dma(n)
        + [vm(win), vm(win)] + _dma(slots)
        + [vm(whole), vm(whole), vm(nblk)] + _dma(n)
        + [vm(blk), vm(whole), vm(nblk)] + _dma(n)
        + [vm(tiles), vm(win), vm(win)] + _dma(slots) + [vm(blk), vm(nblk)] + _dma(n) + [vm(whole), vm(whole)]
        + [vm(tiles), vm(win), vm(win)] + _dma(slots) + [vm(whole), vm(nblk)] + _dma(n),
        compiler_params=_params(0),
    )(*args)
    return outs[0]


def solution(mesh):
    placed = (
        P(None, "rows", "cols", None),
        P(None, "rows", "cols", None),
        P(None, "rows", None, "cols", None),
        P(None, "rows", None),
        P(None, "rows"),
    )
    return jax.shard_map(
        local, mesh=mesh, in_specs=placed, out_specs=P(None, "rows", "cols", None), check_vma=False
    )
```

```python
import functools

import jax
import jax.numpy as jnp
from jax import lax
from jax.experimental import pallas as pl
from jax.experimental.pallas import tpu as pltpu
from jax.sharding import PartitionSpec as P

KDEV = 7
MESH = pl.DeviceIdType.MESH
OFFSETS = [d for d in range(-KDEV, KDEV + 1) if d != 0]
SEND_OFFSETS = sorted(OFFSETS, key=lambda d: (-abs(d), d))


def _send_order(n):
    return sorted(range(1, n), key=lambda k: (-min(k, n - k), k))


def _params(cid):
    return pltpu.CompilerParams(collective_id=cid, has_side_effects=True)


def _vmem():
    return pl.BlockSpec(memory_space=pltpu.VMEM)


class Place:
    def __init__(self, n, count):
        self.n = n
        self.count = count
        self.col = lax.axis_index("cols")
        self.row = lax.axis_index("rows")

    def col_peer(self, k):
        return lax.rem(self.col + k, self.n)

    def row_peer(self, d):
        return lax.rem(self.row + d + self.count, self.count)

    def barrier(self, cols, rows):
        targets = []
        if cols:
            targets += [(self.row, self.col_peer(k)) for k in range(1, self.n)]
        if rows:
            targets += [(self.row_peer(d), self.col) for d in OFFSETS]
        barrier = pltpu.get_barrier_semaphore()
        for t in targets:
            pl.semaphore_signal(barrier, 1, device_id=t, device_id_type=MESH)
        pl.semaphore_wait(barrier, len(targets))


def _copy(src_ref, dst_ref, send, recv, device):
    return pltpu.make_async_remote_copy(
        src_ref=src_ref,
        dst_ref=dst_ref,
        send_sem=send,
        recv_sem=recv,
        device_id=device,
        device_id_type=MESH,
    )


def _rows_of(ref, index, chunk):
    return ref.at[:, pl.ds(pl.multiple_of(index * chunk, chunk), chunk), :]


def _start_all(copies):
    for c in copies:
        c.start()
    return copies


def _wait_sends(copies):
    for c in copies:
        c.wait_send()


def scatter_start(p, x_ref, got, send, recv):
    chunk = got.shape[2]
    out = []
    for k in _send_order(p.n):
        peer = p.col_peer(k)
        out.append(
            _copy(_rows_of(x_ref, peer, chunk), got.at[p.col], send.at[peer], recv.at[p.col], (p.row, peer))
        )
    return _start_all(out)


def scatter_finish(p, x_ref, got, send, recv):
    chunk = got.shape[2]
    acc = _rows_of(x_ref, p.col, chunk)[...]
    for k in range(1, p.n):
        src = p.col_peer(p.n - k)
        _copy(_rows_of(x_ref, src, chunk), got.at[src], send.at[src], recv.at[src], (p.row, src)).wait_recv()
        acc = acc + got[src]
    return acc


def gather_start(p, y_ref, got, send, recv):
    out = []
    for k in _send_order(p.n):
        peer = p.col_peer(k)
        out.append(_copy(y_ref, got.at[p.col], send.at[peer], recv.at[p.col], (p.row, peer)))
    return _start_all(out)


def gather_finish(p, y_ref, got, send, recv, full_ref):
    chunk = got.shape[2]
    _rows_of(full_ref, p.col, chunk)[...] = y_ref[...]
    for k in range(1, p.n):
        src = p.col_peer(p.n - k)
        _copy(y_ref, got.at[src], send.at[src], recv.at[src], (p.row, src)).wait_recv()
        _rows_of(full_ref, src, chunk)[...] = got[src]


def bcast_start(p, v_ref, got, send, recv):
    out = []
    for d in SEND_OFFSETS:
        out.append(_copy(v_ref, got.at[KDEV - d], send.at[KDEV + d], recv.at[KDEV - d], (p.row_peer(d), p.col)))
    return _start_all(out)


def bcast_finish(p, v_ref, got, send, recv, win_ref):
    win_ref[KDEV] = v_ref[...]
    for o in OFFSETS:
        w = KDEV + o
        _copy(v_ref, got.at[w], send.at[w], recv.at[w], (p.row_peer(o), p.col)).wait_recv()
        win_ref[w] = got[w]


def spread_start(p, x_ref, got, send, recv):
    out = []
    for d in SEND_OFFSETS:
        out.append(
            _copy(x_ref.at[KDEV + d], got.at[KDEV - d], send.at[KDEV + d], recv.at[KDEV - d], (p.row_peer(d), p.col))
        )
    return _start_all(out)


def spread_finish(p, x_ref, got, send, recv):
    acc = x_ref[KDEV]
    for o in OFFSETS:
        w = KDEV + o
        _copy(x_ref.at[w], got.at[w], send.at[w], recv.at[w], (p.row_peer(o), p.col)).wait_recv()
        acc = acc + got[w]
    return acc


def _gather_kernel(n, count, y_ref, full_ref, got, s, r):
    p = Place(n, count)
    p.barrier(True, False)
    sends = gather_start(p, y_ref, got, s, r)
    gather_finish(p, y_ref, got, s, r, full_ref)
    _wait_sends(sends)


def _scatter_kernel(n, count, x_ref, own_ref, got, s, r):
    p = Place(n, count)
    p.barrier(True, False)
    sends = scatter_start(p, x_ref, got, s, r)
    own_ref[...] = scatter_finish(p, x_ref, got, s, r)
    _wait_sends(sends)


def _bcast_gather_kernel(n, count, v_ref, d_ref, win_ref, dfull_ref, got_w, sw, rw, got_d, sd, rd):
    p = Place(n, count)
    p.barrier(True, True)
    sends = bcast_start(p, v_ref, got_w, sw, rw) + gather_start(p, d_ref, got_d, sd, rd)
    bcast_finish(p, v_ref, got_w, sw, rw, win_ref)
    gather_finish(p, d_ref, got_d, sd, rd, dfull_ref)
    _wait_sends(sends)


def _scatter_bcast_gather_kernel(
    n, count, x_ref, d_ref, own_ref, win_ref, dfull_ref, got_x, sx, rx, got_w, sw, rw, got_d, sd, rd
):
    p = Place(n, count)
    p.barrier(True, True)
    sends = scatter_start(p, x_ref, got_x, sx, rx)
    own_ref[...] = scatter_finish(p, x_ref, got_x, sx, rx)
    sends += bcast_start(p, own_ref, got_w, sw, rw) + gather_start(p, d_ref, got_d, sd, rd)
    bcast_finish(p, own_ref, got_w, sw, rw, win_ref)
    gather_finish(p, d_ref, got_d, sd, rd, dfull_ref)
    _wait_sends(sends)


def _scatter_gather_kernel(n, count, x_ref, own_ref, full_ref, got_x, sx, rx, got_y, sy, ry):
    p = Place(n, count)
    p.barrier(True, False)
    sends = scatter_start(p, x_ref, got_x, sx, rx)
    own_ref[...] = scatter_finish(p, x_ref, got_x, sx, rx)
    sends += gather_start(p, own_ref, got_y, sy, ry)
    gather_finish(p, own_ref, got_y, sy, ry, full_ref)
    _wait_sends(sends)


def _spread_gather_kernel(n, count, x_ref, f_ref, sum_ref, full_ref, got_b, sb, rb, res, got_y, sy, ry):
    p = Place(n, count)
    p.barrier(True, True)
    sends = spread_start(p, x_ref, got_b, sb, rb)
    acc = spread_finish(p, x_ref, got_b, sb, rb)
    sum_ref[...] = acc
    res[...] = f_ref[...] - acc[acc.shape[0] - 1]
    sends += gather_start(p, res, got_y, sy, ry)
    gather_finish(p, res, got_y, sy, ry, full_ref)
    _wait_sends(sends)


def _spread_kernel(n, count, x_ref, sum_ref, got_b, sb, rb):
    p = Place(n, count)
    p.barrier(False, True)
    sends = spread_start(p, x_ref, got_b, sb, rb)
    sum_ref[...] = spread_finish(p, x_ref, got_b, sb, rb)
    _wait_sends(sends)


def _dots(a_ref, b_ref, transpose_a=False):
    outs = []
    for s in range(a_ref.shape[0]):
        a = a_ref[s]
        if transpose_a:
            a = a.T
        outs.append(jnp.dot(a, b_ref[s], precision=lax.Precision.HIGHEST, preferred_element_type=jnp.float32))
    return jnp.stack(outs, 0)


def _first_kernel(n, count, rhs_ref, dinv_ref, fv_ref, win_ref, dfull_ref, got_y, sy, ry, whole, got_w, sw, rw, got_d, sd, rd):
    y_ref, d0_ref, d1_ref = rhs_ref.at[0], dinv_ref.at[0], dinv_ref.at[1]
    p = Place(n, count)
    p.barrier(True, True)
    sends = gather_start(p, y_ref, got_y, sy, ry)
    gather_finish(p, y_ref, got_y, sy, ry, whole)
    fv_ref[...] = _dots(d0_ref, whole)
    sends += bcast_start(p, fv_ref, got_w, sw, rw) + gather_start(p, d1_ref, got_d, sd, rd)
    bcast_finish(p, fv_ref, got_w, sw, rw, win_ref)
    gather_finish(p, d1_ref, got_d, sd, rd, dfull_ref)
    _wait_sends(sends)


def _level1_kernel(
    n, count, share_ref, dw_ref, dinv_ref, own_ref, win_ref, dfull_ref, x_ref, got_x, sx, rx, got_w, sw, rw, got_d, sd, rd
):
    d_ref = dinv_ref.at[2]
    p = Place(n, count)
    p.barrier(True, True)
    x_ref[...] = _dots(dw_ref, share_ref)
    sends = scatter_start(p, x_ref, got_x, sx, rx)
    own_ref[...] = scatter_finish(p, x_ref, got_x, sx, rx)
    sends += bcast_start(p, own_ref, got_w, sw, rw) + gather_start(p, d_ref, got_d, sd, rd)
    bcast_finish(p, own_ref, got_w, sw, rw, win_ref)
    gather_finish(p, d_ref, got_d, sd, rd, dfull_ref)
    _wait_sends(sends)


def _level2_kernel(n, count, share_ref, dw_ref, own_ref, sol_ref, mine_ref, x_ref, got_x, sx, rx, full, got_y, sy, ry):
    p = Place(n, count)
    p.barrier(True, False)
    x_ref[...] = _dots(dw_ref, share_ref)
    sends = scatter_start(p, x_ref, got_x, sx, rx)
    own_ref[...] = scatter_finish(p, x_ref, got_x, sx, rx)
    sends += gather_start(p, own_ref, got_y, sy, ry)
    gather_finish(p, own_ref, got_y, sy, ry, full)
    sol_ref[...] = _dots(dw_ref, full, transpose_a=True)
    mine_ref[...] = _rows_of(sol_ref, p.col, mine_ref.shape[1])[...]
    _wait_sends(sends)


def _back2_kernel(n, count, x_ref, f_ref, dw_ref, sum_ref, sol_ref, mine_ref, got_b, sb, rb, res, full, got_y, sy, ry):
    p = Place(n, count)
    p.barrier(True, True)
    sends = spread_start(p, x_ref, got_b, sb, rb)
    acc = spread_finish(p, x_ref, got_b, sb, rb)
    sum_ref[...] = acc
    res[...] = f_ref[...] - acc[acc.shape[0] - 1]
    sends += gather_start(p, res, got_y, sy, ry)
    gather_finish(p, res, got_y, sy, ry, full)
    sol_ref[...] = _dots(dw_ref, full, transpose_a=True)
    mine_ref[...] = _rows_of(sol_ref, p.col, mine_ref.shape[1])[...]
    _wait_sends(sends)


def _last_kernel(n, count, res_ref, d0_ref, own_ref, x_ref, got, s, r):
    p = Place(n, count)
    p.barrier(True, False)
    x_ref[...] = _dots(d0_ref, res_ref, transpose_a=True)
    sends = scatter_start(p, x_ref, got, s, r)
    own_ref[...] = scatter_finish(p, x_ref, got, s, r)
    _wait_sends(sends)


def _final_kernel(n, count, x_ref, f_ref, dinv_ref, own_ref, got_b, sb, rb, x2_ref, got, s, r):
    d0_ref = dinv_ref.at[0]
    p = Place(n, count)
    p.barrier(True, True)
    sends = spread_start(p, x_ref, got_b, sb, rb)
    acc = spread_finish(p, x_ref, got_b, sb, rb)
    res = f_ref[...] - acc[0]
    outs = []
    for q in range(d0_ref.shape[0]):
        outs.append(
            jnp.dot(d0_ref[q].T, res[q], precision=lax.Precision.HIGHEST, preferred_element_type=jnp.float32)
        )
    x2_ref[...] = jnp.stack(outs, 0)
    sends += scatter_start(p, x2_ref, got, s, r)
    own_ref[...] = scatter_finish(p, x2_ref, got, s, r)
    _wait_sends(sends)


def _mm(a, b):
    return jnp.dot(a, b, precision=lax.Precision.HIGHEST, preferred_element_type=jnp.float32)


def _smem():
    return pl.BlockSpec(memory_space=pltpu.SMEM)


def _share(p, wins, t_ref, table, base, slots, rhs_ref, out_ref):
    owned, share, r = rhs_ref.shape
    mine = pl.ds(pl.multiple_of(p.col * share, share), share)
    size = owned * slots
    for s in range(owned):
        pieces = []
        for k in range(slots):
            at = base + s * slots + k
            w = table[at + size]
            q = table[at + 2 * size]
            v = wins[0][w, q]
            if len(wins) > 1:
                v = jnp.where(table[at] == 0, v, wins[1][w, q])
            pieces.append(jnp.where(table[at + 3 * size] != 0, v, 0.0))
        picked = jnp.concatenate(pieces, axis=0)
        out_ref[s] = -_mm(t_ref[s].T, picked)
        out_ref[s, mine, :] = rhs_ref[s] + out_ref[s, mine, :]


def _terms(t_ref, sol_ref, terms_ref):
    owned, slots, share, r = terms_ref.shape
    for s in range(owned):
        full = _mm(t_ref[s], sol_ref[s])
        for k in range(slots):
            terms_ref[s, k] = full[k * share : (k + 1) * share]


def _route(bucket_ref, level, table, parts):
    slots, owned, share, r = bucket_ref.shape
    for w in range(slots):
        for q in range(owned):
            m = (level * slots + w) * owned + q
            acc = None
            for terms_ref, base in parts:
                count = terms_ref.shape[0]
                for s in range(count):
                    at = base + 2 * (m * count + s)
                    v = jnp.where(table[at + 1] != 0, terms_ref[s, table[at]], 0.0)
                    acc = v if acc is None else acc + v
            bucket_ref[w, q] = acc


def _forward_kernel(
    n, count,
    rhs_ref, dinv_ref, ft_ref, table,
    out_ref,
    fv0_ref, fv1_ref, sol2_ref, d1_ref, d2_ref,
    got_y, sy, ry, whole, win0, got_w0, sw0, rw0, got_d1, sd1, rd1, got_d2, sd2, rd2,
    share1, x1, got_x1, sx1, rx1, win1, got_w1, sw1, rw1,
    share2, x2, got_x2, sx2, rx2, fv2, full2, got_y2, sy2, ry2,
    terms2, bucket1, got_b1, sb1, rb1, res1, got_z1, sz1, rz1, full1, sol1,
    terms1, bucket0, got_b0, sb0, rb0, x0, got_x0, sx0, rx0,
):
    t1_ref, t2_ref = ft_ref.at[0], ft_ref.at[1]
    owned = rhs_ref.shape[1]
    slots = terms1.shape[1]
    size = owned * slots
    lookup1 = 8 * size
    lookup2 = lookup1 + (2 * KDEV + 1) * owned * owned * 2
    p = Place(n, count)
    p.barrier(True, True)
    sends = gather_start(p, rhs_ref.at[0], got_y, sy, ry)
    gather_finish(p, rhs_ref.at[0], got_y, sy, ry, whole)
    fv0_ref[...] = _dots(dinv_ref.at[0], whole)
    sends += bcast_start(p, fv0_ref, got_w0, sw0, rw0)
    sends += gather_start(p, dinv_ref.at[1], got_d1, sd1, rd1)
    bcast_finish(p, fv0_ref, got_w0, sw0, rw0, win0)
    gather_finish(p, dinv_ref.at[1], got_d1, sd1, rd1, d1_ref)
    _share(p, [win0], t1_ref, table, 0, slots, rhs_ref.at[1], share1)
    x1[...] = _dots(d1_ref, share1)
    sends += scatter_start(p, x1, got_x1, sx1, rx1)
    fv1_ref[...] = scatter_finish(p, x1, got_x1, sx1, rx1)
    sends += bcast_start(p, fv1_ref, got_w1, sw1, rw1) + gather_start(p, dinv_ref.at[2], got_d2, sd2, rd2)
    bcast_finish(p, fv1_ref, got_w1, sw1, rw1, win1)
    gather_finish(p, dinv_ref.at[2], got_d2, sd2, rd2, d2_ref)
    _share(p, [win0, win1], t2_ref, table, 4 * size, slots, rhs_ref.at[2], share2)
    x2[...] = _dots(d2_ref, share2)
    sends += scatter_start(p, x2, got_x2, sx2, rx2)
    fv2[...] = scatter_finish(p, x2, got_x2, sx2, rx2)
    sends += gather_start(p, fv2, got_y2, sy2, ry2)
    gather_finish(p, fv2, got_y2, sy2, ry2, full2)
    sol2_ref[...] = _dots(d2_ref, full2, transpose_a=True)
    share = fv2.shape[1]
    out_ref[2] = _rows_of(sol2_ref, p.col, share)[...]
    _terms(t2_ref, sol2_ref, terms2)
    _route(bucket1, 1, table, [(terms2, lookup2)])
    sends += spread_start(p, bucket1, got_b1, sb1, rb1)
    res1[...] = fv1_ref[...] - spread_finish(p, bucket1, got_b1, sb1, rb1)
    sends += gather_start(p, res1, got_z1, sz1, rz1)
    gather_finish(p, res1, got_z1, sz1, rz1, full1)
    sol1[...] = _dots(d1_ref, full1, transpose_a=True)
    out_ref[1] = _rows_of(sol1, p.col, share)[...]
    _terms(t1_ref, sol1, terms1)
    _route(bucket0, 0, table, [(terms2, lookup2), (terms1, lookup1)])
    sends += spread_start(p, bucket0, got_b0, sb0, rb0)
    res0 = fv0_ref[...] - spread_finish(p, bucket0, got_b0, sb0, rb0)
    d0 = dinv_ref.at[0]
    x0[...] = jnp.stack([_mm(d0[q].T, res0[q]) for q in range(res0.shape[0])], 0)
    sends += scatter_start(p, x0, got_x0, sx0, rx0)
    out_ref[0] = scatter_finish(p, x0, got_x0, sx0, rx0)
    _wait_sends(sends)


def _f32(shape):
    return jax.ShapeDtypeStruct(shape, jnp.float32)


def _dma(k):
    return [pltpu.SemaphoreType.DMA((k,)), pltpu.SemaphoreType.DMA((k,))]


def _call(body, n, count, cid, args, outs, scratch):
    return pl.pallas_call(
        functools.partial(body, n, count),
        out_shape=tuple(_f32(o) for o in outs),
        in_specs=[_vmem() for a in args],
        out_specs=tuple(_vmem() for o in outs),
        scratch_shapes=scratch,
        compiler_params=_params(cid),
    )(*args)


def local(rhs, diag_inv, factor_tiles, tile_source, tile_count):
    levels = rhs.shape[0]
    owned_count = rhs.shape[1]
    share_rows = rhs.shape[2]
    columns = rhs.shape[3]
    slot_count = tile_source.shape[2]
    reach_dev = KDEV
    window_len = 2 * reach_dev + 1
    n = lax.axis_size("cols")
    count = lax.axis_size("rows")
    total_sup = count * owned_count
    row_place = lax.axis_index("rows")
    my_rows = lax.axis_index("cols") * share_rows
    highest = lax.Precision.HIGHEST
    slot_ids = jnp.arange(slot_count, dtype=jnp.int32)
    assert levels == 3 and count >= window_len
    blk = (owned_count, share_rows, columns)
    whole = (owned_count, n * share_rows, columns)
    dblk = diag_inv.shape[1:]
    dwhole = (owned_count, n * share_rows, diag_inv.shape[3])
    win = (window_len,) + blk
    slots = window_len

    def window_places(sources):
        src_level = sources // total_sup
        within = sources % total_sup
        return (
            src_level * window_len + within // owned_count - row_place + reach_dev
        ) * owned_count + within % owned_count

    def live_mask(counts):
        return (slot_ids[None, :] < counts[:, None]).astype(jnp.float32)

    def own_rows(block):
        return lax.dynamic_slice_in_dim(block, my_rows, share_rows, axis=1)

    def forward_share(height, windows):
        stacked = jnp.stack(windows, 0).reshape(height * window_len * owned_count, share_rows, columns)
        places = window_places(tile_source[height - 1])
        picked = jnp.take(stacked, places, axis=0) * live_mask(tile_count[height - 1])[:, :, None, None]
        partial_value = jnp.einsum(
            "skci,skcr->sir", factor_tiles[height - 1], picked, precision=highest
        )
        return lax.dynamic_update_slice_in_dim(
            -partial_value, rhs[height] - own_rows(partial_value), my_rows, axis=1
        )

    def buckets(height, whole_block):
        term_set = jnp.einsum(
            "skci,sir->skcr", factor_tiles[height - 1], whole_block, precision=highest
        )
        term_set = term_set * live_mask(tile_count[height - 1])[:, :, None, None]
        places = window_places(tile_source[height - 1]).reshape(-1)
        targets = height * window_len * owned_count
        one_hot = (jnp.arange(targets, dtype=jnp.int32)[:, None] == places[None, :]).astype(
            jnp.float32
        )
        outgoing = jnp.einsum(
            "ms,slg->mlg",
            one_hot,
            term_set.reshape(owned_count * slot_count, share_rows, columns),
            precision=highest,
        )
        push_outgoing = outgoing.reshape(height, window_len, owned_count, share_rows, columns)
        return push_outgoing.transpose(1, 0, 2, 3, 4)

    def vm(shape):
        return pltpu.VMEM(shape, jnp.float32)

    def source_tables(height):
        sources = tile_source[height - 1]
        src_level = jnp.clip(sources // total_sup, 0, height - 1)
        within = sources % total_sup
        slot = jnp.clip(within // owned_count - row_place + reach_dev, 0, window_len - 1)
        live = (tile_count[height - 1][:, None] > slot_ids[None, :]).astype(jnp.int32)
        return [src_level, slot, within % owned_count, live]

    def flat_tiles(height):
        t = factor_tiles[height - 1]
        return t.reshape(t.shape[0], t.shape[1] * t.shape[2], t.shape[3])

    def lookup(height):
        places = window_places(tile_source[height - 1])
        live = tile_count[height - 1][:, None] > slot_ids[None, :]
        targets = height * window_len * owned_count
        match = (places[None, :, :] == jnp.arange(targets, dtype=jnp.int32)[:, None, None]) & live[None]
        pick = jnp.sum(match.astype(jnp.int32) * slot_ids[None, None, :], axis=-1)
        return [jnp.stack([pick, jnp.any(match, axis=-1).astype(jnp.int32)], -1)]

    nblk = (n,) + blk
    tiles = (owned_count, slot_count, share_rows, columns)
    args = (
        [rhs, diag_inv, factor_tiles.reshape(factor_tiles.shape[:2] + (slot_count * share_rows, -1))]
        + [jnp.concatenate([t.reshape(-1) for t in source_tables(1) + source_tables(2) + lookup(1) + lookup(2)])]
    )
    outs = pl.pallas_call(
        functools.partial(_forward_kernel, n, count),
        out_shape=tuple(_f32(o) for o in [rhs.shape, blk, blk, whole, dwhole, dwhole]),
        in_specs=[_vmem()] * 3 + [_smem()],
        out_specs=tuple(_vmem() for o in range(6)),
        scratch_shapes=[vm(nblk)] + _dma(n) + [vm(whole)]
        + [vm(win), vm(win)] + _dma(slots)
        + [vm((n,) + dblk)] + _dma(n) + [vm((n,) + dblk)] + _dma(n)
        + [vm(whole), vm(whole), vm(nblk)] + _dma(n)
        + [vm(win), vm(win)] + _dma(slots)
        + [vm(whole), vm(whole), vm(nblk)] + _dma(n)
        + [vm(blk), vm(whole), vm(nblk)] + _dma(n)
        + [vm(tiles), vm(win), vm(win)] + _dma(slots) + [vm(blk), vm(nblk)] + _dma(n) + [vm(whole), vm(whole)]
        + [vm(tiles), vm(win), vm(win)] + _dma(slots) + [vm(whole), vm(nblk)] + _dma(n),
        compiler_params=_params(0),
    )(*args)
    return outs[0]


def solution(mesh):
    placed = (
        P(None, "rows", "cols", None),
        P(None, "rows", "cols", None),
        P(None, "rows", None, "cols", None),
        P(None, "rows", None),
        P(None, "rows"),
    )
    return jax.shard_map(
        local, mesh=mesh, in_specs=placed, out_specs=P(None, "rows", "cols", None), check_vma=False
    )
```

```python
import functools

import jax
import jax.numpy as jnp
from jax import lax
from jax.experimental import pallas as pl
from jax.experimental.pallas import tpu as pltpu
from jax.sharding import PartitionSpec as P

KDEV = 7
MESH = pl.DeviceIdType.MESH
OFFSETS = [d for d in range(-KDEV, KDEV + 1) if d != 0]
SEND_OFFSETS = sorted(OFFSETS, key=lambda d: (-abs(d), d))


def _send_order(n):
    return sorted(range(1, n), key=lambda k: (-min(k, n - k), k))


def _params(cid):
    return pltpu.CompilerParams(collective_id=cid, has_side_effects=True)


def _vmem():
    return pl.BlockSpec(memory_space=pltpu.VMEM)


class Place:
    def __init__(self, n, count):
        self.n = n
        self.count = count
        self.col = lax.axis_index("cols")
        self.row = lax.axis_index("rows")

    def col_peer(self, k):
        return lax.rem(self.col + k, self.n)

    def row_peer(self, d):
        return lax.rem(self.row + d + self.count, self.count)

    def barrier(self, cols, rows):
        targets = []
        if cols:
            targets += [(self.row, self.col_peer(k)) for k in range(1, self.n)]
        if rows:
            targets += [(self.row_peer(d), self.col) for d in OFFSETS]
        barrier = pltpu.get_barrier_semaphore()
        for t in targets:
            pl.semaphore_signal(barrier, 1, device_id=t, device_id_type=MESH)
        pl.semaphore_wait(barrier, len(targets))


def _copy(src_ref, dst_ref, send, recv, device):
    return pltpu.make_async_remote_copy(
        src_ref=src_ref,
        dst_ref=dst_ref,
        send_sem=send,
        recv_sem=recv,
        device_id=device,
        device_id_type=MESH,
    )


def _rows_of(ref, index, chunk):
    return ref.at[:, pl.ds(pl.multiple_of(index * chunk, chunk), chunk), :]


def _start_all(copies):
    for c in copies:
        c.start()
    return copies


def _wait_sends(copies):
    for c in copies:
        c.wait_send()


def scatter_start(p, x_ref, got, send, recv):
    chunk = got.shape[2]
    out = []
    for k in _send_order(p.n):
        peer = p.col_peer(k)
        out.append(
            _copy(_rows_of(x_ref, peer, chunk), got.at[p.col], send.at[peer], recv.at[p.col], (p.row, peer))
        )
    return _start_all(out)


def scatter_finish(p, x_ref, got, send, recv):
    chunk = got.shape[2]
    acc = _rows_of(x_ref, p.col, chunk)[...]
    for k in range(1, p.n):
        src = p.col_peer(p.n - k)
        _copy(_rows_of(x_ref, src, chunk), got.at[src], send.at[src], recv.at[src], (p.row, src)).wait_recv()
        acc = acc + got[src]
    return acc


def gather_start(p, y_ref, got, send, recv):
    out = []
    for k in _send_order(p.n):
        peer = p.col_peer(k)
        out.append(_copy(y_ref, got.at[p.col], send.at[peer], recv.at[p.col], (p.row, peer)))
    return _start_all(out)


def gather_finish(p, y_ref, got, send, recv, full_ref):
    chunk = got.shape[2]
    _rows_of(full_ref, p.col, chunk)[...] = y_ref[...]
    for k in range(1, p.n):
        src = p.col_peer(p.n - k)
        _copy(y_ref, got.at[src], send.at[src], recv.at[src], (p.row, src)).wait_recv()
        _rows_of(full_ref, src, chunk)[...] = got[src]


def bcast_start(p, v_ref, got, send, recv):
    out = []
    for d in SEND_OFFSETS:
        out.append(_copy(v_ref, got.at[KDEV - d], send.at[KDEV + d], recv.at[KDEV - d], (p.row_peer(d), p.col)))
    return _start_all(out)


def bcast_finish(p, v_ref, got, send, recv, win_ref):
    win_ref[KDEV] = v_ref[...]
    for o in OFFSETS:
        w = KDEV + o
        _copy(v_ref, got.at[w], send.at[w], recv.at[w], (p.row_peer(o), p.col)).wait_recv()
        win_ref[w] = got[w]


def spread_start(p, x_ref, got, send, recv):
    out = []
    for d in SEND_OFFSETS:
        out.append(
            _copy(x_ref.at[KDEV + d], got.at[KDEV - d], send.at[KDEV + d], recv.at[KDEV - d], (p.row_peer(d), p.col))
        )
    return _start_all(out)


def spread_finish(p, x_ref, got, send, recv):
    acc = x_ref[KDEV]
    for o in OFFSETS:
        w = KDEV + o
        _copy(x_ref.at[w], got.at[w], send.at[w], recv.at[w], (p.row_peer(o), p.col)).wait_recv()
        acc = acc + got[w]
    return acc


def _gather_kernel(n, count, y_ref, full_ref, got, s, r):
    p = Place(n, count)
    p.barrier(True, False)
    sends = gather_start(p, y_ref, got, s, r)
    gather_finish(p, y_ref, got, s, r, full_ref)
    _wait_sends(sends)


def _scatter_kernel(n, count, x_ref, own_ref, got, s, r):
    p = Place(n, count)
    p.barrier(True, False)
    sends = scatter_start(p, x_ref, got, s, r)
    own_ref[...] = scatter_finish(p, x_ref, got, s, r)
    _wait_sends(sends)


def _bcast_gather_kernel(n, count, v_ref, d_ref, win_ref, dfull_ref, got_w, sw, rw, got_d, sd, rd):
    p = Place(n, count)
    p.barrier(True, True)
    sends = bcast_start(p, v_ref, got_w, sw, rw) + gather_start(p, d_ref, got_d, sd, rd)
    bcast_finish(p, v_ref, got_w, sw, rw, win_ref)
    gather_finish(p, d_ref, got_d, sd, rd, dfull_ref)
    _wait_sends(sends)


def _scatter_bcast_gather_kernel(
    n, count, x_ref, d_ref, own_ref, win_ref, dfull_ref, got_x, sx, rx, got_w, sw, rw, got_d, sd, rd
):
    p = Place(n, count)
    p.barrier(True, True)
    sends = scatter_start(p, x_ref, got_x, sx, rx)
    own_ref[...] = scatter_finish(p, x_ref, got_x, sx, rx)
    sends += bcast_start(p, own_ref, got_w, sw, rw) + gather_start(p, d_ref, got_d, sd, rd)
    bcast_finish(p, own_ref, got_w, sw, rw, win_ref)
    gather_finish(p, d_ref, got_d, sd, rd, dfull_ref)
    _wait_sends(sends)


def _scatter_gather_kernel(n, count, x_ref, own_ref, full_ref, got_x, sx, rx, got_y, sy, ry):
    p = Place(n, count)
    p.barrier(True, False)
    sends = scatter_start(p, x_ref, got_x, sx, rx)
    own_ref[...] = scatter_finish(p, x_ref, got_x, sx, rx)
    sends += gather_start(p, own_ref, got_y, sy, ry)
    gather_finish(p, own_ref, got_y, sy, ry, full_ref)
    _wait_sends(sends)


def _spread_gather_kernel(n, count, x_ref, f_ref, sum_ref, full_ref, got_b, sb, rb, res, got_y, sy, ry):
    p = Place(n, count)
    p.barrier(True, True)
    sends = spread_start(p, x_ref, got_b, sb, rb)
    acc = spread_finish(p, x_ref, got_b, sb, rb)
    sum_ref[...] = acc
    res[...] = f_ref[...] - acc[acc.shape[0] - 1]
    sends += gather_start(p, res, got_y, sy, ry)
    gather_finish(p, res, got_y, sy, ry, full_ref)
    _wait_sends(sends)


def _spread_kernel(n, count, x_ref, sum_ref, got_b, sb, rb):
    p = Place(n, count)
    p.barrier(False, True)
    sends = spread_start(p, x_ref, got_b, sb, rb)
    sum_ref[...] = spread_finish(p, x_ref, got_b, sb, rb)
    _wait_sends(sends)


def _dots(a_ref, b_ref, transpose_a=False):
    outs = []
    for s in range(a_ref.shape[0]):
        a = a_ref[s]
        if transpose_a:
            a = a.T
        outs.append(jnp.dot(a, b_ref[s], precision=lax.Precision.HIGHEST, preferred_element_type=jnp.float32))
    return jnp.stack(outs, 0)


def _first_kernel(n, count, rhs_ref, dinv_ref, fv_ref, win_ref, dfull_ref, got_y, sy, ry, whole, got_w, sw, rw, got_d, sd, rd):
    y_ref, d0_ref, d1_ref = rhs_ref.at[0], dinv_ref.at[0], dinv_ref.at[1]
    p = Place(n, count)
    p.barrier(True, True)
    sends = gather_start(p, y_ref, got_y, sy, ry)
    gather_finish(p, y_ref, got_y, sy, ry, whole)
    fv_ref[...] = _dots(d0_ref, whole)
    sends += bcast_start(p, fv_ref, got_w, sw, rw) + gather_start(p, d1_ref, got_d, sd, rd)
    bcast_finish(p, fv_ref, got_w, sw, rw, win_ref)
    gather_finish(p, d1_ref, got_d, sd, rd, dfull_ref)
    _wait_sends(sends)


def _level1_kernel(
    n, count, share_ref, dw_ref, dinv_ref, own_ref, win_ref, dfull_ref, x_ref, got_x, sx, rx, got_w, sw, rw, got_d, sd, rd
):
    d_ref = dinv_ref.at[2]
    p = Place(n, count)
    p.barrier(True, True)
    x_ref[...] = _dots(dw_ref, share_ref)
    sends = scatter_start(p, x_ref, got_x, sx, rx)
    own_ref[...] = scatter_finish(p, x_ref, got_x, sx, rx)
    sends += bcast_start(p, own_ref, got_w, sw, rw) + gather_start(p, d_ref, got_d, sd, rd)
    bcast_finish(p, own_ref, got_w, sw, rw, win_ref)
    gather_finish(p, d_ref, got_d, sd, rd, dfull_ref)
    _wait_sends(sends)


def _level2_kernel(n, count, share_ref, dw_ref, own_ref, sol_ref, mine_ref, x_ref, got_x, sx, rx, full, got_y, sy, ry):
    p = Place(n, count)
    p.barrier(True, False)
    x_ref[...] = _dots(dw_ref, share_ref)
    sends = scatter_start(p, x_ref, got_x, sx, rx)
    own_ref[...] = scatter_finish(p, x_ref, got_x, sx, rx)
    sends += gather_start(p, own_ref, got_y, sy, ry)
    gather_finish(p, own_ref, got_y, sy, ry, full)
    sol_ref[...] = _dots(dw_ref, full, transpose_a=True)
    mine_ref[...] = _rows_of(sol_ref, p.col, mine_ref.shape[1])[...]
    _wait_sends(sends)


def _back2_kernel(n, count, x_ref, f_ref, dw_ref, sum_ref, sol_ref, mine_ref, got_b, sb, rb, res, full, got_y, sy, ry):
    p = Place(n, count)
    p.barrier(True, True)
    sends = spread_start(p, x_ref, got_b, sb, rb)
    acc = spread_finish(p, x_ref, got_b, sb, rb)
    sum_ref[...] = acc
    res[...] = f_ref[...] - acc[acc.shape[0] - 1]
    sends += gather_start(p, res, got_y, sy, ry)
    gather_finish(p, res, got_y, sy, ry, full)
    sol_ref[...] = _dots(dw_ref, full, transpose_a=True)
    mine_ref[...] = _rows_of(sol_ref, p.col, mine_ref.shape[1])[...]
    _wait_sends(sends)


def _last_kernel(n, count, res_ref, d0_ref, own_ref, x_ref, got, s, r):
    p = Place(n, count)
    p.barrier(True, False)
    x_ref[...] = _dots(d0_ref, res_ref, transpose_a=True)
    sends = scatter_start(p, x_ref, got, s, r)
    own_ref[...] = scatter_finish(p, x_ref, got, s, r)
    _wait_sends(sends)


def _final_kernel(n, count, x_ref, f_ref, dinv_ref, own_ref, got_b, sb, rb, x2_ref, got, s, r):
    d0_ref = dinv_ref.at[0]
    p = Place(n, count)
    p.barrier(True, True)
    sends = spread_start(p, x_ref, got_b, sb, rb)
    acc = spread_finish(p, x_ref, got_b, sb, rb)
    res = f_ref[...] - acc[0]
    outs = []
    for q in range(d0_ref.shape[0]):
        outs.append(
            jnp.dot(d0_ref[q].T, res[q], precision=lax.Precision.HIGHEST, preferred_element_type=jnp.float32)
        )
    x2_ref[...] = jnp.stack(outs, 0)
    sends += scatter_start(p, x2_ref, got, s, r)
    own_ref[...] = scatter_finish(p, x2_ref, got, s, r)
    _wait_sends(sends)


def _mm(a, b):
    return jnp.dot(a, b, precision=lax.Precision.HIGHEST, preferred_element_type=jnp.float32)


def _smem():
    return pl.BlockSpec(memory_space=pltpu.SMEM)


def _share(p, wins, t_ref, table, base, slots, rhs_ref, out_ref):
    owned, share, r = rhs_ref.shape
    mine = pl.ds(pl.multiple_of(p.col * share, share), share)
    size = owned * slots
    for s in range(owned):
        pieces = []
        for k in range(slots):
            at = base + s * slots + k
            w = table[at + size]
            q = table[at + 2 * size]
            v = wins[0][w, q]
            if len(wins) > 1:
                v = jnp.where(table[at] == 0, v, wins[1][w, q])
            pieces.append(jnp.where(table[at + 3 * size] != 0, v, 0.0))
        picked = jnp.concatenate(pieces, axis=0)
        out_ref[s] = -_mm(t_ref[s].T, picked)
        out_ref[s, mine, :] = rhs_ref[s] + out_ref[s, mine, :]


def _terms(t_ref, sol_ref, terms_ref):
    owned, slots, share, r = terms_ref.shape
    for s in range(owned):
        full = _mm(t_ref[s], sol_ref[s])
        for k in range(slots):
            terms_ref[s, k] = full[k * share : (k + 1) * share]


def _route(bucket_ref, level, table, parts):
    slots, owned, share, r = bucket_ref.shape
    for w in range(slots):
        for q in range(owned):
            m = (level * slots + w) * owned + q
            acc = None
            for terms_ref, base in parts:
                count = terms_ref.shape[0]
                for s in range(count):
                    at = base + 2 * (m * count + s)
                    v = jnp.where(table[at + 1] != 0, terms_ref[s, table[at]], 0.0)
                    acc = v if acc is None else acc + v
            bucket_ref[w, q] = acc


def _forward_kernel(
    n, count,
    rhs_ref, dinv_ref, ft_ref, table,
    out_ref,
    fv0_ref, fv1_ref, sol2_ref, d1_ref, d2_ref,
    got_y, sy, ry, whole, win0, got_w0, sw0, rw0, got_d1, sd1, rd1, got_d2, sd2, rd2,
    share1, x1, got_x1, sx1, rx1, win1, got_w1, sw1, rw1,
    share2, x2, got_x2, sx2, rx2, fv2, full2, got_y2, sy2, ry2,
    terms2, bucket1, got_b1, sb1, rb1, res1, got_z1, sz1, rz1, full1, sol1,
    terms1, bucket0, got_b0, sb0, rb0, x0, got_x0, sx0, rx0,
):
    t1_ref, t2_ref = ft_ref.at[0], ft_ref.at[1]
    owned = rhs_ref.shape[1]
    slots = terms1.shape[1]
    size = owned * slots
    lookup1 = 8 * size
    lookup2 = lookup1 + (2 * KDEV + 1) * owned * owned * 2
    p = Place(n, count)
    p.barrier(True, True)
    sends = gather_start(p, rhs_ref.at[0], got_y, sy, ry)
    gather_finish(p, rhs_ref.at[0], got_y, sy, ry, whole)
    sends += gather_start(p, dinv_ref.at[1], got_d1, sd1, rd1)
    fv0_ref[...] = _dots(dinv_ref.at[0], whole)
    sends += bcast_start(p, fv0_ref, got_w0, sw0, rw0)
    bcast_finish(p, fv0_ref, got_w0, sw0, rw0, win0)
    gather_finish(p, dinv_ref.at[1], got_d1, sd1, rd1, d1_ref)
    _share(p, [win0], t1_ref, table, 0, slots, rhs_ref.at[1], share1)
    x1[...] = _dots(d1_ref, share1)
    sends += scatter_start(p, x1, got_x1, sx1, rx1)
    fv1_ref[...] = scatter_finish(p, x1, got_x1, sx1, rx1)
    sends += bcast_start(p, fv1_ref, got_w1, sw1, rw1) + gather_start(p, dinv_ref.at[2], got_d2, sd2, rd2)
    bcast_finish(p, fv1_ref, got_w1, sw1, rw1, win1)
    gather_finish(p, dinv_ref.at[2], got_d2, sd2, rd2, d2_ref)
    _share(p, [win0, win1], t2_ref, table, 4 * size, slots, rhs_ref.at[2], share2)
    x2[...] = _dots(d2_ref, share2)
    sends += scatter_start(p, x2, got_x2, sx2, rx2)
    fv2[...] = scatter_finish(p, x2, got_x2, sx2, rx2)
    sends += gather_start(p, fv2, got_y2, sy2, ry2)
    gather_finish(p, fv2, got_y2, sy2, ry2, full2)
    sol2_ref[...] = _dots(d2_ref, full2, transpose_a=True)
    share = fv2.shape[1]
    out_ref[2] = _rows_of(sol2_ref, p.col, share)[...]
    _terms(t2_ref, sol2_ref, terms2)
    _route(bucket1, 1, table, [(terms2, lookup2)])
    sends += spread_start(p, bucket1, got_b1, sb1, rb1)
    res1[...] = fv1_ref[...] - spread_finish(p, bucket1, got_b1, sb1, rb1)
    sends += gather_start(p, res1, got_z1, sz1, rz1)
    gather_finish(p, res1, got_z1, sz1, rz1, full1)
    sol1[...] = _dots(d1_ref, full1, transpose_a=True)
    out_ref[1] = _rows_of(sol1, p.col, share)[...]
    _terms(t1_ref, sol1, terms1)
    _route(bucket0, 0, table, [(terms2, lookup2), (terms1, lookup1)])
    sends += spread_start(p, bucket0, got_b0, sb0, rb0)
    res0 = fv0_ref[...] - spread_finish(p, bucket0, got_b0, sb0, rb0)
    d0 = dinv_ref.at[0]
    x0[...] = jnp.stack([_mm(d0[q].T, res0[q]) for q in range(res0.shape[0])], 0)
    sends += scatter_start(p, x0, got_x0, sx0, rx0)
    out_ref[0] = scatter_finish(p, x0, got_x0, sx0, rx0)
    _wait_sends(sends)


def _f32(shape):
    return jax.ShapeDtypeStruct(shape, jnp.float32)


def _dma(k):
    return [pltpu.SemaphoreType.DMA((k,)), pltpu.SemaphoreType.DMA((k,))]


def _call(body, n, count, cid, args, outs, scratch):
    return pl.pallas_call(
        functools.partial(body, n, count),
        out_shape=tuple(_f32(o) for o in outs),
        in_specs=[_vmem() for a in args],
        out_specs=tuple(_vmem() for o in outs),
        scratch_shapes=scratch,
        compiler_params=_params(cid),
    )(*args)


def local(rhs, diag_inv, factor_tiles, tile_source, tile_count):
    levels = rhs.shape[0]
    owned_count = rhs.shape[1]
    share_rows = rhs.shape[2]
    columns = rhs.shape[3]
    slot_count = tile_source.shape[2]
    reach_dev = KDEV
    window_len = 2 * reach_dev + 1
    n = lax.axis_size("cols")
    count = lax.axis_size("rows")
    total_sup = count * owned_count
    row_place = lax.axis_index("rows")
    my_rows = lax.axis_index("cols") * share_rows
    highest = lax.Precision.HIGHEST
    slot_ids = jnp.arange(slot_count, dtype=jnp.int32)
    assert levels == 3 and count >= window_len
    blk = (owned_count, share_rows, columns)
    whole = (owned_count, n * share_rows, columns)
    dblk = diag_inv.shape[1:]
    dwhole = (owned_count, n * share_rows, diag_inv.shape[3])
    win = (window_len,) + blk
    slots = window_len

    def window_places(sources):
        src_level = sources // total_sup
        within = sources % total_sup
        return (
            src_level * window_len + within // owned_count - row_place + reach_dev
        ) * owned_count + within % owned_count

    def live_mask(counts):
        return (slot_ids[None, :] < counts[:, None]).astype(jnp.float32)

    def own_rows(block):
        return lax.dynamic_slice_in_dim(block, my_rows, share_rows, axis=1)

    def forward_share(height, windows):
        stacked = jnp.stack(windows, 0).reshape(height * window_len * owned_count, share_rows, columns)
        places = window_places(tile_source[height - 1])
        picked = jnp.take(stacked, places, axis=0) * live_mask(tile_count[height - 1])[:, :, None, None]
        partial_value = jnp.einsum(
            "skci,skcr->sir", factor_tiles[height - 1], picked, precision=highest
        )
        return lax.dynamic_update_slice_in_dim(
            -partial_value, rhs[height] - own_rows(partial_value), my_rows, axis=1
        )

    def buckets(height, whole_block):
        term_set = jnp.einsum(
            "skci,sir->skcr", factor_tiles[height - 1], whole_block, precision=highest
        )
        term_set = term_set * live_mask(tile_count[height - 1])[:, :, None, None]
        places = window_places(tile_source[height - 1]).reshape(-1)
        targets = height * window_len * owned_count
        one_hot = (jnp.arange(targets, dtype=jnp.int32)[:, None] == places[None, :]).astype(
            jnp.float32
        )
        outgoing = jnp.einsum(
            "ms,slg->mlg",
            one_hot,
            term_set.reshape(owned_count * slot_count, share_rows, columns),
            precision=highest,
        )
        push_outgoing = outgoing.reshape(height, window_len, owned_count, share_rows, columns)
        return push_outgoing.transpose(1, 0, 2, 3, 4)

    def vm(shape):
        return pltpu.VMEM(shape, jnp.float32)

    def source_tables(height):
        sources = tile_source[height - 1]
        src_level = jnp.clip(sources // total_sup, 0, height - 1)
        within = sources % total_sup
        slot = jnp.clip(within // owned_count - row_place + reach_dev, 0, window_len - 1)
        live = (tile_count[height - 1][:, None] > slot_ids[None, :]).astype(jnp.int32)
        return [src_level, slot, within % owned_count, live]

    def flat_tiles(height):
        t = factor_tiles[height - 1]
        return t.reshape(t.shape[0], t.shape[1] * t.shape[2], t.shape[3])

    def lookup(height):
        places = window_places(tile_source[height - 1])
        live = tile_count[height - 1][:, None] > slot_ids[None, :]
        targets = height * window_len * owned_count
        match = (places[None, :, :] == jnp.arange(targets, dtype=jnp.int32)[:, None, None]) & live[None]
        pick = jnp.sum(match.astype(jnp.int32) * slot_ids[None, None, :], axis=-1)
        return [jnp.stack([pick, jnp.any(match, axis=-1).astype(jnp.int32)], -1)]

    nblk = (n,) + blk
    tiles = (owned_count, slot_count, share_rows, columns)
    args = (
        [rhs, diag_inv, factor_tiles.reshape(factor_tiles.shape[:2] + (slot_count * share_rows, -1))]
        + [jnp.concatenate([t.reshape(-1) for t in source_tables(1) + source_tables(2) + lookup(1) + lookup(2)])]
    )
    outs = pl.pallas_call(
        functools.partial(_forward_kernel, n, count),
        out_shape=tuple(_f32(o) for o in [rhs.shape, blk, blk, whole, dwhole, dwhole]),
        in_specs=[_vmem()] * 3 + [_smem()],
        out_specs=tuple(_vmem() for o in range(6)),
        scratch_shapes=[vm(nblk)] + _dma(n) + [vm(whole)]
        + [vm(win), vm(win)] + _dma(slots)
        + [vm((n,) + dblk)] + _dma(n) + [vm((n,) + dblk)] + _dma(n)
        + [vm(whole), vm(whole), vm(nblk)] + _dma(n)
        + [vm(win), vm(win)] + _dma(slots)
        + [vm(whole), vm(whole), vm(nblk)] + _dma(n)
        + [vm(blk), vm(whole), vm(nblk)] + _dma(n)
        + [vm(tiles), vm(win), vm(win)] + _dma(slots) + [vm(blk), vm(nblk)] + _dma(n) + [vm(whole), vm(whole)]
        + [vm(tiles), vm(win), vm(win)] + _dma(slots) + [vm(whole), vm(nblk)] + _dma(n),
        compiler_params=_params(0),
    )(*args)
    return outs[0]


def solution(mesh):
    placed = (
        P(None, "rows", "cols", None),
        P(None, "rows", "cols", None),
        P(None, "rows", None, "cols", None),
        P(None, "rows", None),
        P(None, "rows"),
    )
    return jax.shard_map(
        local, mesh=mesh, in_specs=placed, out_specs=P(None, "rows", "cols", None), check_vma=False
    )
```
